32 devices in a mesh: row: 4 (over y, x), col: 8 (over z, core).
Axes of the slice: x: 2, y: 2, z: 4, core: 2. Of those that a mesh axis runs over, the one named last changes fastest.
Arguments:
- node_features: bfloat16 [2048, 128, 512], P(('row', 'col')), may hold values from -6 to 6
- node_counts: int32 [2048], P(('row', 'col')), may hold values from 16 to 128, as said below
- edge_list: int32 [2048, 2, 256], P(('row', 'col')), may hold values from 0 to 128, as said below
- readout_ids: int32 [2048], P(('row', 'col')), may hold values from 0 to 255
- live_graphs: int32 [32], P(('row', 'col')), may hold values from 1 to 64, as said below
- self_weight: float32 [1], replicated, may hold values from 0.5 to 1.5
- w_first: bfloat16 [512, 512], replicated, may hold values from -0.25 to 0.25
- b_first: float32 [512], replicated, may hold values from -3 to 3
- w_second: bfloat16 [512, 512], replicated, may hold values from -0.25 to 0.25
- b_second: float32 [512], replicated, may hold values from -3 to 3
- w_third: bfloat16 [512, 512], replicated, may hold values from -0.25 to 0.25
- b_third: float32 [512], replicated, may hold values from -3 to 3
Outputs:
- node_out: bfloat16 [1024, 128, 512], P(('row', 'col'))
- readout: float32 [256, 512], P(('row', 'col'))
The draws below stay inside these ranges and needn't reach their ends.
Inputs may be any that keep to these rules, and one draw needn't show every extreme that they name: `live_graphs`: the entries sum to 1024, and at least one equals 64. `node_counts`: node slots 0 to count - 1 of a graph are live; the rest of its block is padding. `edge_list`: each edge slot holds two node indices below its graph's node count, or 128 in both rows for an unused slot.
All inputs are finite; a program needn't handle non-finite values.
Results may differ from the reference program's by a relative error of at most 0.0058.
Values may be sent and summed in bfloat16 or wider, within the bound.
A program may use at most 128 MiB of HBM per device.

```python
import jax
import jax.numpy as jnp
from jax import lax

H = 512
BLOCK = 128
G_DEV = 32
MIN_NODES = 16
CAP_IN = 64
GRAPHS = 1024
GRAPHS_IN = 2048
READOUTS = 256
DEVICES = 32


def graph_shapes(key):
    folded = jax.random.fold_in(key, 11)
    counts = jax.random.randint(jax.random.fold_in(folded, 1), (GRAPHS_IN,), MIN_NODES, BLOCK + 1, dtype=jnp.int32)
    pair_total = jax.random.randint(jax.random.fold_in(folded, 2), (GRAPHS_IN,), counts // 2, counts + 1, dtype=jnp.int32)
    ends_first = jax.random.randint(jax.random.fold_in(folded, 3), (GRAPHS_IN, BLOCK), 0, counts[:, None], dtype=jnp.int32)
    ends_second = jax.random.randint(jax.random.fold_in(folded, 4), (GRAPHS_IN, BLOCK), 0, counts[:, None], dtype=jnp.int32)
    pair_index = jnp.arange(BLOCK, dtype=jnp.int32)[None, :]
    pair_used = jnp.concatenate([pair_index < pair_total[:, None], pair_index < pair_total[:, None]], axis=1)
    sources = jnp.where(pair_used, jnp.concatenate([ends_first, ends_second], axis=1), BLOCK)
    targets = jnp.where(pair_used, jnp.concatenate([ends_second, ends_first], axis=1), BLOCK)
    return (counts, jnp.stack([sources, targets], axis=1).astype(jnp.int32))


def draw_node_counts(key, part):
    return graph_shapes(key)[0]


def draw_edge_list(key, part):
    return graph_shapes(key)[1]


def draw_live_graphs(key, part):
    halves = DEVICES // 2
    shuffled = jax.random.permutation(jax.random.fold_in(key, 23), DEVICES)
    moves = jax.random.randint(jax.random.fold_in(key, 29), (halves,), 0, G_DEV, dtype=jnp.int32)
    moves = moves.at[0].set(G_DEV - 1)
    higher = G_DEV + moves
    lower = G_DEV - moves
    higher = higher.at[0].add(1)
    higher = higher.at[1].add(-1)
    counts = jnp.zeros((DEVICES,), jnp.int32)
    counts = counts.at[shuffled[0::2]].set(higher)
    counts = counts.at[shuffled[1::2]].set(lower)
    return counts.astype(jnp.int32)


def set_ends(values, own_key, smallest, largest):
    extent = values.shape
    place = [jax.random.randint(jax.random.fold_in(own_key, axis), (), 0, extent[axis]) for axis in range(len(extent))]
    values = values.at[tuple(place)].set(smallest)
    longest = extent.index(max(extent))
    place[longest] = (place[longest] + 1) % extent[longest]
    return values.at[tuple(place)].set(largest)


def levels(key, shape, pieces, least, high):
    gain, own = 1.0, jax.random.fold_in(key, 6)
    for position, blocks in pieces:
        steps = jnp.exp(jax.random.uniform(jax.random.fold_in(own, position), (blocks,), jnp.float32, least / len(pieces), high / len(pieces)))
        gain = gain * jnp.repeat(steps, shape[position] // blocks).reshape([-1 if axis == position else 1 for axis in range(len(shape))])
    return gain


def normal_values(key, dims, spread, reach, pieces=(), kind=jnp.bfloat16):
    values = jax.random.normal(key, dims, jnp.float32) * spread
    if len(pieces) > 0:
        values = levels(key, dims, pieces, -0.22, 0.18) * values
    return jnp.clip(values, min=-reach, max=reach).astype(kind)


def setup_inputs(seed: int = 0) -> dict:
    splits = jax.random.split(jax.random.key(seed), 13)
    node_features = normal_values(splits[0], (GRAPHS_IN, BLOCK, H), 1.0, 6.0, ((0, 32),))
    node_counts = draw_node_counts(jax.random.fold_in(splits[12], 71), 0)
    edge_list = draw_edge_list(jax.random.fold_in(splits[12], 71), 0)
    readout_ids = set_ends(jax.random.randint(splits[3], (GRAPHS_IN,), 0, READOUTS), jax.random.fold_in(splits[3], 1), 0, READOUTS - 1).astype(jnp.int32)
    live_graphs = draw_live_graphs(jax.random.fold_in(splits[12], 71), 0)
    self_weight = jnp.clip(jax.random.uniform(splits[5], (1,), jnp.float32, 0.5, 1.5), 0.5, 1.5)
    w_first = normal_values(splits[6], (H, H), H ** -0.5, 0.25)
    b_first = normal_values(splits[7], (H,), 0.5, 3.0, (), jnp.float32)
    w_second = normal_values(splits[8], (H, H), H ** -0.5, 0.25)
    b_second = normal_values(splits[9], (H,), 0.5, 3.0, (), jnp.float32)
    w_third = normal_values(splits[10], (H, H), H ** -0.5, 0.25)
    b_third = normal_values(splits[11], (H,), 0.5, 3.0, (), jnp.float32)
    return {"node_features": node_features, "node_counts": node_counts, "edge_list": edge_list, "readout_ids": readout_ids, "live_graphs": live_graphs, "self_weight": self_weight, "w_first": w_first, "b_first": b_first, "w_second": w_second, "b_second": b_second, "w_third": w_third, "b_third": b_third}


def blend_nodes(features, edge_slots, self_weight):
    node_index = jnp.arange(BLOCK, dtype=jnp.int32)
    sources = (edge_slots[:, 0, :, None] == node_index[None, None, :]).astype(jnp.float32)
    targets = (edge_slots[:, 1, :, None] == node_index[None, None, :]).astype(jnp.float32)
    adjacency = jnp.einsum("gek,gel->gkl", targets, sources)
    neighbour = jnp.einsum("gkl,glh->gkh", adjacency, features.astype(jnp.float32))
    return (self_weight[0] * features.astype(jnp.float32) + neighbour).astype(jnp.bfloat16)


def perceptron(blended, weights):
    w_first, b_first, w_second, b_second, w_third, b_third = weights
    flat_rows = blended.reshape(-1, blended.shape[-1])
    hidden_one = jax.nn.relu(jnp.dot(flat_rows, w_first, preferred_element_type=jnp.float32) + b_first).astype(jnp.bfloat16)
    hidden_two = jax.nn.relu(jnp.dot(hidden_one, w_second, preferred_element_type=jnp.float32) + b_second).astype(jnp.bfloat16)
    result = jnp.dot(hidden_two, w_third, preferred_element_type=jnp.float32) + b_third
    return result.reshape(blended.shape)


def source_rows(live_graphs):
    inclusive = jnp.cumsum(live_graphs).astype(jnp.int32)
    offsets = (inclusive - live_graphs).astype(jnp.int32)
    order_index = jnp.arange(GRAPHS, dtype=jnp.int32)
    number = (order_index % G_DEV) * DEVICES + order_index // G_DEV
    source = jnp.sum((inclusive[None, :] <= number[:, None]).astype(jnp.int32), axis=1).astype(jnp.int32)
    return (source * CAP_IN + number - offsets[source]).astype(jnp.int32)


def reference(node_features, node_counts, edge_list, readout_ids, live_graphs, self_weight, w_first, b_first, w_second, b_second, w_third, b_third):
    weights = (w_first, b_first, w_second, b_second, w_third, b_third)
    chosen = source_rows(live_graphs).reshape(DEVICES, G_DEV)

    def one_group(indices):
        features = node_features[indices]
        counts_here = node_counts[indices]
        blended = blend_nodes(features, edge_list[indices], self_weight)
        live_nodes = jnp.arange(BLOCK, dtype=jnp.int32)[None, :] < counts_here[:, None]
        outputs = jnp.where(live_nodes[:, :, None], perceptron(blended, weights), 0.0).astype(jnp.bfloat16)
        pooled = jnp.sum(outputs.astype(jnp.float32), axis=1) / counts_here[:, None].astype(jnp.float32)
        return outputs, pooled

    node_out, pooled = lax.map(one_group, chosen)
    node_out = node_out.reshape(GRAPHS, BLOCK, H)
    pooled = pooled.reshape(GRAPHS, H)
    graph_ids = readout_ids[chosen.reshape(-1)]
    id_keys = jnp.arange(READOUTS, dtype=jnp.int32)
    members = (id_keys[:, None] == graph_ids[None, :]).astype(jnp.float32)
    readout = jnp.dot(members, pooled, precision=lax.Precision.HIGHEST, preferred_element_type=jnp.float32)
    return node_out, readout
```

```python
import functools

import jax
import jax.numpy as jnp
from jax import lax
from jax.experimental import pallas as pl
from jax.experimental.pallas import tpu as pltpu
from jax.sharding import PartitionSpec as P

MESH = pl.DeviceIdType.MESH
VMEM = pl.BlockSpec(memory_space=pltpu.VMEM)
SMEM = pl.BlockSpec(memory_space=pltpu.SMEM)
HBM = pl.BlockSpec(memory_space=pltpu.HBM)
PLANES = 4
UNIT = 16
CLASSES = (2, 3, 1, 0)
TIERS = ((36, 36, 68), (40, 36, 72), (48, 40, 76), (60, 48, 88))


def partners(step, sizes):
    rows, cols = sizes
    row, col = lax.axis_index("row"), lax.axis_index("col")
    by_row, by_col = step // cols, (step % cols) * 3 % cols
    to_row, to_col = (row + by_row) % rows, (col + by_col) % cols
    from_row, from_col = (row + rows - by_row) % rows, (col + cols - by_col) % cols
    return (to_row, to_col), to_row * cols + to_col, from_row * cols + from_col


def greet(sizes):
    barrier = pltpu.get_barrier_semaphore()
    devices = sizes[0] * sizes[1]

    def signal(step, carry):
        where, _, _ = partners(step, sizes)
        pl.semaphore_signal(barrier, inc=1, device_id=where, device_id_type=MESH)
        return carry

    lax.fori_loop(1, devices, signal, 0)
    return barrier


def gather_kernel(sizes, own_ref, all_ref, send_sem, recv_sem):
    devices = sizes[0] * sizes[1]
    me = lax.axis_index("row") * sizes[1] + lax.axis_index("col")
    barrier = greet(sizes)
    all_ref[me] = own_ref[0]
    pl.semaphore_wait(barrier, devices - 1)

    def copy(step, slot):
        where, _, _ = partners(step, sizes)
        return pltpu.make_async_remote_copy(
            src_ref=own_ref.at[0],
            dst_ref=all_ref.at[slot],
            send_sem=send_sem.at[step],
            recv_sem=recv_sem.at[step],
            device_id=where,
            device_id_type=MESH,
        )

    def send(step, carry):
        copy(step, me).start()
        return carry

    def finish(step, carry):
        _, _, source = partners(step, sizes)
        copy(step, me).wait_send()
        copy(step, source).wait_recv()
        return carry

    lax.fori_loop(1, devices, send, 0)
    lax.fori_loop(1, devices, finish, 0)


def gather_counts(node_counts, live_graphs, sizes):
    devices = sizes[0] * sizes[1]
    own = jnp.concatenate([node_counts, live_graphs])
    own = jnp.pad(own, (0, -own.shape[0] % 128)).reshape(1, 1, -1)
    every = pl.pallas_call(
        functools.partial(gather_kernel, sizes),
        out_shape=jax.ShapeDtypeStruct((devices, 1, own.shape[2]), jnp.int32),
        in_specs=[VMEM],
        out_specs=VMEM,
        scratch_shapes=[
            pltpu.SemaphoreType.DMA((devices,)),
            pltpu.SemaphoreType.DMA((devices,)),
        ],
        compiler_params=pltpu.CompilerParams(collective_id=0, has_side_effects=True),
        name="gather_counts",
    )(own)
    return every[:, 0, :]


def layer_kernel(
    sizes,
    bucket,
    picked_ref,
    counts_ref,
    arrival_ref,
    weight_ref,
    features_ref,
    edges_ref,
    ids_ref,
    w_first_ref,
    b_first_ref,
    w_second_ref,
    b_second_ref,
    w_third_ref,
    b_third_ref,
    out_ref,
    readout_ref,
    sent,
    arrived,
    pooled,
    terms,
    terms_in,
    send_sem,
    recv_sem,
    terms_send_sem,
    terms_recv_sem,
):
    devices = sizes[0] * sizes[1]
    read_rows = readout_ref.shape[0]
    block, hidden = features_ref.shape[1:]
    me = lax.axis_index("row") * sizes[1] + lax.axis_index("col")
    barrier = greet(sizes)

    def graph_copy(step, target, slot):
        where, _, _ = partners(step, sizes)
        return pltpu.make_async_remote_copy(
            src_ref=sent.at[target],
            dst_ref=arrived.at[slot],
            send_sem=send_sem.at[step],
            recv_sem=recv_sem.at[step],
            device_id=where,
            device_id_type=MESH,
        )

    def terms_copy(step, target, slot):
        where, _, _ = partners(step, sizes)
        return pltpu.make_async_remote_copy(
            src_ref=terms.at[target],
            dst_ref=terms_in.at[slot],
            send_sem=terms_send_sem.at[step],
            recv_sem=terms_recv_sem.at[step],
            device_id=where,
            device_id_type=MESH,
        )

    node_rows = lax.broadcasted_iota(jnp.int32, (block, edges_ref.shape[2]), 0)
    node_index = lax.broadcasted_iota(jnp.int32, (block, hidden), 0)

    def compute(target, store):
        blends = []
        for j in range(bucket):
            graph = picked_ref[target * bucket + j]
            features = features_ref[graph]
            edges = edges_ref[graph]
            sources = (node_rows == edges[0:1, :]).astype(jnp.float32).astype(jnp.bfloat16)
            targets = (node_rows == edges[1:2, :]).astype(jnp.float32).astype(jnp.bfloat16)
            adjacency = lax.dot_general(
                targets,
                sources,
                (((1,), (1,)), ((), ())),
                preferred_element_type=jnp.float32,
            ).astype(jnp.bfloat16)
            neighbour = jnp.dot(adjacency, features, preferred_element_type=jnp.float32)
            blends.append(
                (weight_ref[0] * features.astype(jnp.float32) + neighbour).astype(jnp.bfloat16)
            )
        blended = jnp.concatenate(blends, axis=0) if bucket > 1 else blends[0]
        hidden_one = jnp.maximum(
            jnp.dot(blended, w_first_ref[...], preferred_element_type=jnp.float32)
            + b_first_ref[...],
            0.0,
        ).astype(jnp.bfloat16)
        hidden_two = jnp.maximum(
            jnp.dot(hidden_one, w_second_ref[...], preferred_element_type=jnp.float32)
            + b_second_ref[...],
            0.0,
        ).astype(jnp.bfloat16)
        result = (
            jnp.dot(hidden_two, w_third_ref[...], preferred_element_type=jnp.float32)
            + b_third_ref[...]
        )
        for j in range(bucket):
            count = counts_ref[picked_ref[target * bucket + j]]
            rows = jnp.where(node_index < count, result[j * block : (j + 1) * block], 0.0)
            rows = rows.astype(jnp.bfloat16)
            store(j, rows)
            total = jnp.sum(rows.astype(jnp.float32), axis=0, keepdims=True)
            pooled[target * bucket + j] = total / jnp.full((1, hidden), count).astype(jnp.float32)

    pl.semaphore_wait(barrier, devices - 1)

    def compute_and_send(step, carry):
        _, target, _ = partners(step, sizes)

        def store(j, rows):
            sent[target, j] = rows

        compute(target, store)

        @pl.when(step > 0)
        def _():
            graph_copy(step, target, me).start()

        return carry

    lax.fori_loop(0, devices, compute_and_send, 0)
    for j in range(bucket):
        arrived[me, j] = sent[me, j]

    slots = devices * bucket
    keys = lax.broadcasted_iota(jnp.int32, (devices * read_rows, slots), 0)
    members = (keys == ids_ref[...]).astype(jnp.float32)
    all_terms = jnp.dot(
        members,
        pooled[...].reshape(slots, hidden),
        precision=lax.Precision.HIGHEST,
        preferred_element_type=jnp.float32,
    )
    terms[...] = all_terms.reshape(devices, read_rows, hidden)

    def send_terms(step, carry):
        _, target, _ = partners(step, sizes)
        terms_copy(step, target, me).start()
        return carry

    lax.fori_loop(1, devices, send_terms, 0)
    terms_in[me] = terms[me]

    def finish(step, carry):
        _, target, source = partners(step, sizes)
        graph_copy(step, target, me).wait_send()
        graph_copy(step, target, source).wait_recv()
        terms_copy(step, target, me).wait_send()
        terms_copy(step, target, source).wait_recv()
        return carry

    lax.fori_loop(1, devices, finish, 0)
    readout_ref[...] = jnp.sum(terms_in[...], axis=0)

    def place(slot, carry):
        which = arrival_ref[slot]
        out_ref[slot] = arrived[which // bucket, which % bucket]
        return carry

    lax.fori_loop(0, out_ref.shape[0], place, 0)


def relay_kernel(
    sizes,
    bucket,
    direct_units,
    spare_units,
    caps,
    table_ref,
    counts_ref,
    weight_ref,
    features_hbm_ref,
    edges_ref,
    ids_ref,
    w_first_ref,
    b_first_ref,
    w_second_ref,
    b_second_ref,
    w_third_ref,
    b_third_ref,
    out_ref,
    readout_ref,
    sent,
    arrived_a,
    arrived_b,
    arrived_c,
    mixed_a,
    mixed_b,
    firsts,
    merged,
    near,
    unpacked,
    pooled,
    terms,
    terms_in,
    plane_terms,
    final_terms,
    send_sem,
    recv_sem,
    first_send_sem,
    first_recv_sem,
    rest_send_sem,
    rest_recv_sem,
    merged_send_sem,
    merged_recv_sem,
    near_send_sem,
    near_recv_sem,
    terms_send_sem,
    terms_recv_sem,
    final_send_sem,
    final_recv_sem,
    out_sem,
    features_ref,
    load_sem,
):
    merge_units, rest_units, near_units = caps
    rows_n, cols_n = sizes
    devices = rows_n * cols_n
    width = cols_n // PLANES
    in_plane = rows_n * width
    read_rows = readout_ref.shape[0]
    block, hidden = features_ref.shape[1:]
    parts = block // UNIT
    slots = devices * bucket
    places = in_plane * bucket
    span = direct_units + spare_units
    list_at = slots
    merge_at = list_at + 3 * span
    final_at = merge_at + 2 * spare_units
    first_base = places * parts
    merged_base = first_base + 2 * direct_units
    near_base = merged_base + spare_units
    zero_base = near_base + span
    arrived = (arrived_a, arrived_b, arrived_c)
    mixed = (mixed_a, mixed_b)
    row, col = lax.axis_index("row"), lax.axis_index("col")
    plane, lane = col // width, col % width
    own_place = row * width + lane
    inner = plane % 2 + plane // 2 == 1

    def other_plane(k):
        return (plane // 2 + k // 2) % 2 * 2 + (plane % 2 + k % 2) % 2

    def neighbour_at(step):
        to_row, to_lane = (row + step // width) % rows_n, (lane + step % width) % width
        from_row = (row + rows_n - step // width) % rows_n
        from_lane = (lane + width - step % width) % width
        return (to_row, plane * width + to_lane), to_row, to_lane, from_row * width + from_lane

    barrier = pltpu.get_barrier_semaphore()

    def signal(step, carry):
        where, _, _, _ = neighbour_at(step)
        pl.semaphore_signal(barrier, inc=1, device_id=where, device_id_type=MESH)
        return carry

    lax.fori_loop(1, in_plane, signal, 0)
    for k in range(1, PLANES):
        where = (row, other_plane(k) * width + lane)
        pl.semaphore_signal(barrier, inc=1, device_id=where, device_id_type=MESH)
    quarter = features_ref.shape[0] // 4
    loads = [
        pltpu.make_async_copy(
            features_hbm_ref.at[pl.ds(n * quarter, quarter)],
            features_ref.at[pl.ds(n * quarter, quarter)],
            load_sem.at[n],
        )
        for n in range(4)
    ]
    for load in loads:
        load.start()
    unpacked[zero_base] = jnp.zeros((UNIT, hidden), jnp.bfloat16)

    def graph_copy(number, step, place):
        where, _, _, _ = neighbour_at(step)
        into = arrived[number] if number < 3 else unpacked
        return pltpu.make_async_remote_copy(
            src_ref=sent.at[number * in_plane + step],
            dst_ref=into.at[pl.ds(place * (bucket * parts), bucket * parts)],
            send_sem=send_sem.at[number * in_plane + step],
            recv_sem=recv_sem.at[number * in_plane + step],
            device_id=where,
            device_id_type=MESH,
        )

    def column_copy(source, target, send, recv, k):
        return pltpu.make_async_remote_copy(
            src_ref=source,
            dst_ref=target,
            send_sem=send,
            recv_sem=recv,
            device_id=(row, other_plane(k) * width + lane),
            device_id_type=MESH,
        )

    def first_copy(number):
        return column_copy(
            firsts.at[number],
            unpacked.at[pl.ds(first_base + number * direct_units, direct_units)],
            first_send_sem.at[number],
            first_recv_sem.at[number],
            CLASSES[number],
        )

    def rest_copy(number):
        return column_copy(
            mixed[number].at[pl.ds(0, rest_units)],
            mixed[1 - number].at[pl.ds(spare_units, rest_units)],
            rest_send_sem.at[number],
            rest_recv_sem.at[1 - number],
            1,
        )

    def merged_copy(number):
        return column_copy(
            merged.at[number],
            unpacked.at[pl.ds(merged_base, merge_units)],
            merged_send_sem.at[number],
            merged_recv_sem.at[0],
            CLASSES[number],
        )

    def near_copy():
        return column_copy(
            near,
            unpacked.at[pl.ds(near_base, near_units)],
            near_send_sem.at[0],
            near_recv_sem.at[0],
            1,
        )

    def terms_copy(step, target, slot):
        where, _, _, _ = neighbour_at(step)
        return pltpu.make_async_remote_copy(
            src_ref=terms.at[target],
            dst_ref=terms_in.at[slot],
            send_sem=terms_send_sem.at[step],
            recv_sem=terms_recv_sem.at[step],
            device_id=where,
            device_id_type=MESH,
        )

    def final_copy(k, to_plane, from_plane):
        return column_copy(
            plane_terms.at[to_plane],
            final_terms.at[from_plane],
            final_send_sem.at[k],
            final_recv_sem.at[k],
            k,
        )

    node_rows = lax.broadcasted_iota(jnp.int32, (block, edges_ref.shape[2]), 0)
    node_index = lax.broadcasted_iota(jnp.int32, (block, hidden), 0)

    def compute(targets, store):
        picks = [target * bucket + j for target in targets for j in range(bucket)]
        blends = []
        for pick in picks:
            graph = table_ref[pick]
            features = features_ref[graph]
            edges = edges_ref[graph]
            sources = (node_rows == edges[0:1, :]).astype(jnp.float32).astype(jnp.bfloat16)
            ends = (node_rows == edges[1:2, :]).astype(jnp.float32).astype(jnp.bfloat16)
            adjacency = lax.dot_general(
                ends,
                sources,
                (((1,), (1,)), ((), ())),
                preferred_element_type=jnp.float32,
            ).astype(jnp.bfloat16)
            neighbour = jnp.dot(adjacency, features, preferred_element_type=jnp.float32)
            blends.append(
                (weight_ref[0] * features.astype(jnp.float32) + neighbour).astype(jnp.bfloat16)
            )
        blended = jnp.concatenate(blends, axis=0)
        hidden_one = jnp.maximum(
            jnp.dot(blended, w_first_ref[...], preferred_element_type=jnp.float32)
            + b_first_ref[...],
            0.0,
        ).astype(jnp.bfloat16)
        hidden_two = jnp.maximum(
            jnp.dot(hidden_one, w_second_ref[...], preferred_element_type=jnp.float32)
            + b_second_ref[...],
            0.0,
        ).astype(jnp.bfloat16)
        result = (
            jnp.dot(hidden_two, w_third_ref[...], preferred_element_type=jnp.float32)
            + b_third_ref[...]
        )
        for n, pick in enumerate(picks):
            count = counts_ref[table_ref[pick]]
            rows = jnp.where(node_index < count, result[n * block : (n + 1) * block], 0.0)
            rows = rows.astype(jnp.bfloat16)
            store(n // bucket, n % bucket, rows.reshape(parts, UNIT, hidden))
            total = jnp.sum(rows.astype(jnp.float32), axis=0, keepdims=True)
            pooled[pick] = total / jnp.full((1, hidden), count).astype(jnp.float32)

    group = max(1, 4 // bucket)
    turns = in_plane // group

    def finish_stage(number):
        def finish(step, carry):
            _, _, _, source = neighbour_at(step)
            graph_copy(number, step, own_place).wait_send()
            graph_copy(number, step, source).wait_recv()
            return carry

        lax.fori_loop(1, in_plane, finish, 0)
        into = arrived[number] if number < 3 else unpacked
        for n in range(bucket * parts):
            into[own_place * (bucket * parts) + n] = sent[number * in_plane, n]

    def gather_units(source, table_base, count, store):
        def gather(step, carry):
            for n in range(4):
                unit = step * 4 + n
                store(unit, source[table_ref[table_base + unit]])
            return carry

        lax.fori_loop(0, count // 4, gather, 0)

    def send_far(number):
        finish_stage(number)
        base = list_at + number * span

        def store_first(unit, value):
            firsts[number, unit] = value

        def store_rest(unit, value):
            mixed[number][unit] = value

        gather_units(arrived[number], base, direct_units, store_first)
        first_copy(number).start()
        gather_units(
            arrived[number], base + direct_units, max(merge_units, rest_units), store_rest
        )

        @pl.when(jnp.logical_not(inner))
        def _():
            rest_copy(number).start()

    def send_merged():
        @pl.when(inner)
        def _():
            for number in range(2):
                rest_copy(1 - number).wait_recv()

                def store(unit, value, number=number):
                    merged[number, unit] = value

                gather_units(mixed[number], merge_at + number * spare_units, merge_units, store)
                merged_copy(number).start()

    def send_near():
        finish_stage(2)

        def store(unit, value):
            near[unit] = value

        gather_units(arrived[2], list_at + 2 * span, near_units, store)
        near_copy().start()

    def compute_class(turn, carry):
        @pl.when(turn == 3 * turns)
        def _():
            send_far(0)

        number = turn // turns
        half, parity = jnp.where(number < 2, 1, 0), jnp.where(number % 3 == 0, 0, 1)
        to_plane = (plane // 2 + half) % 2 * 2 + (plane % 2 + parity) % 2
        steps = [turn % turns * group + n for n in range(group)]
        targets = []
        for step in steps:
            _, to_row, to_lane, _ = neighbour_at(step)
            targets.append(to_row * cols_n + to_plane * width + to_lane)

        def store(n, j, rows):
            sent[number * in_plane + steps[n], pl.ds(j * parts, parts)] = rows

        compute(targets, store)
        for own_number in range(PLANES):

            @pl.when(number == own_number)
            def _():
                for n in range(1, group):
                    graph_copy(own_number, steps[n], own_place).start()

            @pl.when(jnp.logical_and(number == own_number, steps[0] > 0))
            def _():
                graph_copy(own_number, steps[0], own_place).start()

        return carry

    pl.semaphore_wait(barrier, in_plane - 1 + PLANES - 1)
    for load in loads:
        load.wait()
    lax.fori_loop(0, 4 * turns, compute_class, 0)

    keys = lax.broadcasted_iota(jnp.int32, (devices * read_rows, slots), 0)
    members = (keys == ids_ref[...]).astype(jnp.float32)
    all_terms = jnp.dot(
        members,
        pooled[...].reshape(slots, hidden),
        precision=lax.Precision.HIGHEST,
        preferred_element_type=jnp.float32,
    )
    for place in range(in_plane):
        for to_plane in range(PLANES):
            device = place // width * cols_n + to_plane * width + place % width
            terms[place, to_plane] = all_terms[device * read_rows : (device + 1) * read_rows]

    def send_terms(step, carry):
        _, to_row, to_lane, _ = neighbour_at(step)
        terms_copy(step, to_row * width + to_lane, own_place).start()
        return carry

    lax.fori_loop(1, in_plane, send_terms, 0)
    terms_in[own_place] = terms[own_place]

    send_far(1)
    send_merged()
    send_near()
    finish_stage(3)

    def finish_terms(step, carry):
        _, to_row, to_lane, source = neighbour_at(step)
        terms_copy(step, to_row * width + to_lane, own_place).wait_send()
        terms_copy(step, to_row * width + to_lane, source).wait_recv()
        return carry

    lax.fori_loop(1, in_plane, finish_terms, 0)
    plane_terms[...] = jnp.sum(terms_in[...], axis=0)
    final_terms[plane] = plane_terms[plane]
    for k in range(1, PLANES):
        final_copy(k, other_plane(k), plane).start()

    for number in range(2):
        first_copy(number).wait_send()
        first_copy(number).wait_recv()
    near_copy().wait_send()
    near_copy().wait_recv()

    @pl.when(inner)
    def _():
        for number in range(2):
            merged_copy(number).wait_send()

    @pl.when(jnp.logical_not(inner))
    def _():
        for number in range(2):
            rest_copy(number).wait_send()

    merged_copy(0).wait_recv()

    def out_copy(slot):
        return pltpu.make_async_copy(
            sent.at[slot // bucket, pl.ds(slot % bucket * parts, parts)],
            out_ref.at[slot],
            out_sem.at[slot],
        )

    def place_graph(slot, carry):
        for part in range(parts):
            value = unpacked[table_ref[final_at + slot * parts + part]]
            sent[slot // bucket, slot % bucket * parts + part] = value
        out_copy(slot).start()
        return carry

    lax.fori_loop(0, out_ref.shape[0], place_graph, 0)
    for k in range(1, PLANES):
        final_copy(k, other_plane(k), plane).wait_send()
        final_copy(k, other_plane(k), other_plane(k)).wait_recv()
    readout_ref[...] = jnp.sum(final_terms[...], axis=0)

    def finish_out(slot, carry):
        out_copy(slot).wait()
        return carry

    lax.fori_loop(0, out_ref.shape[0], finish_out, 0)


def body(
    sizes,
    node_features,
    node_counts,
    edge_list,
    readout_ids,
    live_graphs,
    self_weight,
    w_first,
    b_first,
    w_second,
    b_second,
    w_third,
    b_third,
):
    rows_n, cols_n = sizes
    devices = rows_n * cols_n
    width = cols_n // PLANES
    in_plane = rows_n * width
    capacity, block, hidden = node_features.shape
    parts = block // UNIT
    graphs_out = capacity // 2
    read_rows = 8
    bucket = (capacity + devices - 1) // devices
    slots_n = devices * bucket
    mean_units = graphs_out * parts // PLANES
    direct_units = mean_units // 2
    spare_units = mean_units
    span = direct_units + spare_units
    tiers = [tuple(mean_units * part // 64 for part in tier) for tier in TIERS]
    own_count = live_graphs[0]
    row, col = lax.axis_index("row"), lax.axis_index("col")
    plane, lane = col // width, col % width
    me = row * cols_n + col
    every = gather_counts(node_counts, live_graphs, sizes)
    every_count = every[:, capacity]
    earlier = jnp.arange(devices)[:, None] >= jnp.arange(devices)[None, :]
    inclusive = jnp.sum(jnp.where(earlier, every_count[None, :], 0), axis=1)
    offsets = inclusive - every_count
    offset = jnp.sum(jnp.where(jnp.arange(devices) == me, offsets, 0))
    slots = lax.broadcasted_iota(jnp.int32, (slots_n,), 0)
    within = (slots // bucket - offset) % devices + slots % bucket * devices
    picked = jnp.minimum(within, capacity - 1)
    choose = picked[:, None] == jnp.arange(capacity)[None, :]
    picked_ids = jnp.sum(jnp.where(choose, readout_ids[None, :], 0), axis=1)
    graph_ids = jnp.where(within < own_count, picked_ids, -1).reshape(1, -1)
    number = lax.broadcasted_iota(jnp.int32, (graphs_out,), 0) * devices + me
    passed = (inclusive[None, :] <= number[:, None]).astype(jnp.int32)
    source = jnp.sum(passed, axis=1)
    start = jnp.sum(passed * every_count[None, :], axis=1)
    turn = (number - start) // devices

    index = jnp.arange(capacity)[None, :]
    sizes_all = jnp.where(
        index < every_count[:, None], (every[:, :capacity] + (UNIT - 1)) // UNIT, 0
    )
    dests = (offsets[:, None] + index) % devices
    by_dest = jnp.sum(
        jnp.where(dests[:, :, None] == jnp.arange(devices), sizes_all[:, :, None], 0), axis=1
    )
    plane_load = jnp.sum(by_dest.reshape(rows_n, PLANES, width, devices), axis=(0, 2))
    planes = jnp.arange(PLANES)[:, None]
    to_planes = jnp.arange(devices)[None, :] % cols_n // width
    far = planes // 2 != to_planes // 2
    plane_rest = jnp.where(far, jnp.maximum(plane_load - direct_units, 0), 0)
    is_inner = planes % 2 + planes // 2 == 1
    most_merged = jnp.max(jnp.sum(plane_rest, axis=0))
    most_rest = jnp.max(jnp.where(is_inner, 0, plane_rest))
    most_near = jnp.max(jnp.where(far | (planes == to_planes), 0, plane_load))
    tier = sum(
        ((most_merged > merge) | (most_rest > rest) | (most_near > near)).astype(jnp.int32)
        for merge, rest, near in tiers
    )

    turns = jnp.arange(bucket)[:, None] == index // devices

    def by_plane(values):
        values = values.reshape(rows_n, PLANES, width, capacity)
        return jnp.swapaxes(values, 0, 1).reshape(PLANES, in_plane, capacity)

    plane_sizes, plane_dests = by_plane(sizes_all), by_plane(dests)
    own_sizes = lax.dynamic_index_in_dim(plane_sizes, plane, 0, keepdims=False)
    own_dests = lax.dynamic_index_in_dim(plane_dests, plane, 0, keepdims=False)

    def slot_sizes(values, wanted):
        chosen = wanted[:, :, None, :] & turns
        return jnp.sum(jnp.where(chosen, values[:, :, None, :], 0), axis=3).reshape(wanted.shape[0], -1)

    other = [
        (plane // 2 + k // 2) % 2 * 2 + (plane % 2 + k % 2) % 2 for k in CLASSES[:3]
    ]
    relay_dests = row * cols_n + jnp.stack(other) * width + lane
    relay_sizes = slot_sizes(own_sizes[None], own_dests[None] == relay_dests[:, None, None])
    final_sizes = slot_sizes(plane_sizes, plane_dests == me)
    places = in_plane * bucket
    before = jnp.arange(places)[:, None] >= jnp.arange(places)[None, :]

    def ends(values):
        return jnp.sum(jnp.where(before, values[:, None, :], 0), axis=2)

    relay_ends = ends(relay_sizes)
    done = relay_ends[:, None, :] <= jnp.arange(span)[None, :, None]
    slot_of = jnp.minimum(jnp.sum(done.astype(jnp.int32), axis=2), places - 1)
    part_of = jnp.arange(span) - jnp.sum(jnp.where(done, relay_sizes[:, None, :], 0), axis=2)
    lists = slot_of * parts + jnp.clip(part_of, 0, parts - 1)
    own_rest = jnp.maximum(relay_ends[:2, -1:] - direct_units, 0)
    spare = jnp.arange(spare_units)[None, :]
    merge_list = jnp.where(spare < own_rest, spare, spare_units + spare - own_rest)

    final_ends = ends(final_sizes)
    starts = final_ends - final_sizes
    source_row, source_col = source // cols_n, source % cols_n
    source_plane = source_col // width
    place = (source_row * width + source_col % width) * bucket + turn
    match = (source_plane * places + place)[:, None] == jnp.arange(PLANES * places)[None, :]
    base = jnp.sum(jnp.where(match, starts.reshape(1, -1), 0), axis=1)[:, None]
    size = jnp.sum(jnp.where(match, final_sizes.reshape(1, -1), 0), axis=1)[:, None]
    inner_plane = 2 - plane // 2
    totals = jnp.sum(jnp.where(jnp.arange(PLANES) == inner_plane, final_ends[:, -1], 0))
    inner_rest = jnp.maximum(totals - direct_units, 0)
    first_base = places * parts
    merged_base = first_base + 2 * direct_units
    near_base = merged_base + spare_units
    zero_base = near_base + span
    from_far = (source_plane // 2 != plane // 2)[:, None]
    same_side = (source_plane % 2 == plane % 2)[:, None]
    from_inner = (source_plane == inner_plane)[:, None]
    part = jnp.arange(parts)[None, :]
    at = base + part
    at_first = first_base + jnp.where(same_side, 0, direct_units) + at
    at_merged = merged_base + jnp.where(from_inner, 0, inner_rest) + at - direct_units
    at_far = jnp.where(at < direct_units, at_first, at_merged)
    at_near = jnp.where(same_side, place[:, None] * parts + part, near_base + at)
    final = jnp.where(part < size, jnp.where(from_far, at_far, at_near), zero_base)
    final = jnp.clip(final, 0, zero_base)
    table = jnp.concatenate(
        [picked, lists.reshape(-1), merge_list.reshape(-1), final.reshape(-1)]
    ).astype(jnp.int32)
    arrival = (source * bucket + turn).astype(jnp.int32)

    out_shape = (
        jax.ShapeDtypeStruct((graphs_out, block, hidden), jnp.bfloat16),
        jax.ShapeDtypeStruct((read_rows, hidden), jnp.float32),
    )
    pooled_scratch = pltpu.VMEM((slots_n, 1, hidden), jnp.float32)

    def semaphores(count):
        return [pltpu.SemaphoreType.DMA((count,)), pltpu.SemaphoreType.DMA((count,))]

    def relayed(tier, caps, *operands):
        table, _, node_counts = operands[:3]
        merge_units, rest_units, near_units = caps

        def graphs(*count):
            return pltpu.VMEM((*count, UNIT, hidden), jnp.bfloat16)

        whole_terms = pltpu.VMEM((in_plane, PLANES, read_rows, hidden), jnp.float32)
        some_terms = pltpu.VMEM((PLANES, read_rows, hidden), jnp.float32)
        node_out, readout = pl.pallas_call(
            functools.partial(relay_kernel, sizes, bucket, direct_units, spare_units, caps),
            out_shape=(
                jax.ShapeDtypeStruct((graphs_out, parts, UNIT, hidden), jnp.bfloat16),
                out_shape[1],
            ),
            in_specs=[SMEM] * 3 + [HBM] + [VMEM] * 8,
            out_specs=(HBM, VMEM),
            scratch_shapes=[graphs(devices, bucket * parts)]
            + [graphs(places * parts)] * 3
            + [graphs(2 * spare_units)] * 2
            + [
                graphs(2, direct_units),
                graphs(2, merge_units),
                graphs(near_units),
                graphs(zero_base + 1),
            ]
            + [pooled_scratch, whole_terms, whole_terms, some_terms, some_terms]
            + semaphores(devices)
            + semaphores(2)
            + semaphores(2)
            + semaphores(2)
            + semaphores(1)
            + semaphores(in_plane)
            + semaphores(PLANES)
            + [
                pltpu.SemaphoreType.DMA((graphs_out,)),
                pltpu.VMEM((capacity, block, hidden), jnp.bfloat16),
                pltpu.SemaphoreType.DMA((4,)),
            ],
            compiler_params=pltpu.CompilerParams(
                collective_id=2 + tier, has_side_effects=True, vmem_limit_bytes=61 * 1024 * 1024
            ),
            name="gin_relay",
        )(table, node_counts, *operands[3:])
        return node_out.reshape(graphs_out, block, hidden), readout

    def direct(*operands):
        table, arrival, node_counts = operands[:3]
        all_terms = pltpu.VMEM((devices, read_rows, hidden), jnp.float32)
        graphs = pltpu.VMEM((devices, bucket, block, hidden), jnp.bfloat16)
        return pl.pallas_call(
            functools.partial(layer_kernel, sizes, bucket),
            out_shape=out_shape,
            in_specs=[SMEM] * 4 + [VMEM] * 9,
            out_specs=(VMEM, VMEM),
            scratch_shapes=[graphs, graphs]
            + [pooled_scratch, all_terms, all_terms]
            + semaphores(devices)
            + semaphores(devices),
            compiler_params=pltpu.CompilerParams(
                collective_id=1, has_side_effects=True, vmem_limit_bytes=60 * 1024 * 1024
            ),
            name="gin_direct",
        )(table[:slots_n], node_counts, arrival, *operands[3:])

    branches = [functools.partial(relayed, number, cap) for number, cap in enumerate(tiers)]
    return lax.switch(
        tier,
        branches + [direct],
        table,
        arrival,
        node_counts,
        self_weight,
        node_features,
        edge_list,
        graph_ids,
        w_first,
        b_first.reshape(1, -1),
        w_second,
        b_second.reshape(1, -1),
        w_third,
        b_third.reshape(1, -1),
    )


def solution(mesh):
    sizes = (mesh.shape["row"], mesh.shape["col"])
    both = ("row", "col")
    in_specs = (
        P(both, None, None),
        P(both),
        P(both, None, None),
        P(both),
        P(both),
        P(),
        P(),
        P(),
        P(),
        P(),
        P(),
        P(),
    )
    out_specs = (P(both, None, None), P(both, None))
    return jax.shard_map(
        functools.partial(body, sizes),
        mesh=mesh,
        in_specs=in_specs,
        out_specs=out_specs,
        check_vma=False,
    )
```

```python
import functools

import jax
import jax.numpy as jnp
from jax import lax
from jax.experimental import pallas as pl
from jax.experimental.pallas import tpu as pltpu
from jax.sharding import PartitionSpec as P

MESH = pl.DeviceIdType.MESH
VMEM = pl.BlockSpec(memory_space=pltpu.VMEM)
SMEM = pl.BlockSpec(memory_space=pltpu.SMEM)
HBM = pl.BlockSpec(memory_space=pltpu.HBM)
PLANES = 4
UNIT = 16
LANES = 128
CLASSES = (2, 3, 1, 0)
TIERS = ((36, 36, 68), (40, 36, 72), (48, 40, 76), (60, 48, 88))


def partners(step, sizes):
    rows, cols = sizes
    row, col = lax.axis_index("row"), lax.axis_index("col")
    by_row, by_col = step // cols, (step % cols) * 3 % cols
    to_row, to_col = (row + by_row) % rows, (col + by_col) % cols
    from_row, from_col = (row + rows - by_row) % rows, (col + cols - by_col) % cols
    return (to_row, to_col), to_row * cols + to_col, from_row * cols + from_col


def greet(sizes):
    barrier = pltpu.get_barrier_semaphore()
    devices = sizes[0] * sizes[1]

    def signal(step, carry):
        where, _, _ = partners(step, sizes)
        pl.semaphore_signal(barrier, inc=1, device_id=where, device_id_type=MESH)
        return carry

    lax.fori_loop(1, devices, signal, 0)
    return barrier


def gather_kernel(sizes, counts_ref, live_ref, all_ref, own, send_sem, recv_sem):
    devices = sizes[0] * sizes[1]
    capacity = counts_ref.shape[1]
    me = lax.axis_index("row") * sizes[1] + lax.axis_index("col")
    barrier = greet(sizes)
    own[:, :capacity] = counts_ref[...]
    own[:, capacity:] = jnp.full((1, own.shape[1] - capacity), live_ref[0])
    all_ref[me] = own[...]
    pl.semaphore_wait(barrier, devices - 1)

    def copy(step, slot):
        where, _, _ = partners(step, sizes)
        return pltpu.make_async_remote_copy(
            src_ref=own,
            dst_ref=all_ref.at[slot],
            send_sem=send_sem.at[step],
            recv_sem=recv_sem.at[step],
            device_id=where,
            device_id_type=MESH,
        )

    def send(step, carry):
        copy(step, me).start()
        return carry

    def finish(step, carry):
        _, _, source = partners(step, sizes)
        copy(step, me).wait_send()
        copy(step, source).wait_recv()
        return carry

    lax.fori_loop(1, devices, send, 0)
    lax.fori_loop(1, devices, finish, 0)


def gather_counts(node_counts, live_graphs, sizes):
    devices = sizes[0] * sizes[1]
    return pl.pallas_call(
        functools.partial(gather_kernel, sizes),
        out_shape=jax.ShapeDtypeStruct((devices, 1, LANES), jnp.int32),
        in_specs=[VMEM, SMEM],
        out_specs=VMEM,
        scratch_shapes=[
            pltpu.VMEM((1, LANES), jnp.int32),
            pltpu.SemaphoreType.DMA((devices,)),
            pltpu.SemaphoreType.DMA((devices,)),
        ],
        compiler_params=pltpu.CompilerParams(collective_id=0, has_side_effects=True),
        name="gather_counts",
    )(node_counts.reshape(1, -1), live_graphs)


def plan_kernel(
    sizes, capacity, bucket, parts, graphs_out, units, tiers, every_ref, ids_ref,
    table_ref, extra_ref, tier_ref,
):
    direct_units, spare_units = units
    rows_n, cols_n = sizes
    devices = rows_n * cols_n
    bits = devices.bit_length() - 1
    width = cols_n // PLANES
    places = rows_n * width * bucket
    row, col = lax.axis_index("row"), lax.axis_index("col")
    plane, lane = col // width, col % width
    me = row * cols_n + col
    shape = (devices, LANES)
    lanes = lax.broadcasted_iota(jnp.int32, shape, 1)
    owner = lax.broadcasted_iota(jnp.int32, (devices, 1), 0)
    owner_col = owner & (cols_n - 1)
    owner_plane = owner_col >> (width.bit_length() - 1)
    owner_place = (owner >> (cols_n.bit_length() - 1)) * width + (owner & (width - 1))

    def total(values, axis):
        return jnp.sum(values.astype(jnp.float32), axis=axis, keepdims=True).astype(jnp.int32)

    def column(values, index):
        return total(jnp.where(lanes == index, values, 0), 1)

    def product(left, right):
        left, right = left.astype(jnp.float32), right.astype(jnp.float32)
        exact = jnp.dot(
            left.astype(jnp.bfloat16),
            right.astype(jnp.bfloat16),
            preferred_element_type=jnp.float32,
        )
        return exact.astype(jnp.int32)

    every = every_ref[:, 0, :]
    live = column(every, capacity)
    first = lax.broadcasted_iota(jnp.int32, (devices, devices), 0)
    second = lax.broadcasted_iota(jnp.int32, (devices, devices), 1)
    offset = column(product((second < first).astype(jnp.int32), every), capacity)
    sizes_all = jnp.where(lanes < live, (every + (UNIT - 1)) >> (UNIT.bit_length() - 1), 0)

    def turned(values, by, turn):
        values = jnp.where((lanes[: values.shape[0]] >> bits) == turn, values, 0)
        shift = devices
        while shift < LANES:
            values = values + pltpu.roll(values, shift, 1)
            shift *= 2
        for bit in range(bits):
            rolled = pltpu.roll(values, 1 << bit, 1)
            values = jnp.where(((by >> bit) & 1) == 1, rolled, values)
        return values

    by_turn = [turned(sizes_all, offset, turn) for turn in range(bucket)]
    size_sum = sum(by_turn)
    same_plane = ((first & (cols_n - 1)) >> (width.bit_length() - 1)) == (
        (second & (cols_n - 1)) >> (width.bit_length() - 1)
    )
    start = product((same_plane & (second < first)).astype(jnp.int32), size_sum)
    starts = [start]
    for turn in range(1, bucket):
        starts.append(starts[-1] + by_turn[turn - 1])

    plane_row = lax.broadcasted_iota(jnp.int32, (8, devices), 0)
    plane_of = lax.broadcasted_iota(jnp.int32, (8, devices), 1)
    plane_of = (plane_of & (cols_n - 1)) >> (width.bit_length() - 1)
    plane_load = product((plane_row == plane_of).astype(jnp.int32), size_sum)
    planes = lax.broadcasted_iota(jnp.int32, (8, LANES), 0)
    to_planes = lax.broadcasted_iota(jnp.int32, (8, LANES), 1) & (cols_n - 1)
    to_planes = to_planes >> (width.bit_length() - 1)
    far = ((planes >> 1) != (to_planes >> 1)) & (planes < PLANES)
    plane_rest = jnp.where(far, jnp.maximum(plane_load - direct_units, 0), 0)
    is_inner = ((planes & 1) + (planes >> 1)) == 1
    merged_load = total(plane_rest, 0)
    rest_load = jnp.where(is_inner, 0, plane_rest)
    near_load = jnp.where(((planes ^ to_planes) == 1), plane_load, 0)
    most_merged = jnp.max(merged_load.astype(jnp.float32))
    most_rest = jnp.max(rest_load.astype(jnp.float32))
    most_near = jnp.max(near_load.astype(jnp.float32))
    tier = jnp.int32(0)
    for merge, rest, near in tiers:
        over = (most_merged > merge) | (most_rest > rest) | (most_near > near)
        tier = tier + jnp.where(over, 1, 0)
    tier_ref[0] = tier

    line = lax.broadcasted_iota(jnp.int32, (1, LANES), 1)
    own_offset = total(jnp.where(owner == me, offset, 0), 0)
    own_live = total(jnp.where(owner == me, live, 0), 0)
    within = ((line - own_offset) & (devices - 1)) + (line >> bits) * devices
    table_ref[0:1, :] = jnp.minimum(within, capacity - 1)

    ids = jnp.where(line < capacity, jnp.concatenate([ids_ref[...]] * (LANES // capacity), 1), 0)
    slot_ids = jnp.zeros((1, LANES), jnp.int32)
    for turn in range(bucket):
        slot_ids = jnp.where((line >> bits) == turn, turned(ids, own_offset, turn), slot_ids)
    extra_ref[0:1, :] = jnp.where(within < own_live, slot_ids, -1)

    for number, k in enumerate(CLASSES[:3]):
        to_plane = (plane // 2 + k // 2) % 2 * 2 + (plane % 2 + k % 2) % 2
        target = row * cols_n + to_plane * width + lane
        listed = jnp.zeros(shape, jnp.int32)
        used = jnp.zeros((devices, 1), jnp.int32)
        for turn in range(bucket):
            size = column(by_turn[turn], target)
            size = jnp.where(owner_plane == plane, size, 0)
            at = lanes - column(starts[turn], target)
            base = (owner_place * bucket + turn) * parts
            listed = listed + jnp.where((at >= 0) & (at < size), base + at, 0)
            used = used + size
        table_ref[1 + number : 2 + number, :] = total(listed, 0)
        if number < 2:
            own_rest = jnp.maximum(total(used, 0) - direct_units, 0)
            merged = jnp.where(line < own_rest, line, spare_units + line - own_rest)
            merged = jnp.minimum(jnp.maximum(merged, 0), 2 * spare_units - 1)
            table_ref[4 + number : 5 + number, :] = merged

    inner_plane = 2 - plane // 2
    own_sizes = [column(by_turn[turn], me) for turn in range(bucket)]
    inner_rest = total(jnp.where(owner_plane == inner_plane, sum(own_sizes), 0), 0)
    inner_rest = jnp.maximum(inner_rest - direct_units, 0)
    first_base = places * parts
    merged_base = first_base + 2 * direct_units
    near_base = merged_base + spare_units
    zero_base = near_base + direct_units + spare_units
    from_own, from_near = owner_plane == plane, (owner_plane ^ 1) == plane
    is_inner = owner_plane == inner_plane
    same_side = (owner_plane & 1) == plane % 2
    low = jnp.where(from_near, near_base, first_base + jnp.where(same_side, 0, direct_units))
    low = jnp.where(from_own, 0, low)
    high = merged_base - direct_units + jnp.where(is_inner, 0, inner_rest)
    high = jnp.where(from_own | from_near, low, high)
    finals = [jnp.zeros(shape, jnp.int32) for _ in range(graphs_out * parts // LANES)]
    arrival = jnp.zeros(shape, jnp.int32)
    part = lanes & (parts - 1)
    graph = lanes >> (parts.bit_length() - 1)
    for turn in range(bucket):
        within = ((me - offset) & (devices - 1)) + turn * devices
        place = jnp.where(within < live, (offset + within) >> bits, -1)
        begin = jnp.where(from_own, (owner_place * bucket + turn) * parts, column(starts[turn], me))
        at = begin + part
        address = jnp.where(at < direct_units, low + at, high + at)
        address = jnp.where(part < own_sizes[turn], address - zero_base, 0)
        for half in range(len(finals)):
            mine = graph + half * (LANES // parts) == place
            finals[half] = finals[half] + jnp.where(mine, address, 0)
        arrival = arrival + jnp.where(lanes == place, owner * bucket + turn, 0)
    for half, values in enumerate(finals):
        address = jnp.clip(total(values, 0) + zero_base, 0, zero_base)
        table_ref[6 + half : 7 + half, :] = address
    extra_ref[1:2, :] = total(arrival, 0)


def layer_kernel(
    sizes,
    bucket,
    picked_ref,
    counts_ref,
    arrival_ref,
    weight_ref,
    features_ref,
    edges_ref,
    ids_ref,
    w_first_ref,
    b_first_ref,
    w_second_ref,
    b_second_ref,
    w_third_ref,
    b_third_ref,
    out_ref,
    readout_ref,
    sent,
    arrived,
    pooled,
    terms,
    terms_in,
    send_sem,
    recv_sem,
    terms_send_sem,
    terms_recv_sem,
):
    devices = sizes[0] * sizes[1]
    read_rows = readout_ref.shape[0]
    block, hidden = features_ref.shape[1:]
    me = lax.axis_index("row") * sizes[1] + lax.axis_index("col")
    barrier = greet(sizes)

    def graph_copy(step, target, slot):
        where, _, _ = partners(step, sizes)
        return pltpu.make_async_remote_copy(
            src_ref=sent.at[target],
            dst_ref=arrived.at[slot],
            send_sem=send_sem.at[step],
            recv_sem=recv_sem.at[step],
            device_id=where,
            device_id_type=MESH,
        )

    def terms_copy(step, target, slot):
        where, _, _ = partners(step, sizes)
        return pltpu.make_async_remote_copy(
            src_ref=terms.at[target],
            dst_ref=terms_in.at[slot],
            send_sem=terms_send_sem.at[step],
            recv_sem=terms_recv_sem.at[step],
            device_id=where,
            device_id_type=MESH,
        )

    node_rows = lax.broadcasted_iota(jnp.int32, (block, edges_ref.shape[2]), 0)
    node_index = lax.broadcasted_iota(jnp.int32, (block, hidden), 0)

    def compute(target, store):
        blends = []
        for j in range(bucket):
            graph = picked_ref[j * devices + target]
            features = features_ref[graph]
            edges = edges_ref[graph]
            sources = (node_rows == edges[0:1, :]).astype(jnp.float32).astype(jnp.bfloat16)
            targets = (node_rows == edges[1:2, :]).astype(jnp.float32).astype(jnp.bfloat16)
            adjacency = lax.dot_general(
                targets,
                sources,
                (((1,), (1,)), ((), ())),
                preferred_element_type=jnp.float32,
            ).astype(jnp.bfloat16)
            neighbour = jnp.dot(adjacency, features, preferred_element_type=jnp.float32)
            blends.append(
                (weight_ref[0] * features.astype(jnp.float32) + neighbour).astype(jnp.bfloat16)
            )
        blended = jnp.concatenate(blends, axis=0) if bucket > 1 else blends[0]
        hidden_one = jnp.maximum(
            jnp.dot(blended, w_first_ref[...], preferred_element_type=jnp.float32)
            + b_first_ref[...],
            0.0,
        ).astype(jnp.bfloat16)
        hidden_two = jnp.maximum(
            jnp.dot(hidden_one, w_second_ref[...], preferred_element_type=jnp.float32)
            + b_second_ref[...],
            0.0,
        ).astype(jnp.bfloat16)
        result = (
            jnp.dot(hidden_two, w_third_ref[...], preferred_element_type=jnp.float32)
            + b_third_ref[...]
        )
        for j in range(bucket):
            count = counts_ref[picked_ref[j * devices + target]]
            rows = jnp.where(node_index < count, result[j * block : (j + 1) * block], 0.0)
            rows = rows.astype(jnp.bfloat16)
            store(j, rows)
            total = jnp.sum(rows.astype(jnp.float32), axis=0, keepdims=True)
            pooled[j * devices + target] = total / jnp.full((1, hidden), count).astype(jnp.float32)

    pl.semaphore_wait(barrier, devices - 1)

    def compute_and_send(step, carry):
        _, target, _ = partners(step, sizes)

        def store(j, rows):
            sent[target, j] = rows

        compute(target, store)

        @pl.when(step > 0)
        def _():
            graph_copy(step, target, me).start()

        return carry

    lax.fori_loop(0, devices, compute_and_send, 0)
    for j in range(bucket):
        arrived[me, j] = sent[me, j]

    slots = devices * bucket
    keys = lax.broadcasted_iota(jnp.int32, (devices * read_rows, slots), 0)
    members = (keys == ids_ref[0:1, :slots]).astype(jnp.float32)
    all_terms = jnp.dot(
        members,
        pooled[...].reshape(slots, hidden),
        precision=lax.Precision.HIGHEST,
        preferred_element_type=jnp.float32,
    )
    terms[...] = all_terms.reshape(devices, read_rows, hidden)

    def send_terms(step, carry):
        _, target, _ = partners(step, sizes)
        terms_copy(step, target, me).start()
        return carry

    lax.fori_loop(1, devices, send_terms, 0)
    terms_in[me] = terms[me]

    def finish(step, carry):
        _, target, source = partners(step, sizes)
        graph_copy(step, target, me).wait_send()
        graph_copy(step, target, source).wait_recv()
        terms_copy(step, target, me).wait_send()
        terms_copy(step, target, source).wait_recv()
        return carry

    lax.fori_loop(1, devices, finish, 0)
    readout_ref[...] = jnp.sum(terms_in[...], axis=0)

    def place(slot, carry):
        which = arrival_ref[slot]
        out_ref[slot] = arrived[which // bucket, which % bucket]
        return carry

    lax.fori_loop(0, out_ref.shape[0], place, 0)


def relay_kernel(
    sizes,
    bucket,
    direct_units,
    spare_units,
    caps,
    table_ref,
    counts_ref,
    weight_ref,
    features_hbm_ref,
    edges_ref,
    ids_ref,
    w_first_ref,
    b_first_ref,
    w_second_ref,
    b_second_ref,
    w_third_ref,
    b_third_ref,
    out_ref,
    readout_ref,
    sent,
    arrived_a,
    arrived_b,
    arrived_c,
    mixed_a,
    mixed_b,
    firsts,
    merged,
    near,
    unpacked,
    pooled,
    terms,
    terms_in,
    plane_terms,
    final_terms,
    send_sem,
    recv_sem,
    first_send_sem,
    first_recv_sem,
    rest_send_sem,
    rest_recv_sem,
    merged_send_sem,
    merged_recv_sem,
    near_send_sem,
    near_recv_sem,
    terms_send_sem,
    terms_recv_sem,
    final_send_sem,
    final_recv_sem,
    out_sem,
    features_ref,
    load_sem,
):
    merge_units, rest_units, near_units = caps
    rows_n, cols_n = sizes
    devices = rows_n * cols_n
    width = cols_n // PLANES
    in_plane = rows_n * width
    read_rows = readout_ref.shape[0]
    block, hidden = features_ref.shape[1:]
    parts = block // UNIT
    slots = devices * bucket
    places = in_plane * bucket
    span = direct_units + spare_units
    list_at, merge_at, final_at = LANES, 4 * LANES, 6 * LANES
    first_base = places * parts
    merged_base = first_base + 2 * direct_units
    near_base = merged_base + spare_units
    zero_base = near_base + span
    arrived = (arrived_a, arrived_b, arrived_c)
    mixed = (mixed_a, mixed_b)
    row, col = lax.axis_index("row"), lax.axis_index("col")
    plane, lane = col // width, col % width
    own_place = row * width + lane
    inner = plane % 2 + plane // 2 == 1

    def other_plane(k):
        return (plane // 2 + k // 2) % 2 * 2 + (plane % 2 + k % 2) % 2

    def neighbour_at(step):
        to_row, to_lane = (row + step // width) % rows_n, (lane + step % width) % width
        from_row = (row + rows_n - step // width) % rows_n
        from_lane = (lane + width - step % width) % width
        return (to_row, plane * width + to_lane), to_row, to_lane, from_row * width + from_lane

    barrier = pltpu.get_barrier_semaphore()

    def signal(step, carry):
        where, _, _, _ = neighbour_at(step)
        pl.semaphore_signal(barrier, inc=1, device_id=where, device_id_type=MESH)
        return carry

    lax.fori_loop(1, in_plane, signal, 0)
    for k in range(1, PLANES):
        where = (row, other_plane(k) * width + lane)
        pl.semaphore_signal(barrier, inc=1, device_id=where, device_id_type=MESH)
    quarter = features_ref.shape[0] // 4
    loads = [
        pltpu.make_async_copy(
            features_hbm_ref.at[pl.ds(n * quarter, quarter)],
            features_ref.at[pl.ds(n * quarter, quarter)],
            load_sem.at[n],
        )
        for n in range(4)
    ]
    for load in loads:
        load.start()
    unpacked[zero_base] = jnp.zeros((UNIT, hidden), jnp.bfloat16)

    def graph_copy(number, step, place):
        where, _, _, _ = neighbour_at(step)
        into = arrived[number] if number < 3 else unpacked
        return pltpu.make_async_remote_copy(
            src_ref=sent.at[number * in_plane + step],
            dst_ref=into.at[pl.ds(place * (bucket * parts), bucket * parts)],
            send_sem=send_sem.at[number * in_plane + step],
            recv_sem=recv_sem.at[number * in_plane + step],
            device_id=where,
            device_id_type=MESH,
        )

    def column_copy(source, target, send, recv, k):
        return pltpu.make_async_remote_copy(
            src_ref=source,
            dst_ref=target,
            send_sem=send,
            recv_sem=recv,
            device_id=(row, other_plane(k) * width + lane),
            device_id_type=MESH,
        )

    def first_copy(number):
        return column_copy(
            firsts.at[number],
            unpacked.at[pl.ds(first_base + number * direct_units, direct_units)],
            first_send_sem.at[number],
            first_recv_sem.at[number],
            CLASSES[number],
        )

    def rest_copy(number):
        return column_copy(
            mixed[number].at[pl.ds(0, rest_units)],
            mixed[1 - number].at[pl.ds(spare_units, rest_units)],
            rest_send_sem.at[number],
            rest_recv_sem.at[1 - number],
            1,
        )

    def merged_copy(number):
        return column_copy(
            merged.at[number],
            unpacked.at[pl.ds(merged_base, merge_units)],
            merged_send_sem.at[number],
            merged_recv_sem.at[0],
            CLASSES[number],
        )

    def near_copy():
        return column_copy(
            near,
            unpacked.at[pl.ds(near_base, near_units)],
            near_send_sem.at[0],
            near_recv_sem.at[0],
            1,
        )

    def terms_copy(step, target, slot):
        where, _, _, _ = neighbour_at(step)
        return pltpu.make_async_remote_copy(
            src_ref=terms.at[target],
            dst_ref=terms_in.at[slot],
            send_sem=terms_send_sem.at[step],
            recv_sem=terms_recv_sem.at[step],
            device_id=where,
            device_id_type=MESH,
        )

    def final_copy(k, to_plane, from_plane):
        return column_copy(
            plane_terms.at[to_plane],
            final_terms.at[from_plane],
            final_send_sem.at[k],
            final_recv_sem.at[k],
            k,
        )

    node_rows = lax.broadcasted_iota(jnp.int32, (block, edges_ref.shape[2]), 0)
    node_index = lax.broadcasted_iota(jnp.int32, (block, hidden), 0)

    def compute(targets, store):
        picks = [j * devices + target for target in targets for j in range(bucket)]
        blends = []
        for pick in picks:
            graph = table_ref[pick]
            features = features_ref[graph]
            edges = edges_ref[graph]
            sources = (node_rows == edges[0:1, :]).astype(jnp.float32).astype(jnp.bfloat16)
            ends = (node_rows == edges[1:2, :]).astype(jnp.float32).astype(jnp.bfloat16)
            adjacency = lax.dot_general(
                ends,
                sources,
                (((1,), (1,)), ((), ())),
                preferred_element_type=jnp.float32,
            ).astype(jnp.bfloat16)
            neighbour = jnp.dot(adjacency, features, preferred_element_type=jnp.float32)
            blends.append(
                (weight_ref[0] * features.astype(jnp.float32) + neighbour).astype(jnp.bfloat16)
            )
        blended = jnp.concatenate(blends, axis=0)
        hidden_one = jnp.maximum(
            jnp.dot(blended, w_first_ref[...], preferred_element_type=jnp.float32)
            + b_first_ref[...],
            0.0,
        ).astype(jnp.bfloat16)
        hidden_two = jnp.maximum(
            jnp.dot(hidden_one, w_second_ref[...], preferred_element_type=jnp.float32)
            + b_second_ref[...],
            0.0,
        ).astype(jnp.bfloat16)
        result = (
            jnp.dot(hidden_two, w_third_ref[...], preferred_element_type=jnp.float32)
            + b_third_ref[...]
        )
        for n, pick in enumerate(picks):
            count = counts_ref[table_ref[pick]]
            rows = jnp.where(node_index < count, result[n * block : (n + 1) * block], 0.0)
            rows = rows.astype(jnp.bfloat16)
            store(n // bucket, n % bucket, rows.reshape(parts, UNIT, hidden))
            total = jnp.sum(rows.astype(jnp.float32), axis=0, keepdims=True)
            pooled[pick] = total / jnp.full((1, hidden), count).astype(jnp.float32)

    group = max(1, 4 // bucket)
    turns = in_plane // group

    def finish_stage(number):
        def finish(step, carry):
            _, _, _, source = neighbour_at(step)
            graph_copy(number, step, own_place).wait_send()
            graph_copy(number, step, source).wait_recv()
            return carry

        lax.fori_loop(1, in_plane, finish, 0)
        into = arrived[number] if number < 3 else unpacked
        for n in range(bucket * parts):
            into[own_place * (bucket * parts) + n] = sent[number * in_plane, n]

    def gather_units(source, table_base, count, store):
        def gather(step, carry):
            for n in range(4):
                unit = step * 4 + n
                store(unit, source[table_ref[table_base + unit]])
            return carry

        lax.fori_loop(0, count // 4, gather, 0)

    def send_far(number):
        finish_stage(number)
        base = list_at + number * LANES

        def store_first(unit, value):
            firsts[number, unit] = value

        def store_rest(unit, value):
            mixed[number][unit] = value

        gather_units(arrived[number], base, direct_units, store_first)
        first_copy(number).start()
        gather_units(
            arrived[number], base + direct_units, max(merge_units, rest_units), store_rest
        )

        @pl.when(jnp.logical_not(inner))
        def _():
            rest_copy(number).start()

    def send_merged():
        @pl.when(inner)
        def _():
            for number in range(2):
                rest_copy(1 - number).wait_recv()

                def store(unit, value, number=number):
                    merged[number, unit] = value

                gather_units(mixed[number], merge_at + number * LANES, merge_units, store)
                merged_copy(number).start()

    def send_near():
        finish_stage(2)

        def store(unit, value):
            near[unit] = value

        gather_units(arrived[2], list_at + 2 * LANES, near_units, store)
        near_copy().start()

    def compute_class(turn, carry):
        @pl.when(turn == 3 * turns)
        def _():
            send_far(0)

        number = turn // turns
        half, parity = jnp.where(number < 2, 1, 0), jnp.where(number % 3 == 0, 0, 1)
        to_plane = (plane // 2 + half) % 2 * 2 + (plane % 2 + parity) % 2
        steps = [turn % turns * group + n for n in range(group)]
        targets = []
        for step in steps:
            _, to_row, to_lane, _ = neighbour_at(step)
            targets.append(to_row * cols_n + to_plane * width + to_lane)

        def store(n, j, rows):
            sent[number * in_plane + steps[n], pl.ds(j * parts, parts)] = rows

        compute(targets, store)
        for own_number in range(PLANES):

            @pl.when(number == own_number)
            def _():
                for n in range(1, group):
                    graph_copy(own_number, steps[n], own_place).start()

            @pl.when(jnp.logical_and(number == own_number, steps[0] > 0))
            def _():
                graph_copy(own_number, steps[0], own_place).start()

        return carry

    pl.semaphore_wait(barrier, in_plane - 1 + PLANES - 1)
    for load in loads:
        load.wait()
    lax.fori_loop(0, 4 * turns, compute_class, 0)

    keys = lax.broadcasted_iota(jnp.int32, (devices * read_rows, slots), 0)
    members = (keys == ids_ref[0:1, :slots]).astype(jnp.float32)
    all_terms = jnp.dot(
        members,
        pooled[...].reshape(slots, hidden),
        precision=lax.Precision.HIGHEST,
        preferred_element_type=jnp.float32,
    )
    for place in range(in_plane):
        for to_plane in range(PLANES):
            device = place // width * cols_n + to_plane * width + place % width
            terms[place, to_plane] = all_terms[device * read_rows : (device + 1) * read_rows]

    def send_terms(step, carry):
        _, to_row, to_lane, _ = neighbour_at(step)
        terms_copy(step, to_row * width + to_lane, own_place).start()
        return carry

    lax.fori_loop(1, in_plane, send_terms, 0)
    terms_in[own_place] = terms[own_place]

    send_far(1)
    send_merged()
    send_near()
    finish_stage(3)

    def finish_terms(step, carry):
        _, to_row, to_lane, source = neighbour_at(step)
        terms_copy(step, to_row * width + to_lane, own_place).wait_send()
        terms_copy(step, to_row * width + to_lane, source).wait_recv()
        return carry

    lax.fori_loop(1, in_plane, finish_terms, 0)
    plane_terms[...] = jnp.sum(terms_in[...], axis=0)
    final_terms[plane] = plane_terms[plane]
    for k in range(1, PLANES):
        final_copy(k, other_plane(k), plane).start()

    for number in range(2):
        first_copy(number).wait_send()
        first_copy(number).wait_recv()
    near_copy().wait_send()
    near_copy().wait_recv()

    @pl.when(inner)
    def _():
        for number in range(2):
            merged_copy(number).wait_send()

    @pl.when(jnp.logical_not(inner))
    def _():
        for number in range(2):
            rest_copy(number).wait_send()

    merged_copy(0).wait_recv()

    def out_copy(slot):
        return pltpu.make_async_copy(
            sent.at[slot // bucket, pl.ds(slot % bucket * parts, parts)],
            out_ref.at[slot],
            out_sem.at[slot],
        )

    def place_graph(slot, carry):
        for part in range(parts):
            value = unpacked[table_ref[final_at + slot * parts + part]]
            sent[slot // bucket, slot % bucket * parts + part] = value
        out_copy(slot).start()
        return carry

    lax.fori_loop(0, out_ref.shape[0], place_graph, 0)
    for k in range(1, PLANES):
        final_copy(k, other_plane(k), plane).wait_send()
        final_copy(k, other_plane(k), other_plane(k)).wait_recv()
    readout_ref[...] = jnp.sum(final_terms[...], axis=0)

    def finish_out(slot, carry):
        out_copy(slot).wait()
        return carry

    lax.fori_loop(0, out_ref.shape[0], finish_out, 0)


def body(
    sizes,
    node_features,
    node_counts,
    edge_list,
    readout_ids,
    live_graphs,
    self_weight,
    w_first,
    b_first,
    w_second,
    b_second,
    w_third,
    b_third,
):
    rows_n, cols_n = sizes
    devices = rows_n * cols_n
    width = cols_n // PLANES
    in_plane = rows_n * width
    capacity, block, hidden = node_features.shape
    parts = block // UNIT
    graphs_out = capacity // 2
    read_rows = 8
    bucket = (capacity + devices - 1) // devices
    slots_n = devices * bucket
    mean_units = graphs_out * parts // PLANES
    direct_units = mean_units // 2
    spare_units = mean_units
    span = direct_units + spare_units
    tiers = [tuple(mean_units * part // 64 for part in tier) for tier in TIERS]
    places = in_plane * bucket
    zero_base = places * parts + 3 * direct_units + 2 * spare_units
    every = gather_counts(node_counts, live_graphs, sizes)
    table, extra, tier = pl.pallas_call(
        functools.partial(
            plan_kernel,
            sizes,
            capacity,
            bucket,
            parts,
            graphs_out,
            (direct_units, spare_units),
            tiers,
        ),
        out_shape=(
            jax.ShapeDtypeStruct((6 + graphs_out * parts // LANES, LANES), jnp.int32),
            jax.ShapeDtypeStruct((8, LANES), jnp.int32),
            jax.ShapeDtypeStruct((1,), jnp.int32),
        ),
        in_specs=[VMEM, VMEM],
        out_specs=(VMEM, VMEM, SMEM),
        name="plan",
    )(every, readout_ids.reshape(1, -1))
    table = table.reshape(-1)

    out_shape = (
        jax.ShapeDtypeStruct((graphs_out, block, hidden), jnp.bfloat16),
        jax.ShapeDtypeStruct((read_rows, hidden), jnp.float32),
    )
    pooled_scratch = pltpu.VMEM((slots_n, 1, hidden), jnp.float32)

    def semaphores(count):
        return [pltpu.SemaphoreType.DMA((count,)), pltpu.SemaphoreType.DMA((count,))]

    def relayed(tier, caps, *operands):
        table, extra, node_counts, self_weight, node_features, edge_list = operands[:6]
        merge_units, rest_units, near_units = caps

        def graphs(*count):
            return pltpu.VMEM((*count, UNIT, hidden), jnp.bfloat16)

        whole_terms = pltpu.VMEM((in_plane, PLANES, read_rows, hidden), jnp.float32)
        some_terms = pltpu.VMEM((PLANES, read_rows, hidden), jnp.float32)
        node_out, readout = pl.pallas_call(
            functools.partial(relay_kernel, sizes, bucket, direct_units, spare_units, caps),
            out_shape=(
                jax.ShapeDtypeStruct((graphs_out, parts, UNIT, hidden), jnp.bfloat16),
                out_shape[1],
            ),
            in_specs=[SMEM] * 3 + [HBM] + [VMEM] * 8,
            out_specs=(HBM, VMEM),
            scratch_shapes=[graphs(devices, bucket * parts)]
            + [graphs(places * parts)] * 3
            + [graphs(2 * spare_units)] * 2
            + [
                graphs(2, direct_units),
                graphs(2, merge_units),
                graphs(near_units),
                graphs(zero_base + 1),
            ]
            + [pooled_scratch, whole_terms, whole_terms, some_terms, some_terms]
            + semaphores(devices)
            + semaphores(2)
            + semaphores(2)
            + semaphores(2)
            + semaphores(1)
            + semaphores(in_plane)
            + semaphores(PLANES)
            + [
                pltpu.SemaphoreType.DMA((graphs_out,)),
                pltpu.VMEM((capacity, block, hidden), jnp.bfloat16),
                pltpu.SemaphoreType.DMA((4,)),
            ],
            compiler_params=pltpu.CompilerParams(
                collective_id=2 + tier, has_side_effects=True, vmem_limit_bytes=61 * 1024 * 1024
            ),
            name="gin_relay",
        )(table, node_counts, self_weight, node_features, edge_list, extra, *operands[6:])
        return node_out.reshape(graphs_out, block, hidden), readout

    def direct(*operands):
        table, extra, node_counts, self_weight, node_features, edge_list = operands[:6]
        all_terms = pltpu.VMEM((devices, read_rows, hidden), jnp.float32)
        graphs = pltpu.VMEM((devices, bucket, block, hidden), jnp.bfloat16)
        return pl.pallas_call(
            functools.partial(layer_kernel, sizes, bucket),
            out_shape=out_shape,
            in_specs=[SMEM] * 4 + [VMEM] * 9,
            out_specs=(VMEM, VMEM),
            scratch_shapes=[graphs, graphs]
            + [pooled_scratch, all_terms, all_terms]
            + semaphores(devices)
            + semaphores(devices),
            compiler_params=pltpu.CompilerParams(
                collective_id=1, has_side_effects=True, vmem_limit_bytes=60 * 1024 * 1024
            ),
            name="gin_direct",
        )(
            table,
            node_counts,
            extra[1],
            self_weight,
            node_features,
            edge_list,
            extra,
            *operands[6:],
        )

    branches = [functools.partial(relayed, number, cap) for number, cap in enumerate(tiers)]
    return lax.switch(
        tier[0],
        branches + [direct],
        table,
        extra,
        node_counts,
        self_weight,
        node_features,
        edge_list,
        w_first,
        b_first.reshape(1, -1),
        w_second,
        b_second.reshape(1, -1),
        w_third,
        b_third.reshape(1, -1),
    )


def solution(mesh):
    sizes = (mesh.shape["row"], mesh.shape["col"])
    both = ("row", "col")
    in_specs = (
        P(both, None, None),
        P(both),
        P(both, None, None),
        P(both),
        P(both),
        P(),
        P(),
        P(),
        P(),
        P(),
        P(),
        P(),
    )
    out_specs = (P(both, None, None), P(both, None))
    return jax.shard_map(
        functools.partial(body, sizes),
        mesh=mesh,
        in_specs=in_specs,
        out_specs=out_specs,
        check_vma=False,
    )
```

```python
import functools

import jax
import jax.numpy as jnp
from jax import lax
from jax.experimental import pallas as pl
from jax.experimental.pallas import tpu as pltpu
from jax.sharding import PartitionSpec as P

MESH = pl.DeviceIdType.MESH
VMEM = pl.BlockSpec(memory_space=pltpu.VMEM)
SMEM = pl.BlockSpec(memory_space=pltpu.SMEM)
HBM = pl.BlockSpec(memory_space=pltpu.HBM)
PLANES = 4
UNIT = 16
LANES = 128
CLASSES = (2, 3, 1, 0)
TIERS = ((36, 36, 40), (40, 36, 40), (44, 36, 40), (52, 40, 44), (60, 48, 56))


def partners(step, sizes):
    rows, cols = sizes
    row, col = lax.axis_index("row"), lax.axis_index("col")
    by_row, by_col = step // cols, (step % cols) * 3 % cols
    to_row, to_col = (row + by_row) % rows, (col + by_col) % cols
    from_row, from_col = (row + rows - by_row) % rows, (col + cols - by_col) % cols
    return (to_row, to_col), to_row * cols + to_col, from_row * cols + from_col


def greet(sizes):
    barrier = pltpu.get_barrier_semaphore()
    devices = sizes[0] * sizes[1]

    def signal(step, carry):
        where, _, _ = partners(step, sizes)
        pl.semaphore_signal(barrier, inc=1, device_id=where, device_id_type=MESH)
        return carry

    lax.fori_loop(1, devices, signal, 0)
    return barrier


def gather_kernel(sizes, counts_ref, live_ref, all_ref, own, send_sem, recv_sem):
    devices = sizes[0] * sizes[1]
    capacity = counts_ref.shape[1]
    me = lax.axis_index("row") * sizes[1] + lax.axis_index("col")
    barrier = greet(sizes)
    own[:, :capacity] = counts_ref[...]
    own[:, capacity:] = jnp.full((1, own.shape[1] - capacity), live_ref[0])
    all_ref[me] = own[...]
    pl.semaphore_wait(barrier, devices - 1)

    def copy(step, slot):
        where, _, _ = partners(step, sizes)
        return pltpu.make_async_remote_copy(
            src_ref=own,
            dst_ref=all_ref.at[slot],
            send_sem=send_sem.at[step],
            recv_sem=recv_sem.at[step],
            device_id=where,
            device_id_type=MESH,
        )

    def send(step, carry):
        copy(step, me).start()
        return carry

    def finish(step, carry):
        _, _, source = partners(step, sizes)
        copy(step, me).wait_send()
        copy(step, source).wait_recv()
        return carry

    lax.fori_loop(1, devices, send, 0)
    lax.fori_loop(1, devices, finish, 0)


def gather_counts(node_counts, live_graphs, sizes):
    devices = sizes[0] * sizes[1]
    return pl.pallas_call(
        functools.partial(gather_kernel, sizes),
        out_shape=jax.ShapeDtypeStruct((devices, 1, LANES), jnp.int32),
        in_specs=[VMEM, SMEM],
        out_specs=VMEM,
        scratch_shapes=[
            pltpu.VMEM((1, LANES), jnp.int32),
            pltpu.SemaphoreType.DMA((devices,)),
            pltpu.SemaphoreType.DMA((devices,)),
        ],
        compiler_params=pltpu.CompilerParams(collective_id=0, has_side_effects=True),
        name="gather_counts",
    )(node_counts.reshape(1, -1), live_graphs)


def plan_kernel(
    sizes, capacity, bucket, parts, graphs_out, units, tiers, every_ref, ids_ref,
    table_ref, extra_ref, tier_ref,
):
    direct_units, spare_units = units
    rows_n, cols_n = sizes
    devices = rows_n * cols_n
    bits = devices.bit_length() - 1
    width = cols_n // PLANES
    in_plane = rows_n * width
    places = in_plane * bucket
    row, col = lax.axis_index("row"), lax.axis_index("col")
    plane, lane = col // width, col % width
    me = row * cols_n + col
    shape = (devices, LANES)
    lanes = lax.broadcasted_iota(jnp.int32, shape, 1)
    owner = lax.broadcasted_iota(jnp.int32, (devices, 1), 0)
    owner_col = owner & (cols_n - 1)
    owner_plane = owner_col >> (width.bit_length() - 1)
    owner_place = (owner >> (cols_n.bit_length() - 1)) * width + (owner & (width - 1))

    def total(values, axis):
        return jnp.sum(values.astype(jnp.float32), axis=axis, keepdims=True).astype(jnp.int32)

    def column(values, index):
        return total(jnp.where(lanes == index, values, 0), 1)

    def product(left, right):
        left, right = left.astype(jnp.float32), right.astype(jnp.float32)
        exact = jnp.dot(
            left.astype(jnp.bfloat16),
            right.astype(jnp.bfloat16),
            preferred_element_type=jnp.float32,
        )
        return exact.astype(jnp.int32)

    every = every_ref[:, 0, :]
    live = column(every, capacity)
    first = lax.broadcasted_iota(jnp.int32, (devices, devices), 0)
    second = lax.broadcasted_iota(jnp.int32, (devices, devices), 1)
    offset = column(product((second < first).astype(jnp.int32), every), capacity)
    sizes_all = jnp.where(lanes < live, (every + (UNIT - 1)) >> (UNIT.bit_length() - 1), 0)

    def turned(values, by, turn):
        values = jnp.where((lanes[: values.shape[0]] >> bits) == turn, values, 0)
        shift = devices
        while shift < LANES:
            values = values + pltpu.roll(values, shift, 1)
            shift *= 2
        for bit in range(bits):
            rolled = pltpu.roll(values, 1 << bit, 1)
            values = jnp.where(((by >> bit) & 1) == 1, rolled, values)
        return values

    by_turn = [turned(sizes_all, offset, turn) for turn in range(bucket)]
    size_sum = sum(by_turn)
    early = by_turn[0]
    same_plane = ((first & (cols_n - 1)) >> (width.bit_length() - 1)) == (
        (second & (cols_n - 1)) >> (width.bit_length() - 1)
    )
    starts, begun = [], jnp.zeros(shape, jnp.int32)
    for turn in range(bucket):
        earlier = (same_plane & (second < first)).astype(jnp.int32)
        starts.append(begun + product(earlier, by_turn[turn]))
        begun = begun + product(same_plane.astype(jnp.int32), by_turn[turn])
        if turn == 0:
            firsts = jnp.minimum(begun, direct_units)

    plane_row = lax.broadcasted_iota(jnp.int32, (8, devices), 0)
    plane_of = lax.broadcasted_iota(jnp.int32, (8, devices), 1)
    plane_of = (plane_of & (cols_n - 1)) >> (width.bit_length() - 1)
    of_plane = (plane_row == plane_of).astype(jnp.int32)
    plane_load = product(of_plane, size_sum)
    plane_load = plane_load - jnp.minimum(product(of_plane, early), direct_units)
    planes = lax.broadcasted_iota(jnp.int32, (8, LANES), 0)
    to_planes = lax.broadcasted_iota(jnp.int32, (8, LANES), 1) & (cols_n - 1)
    to_planes = to_planes >> (width.bit_length() - 1)
    far = ((planes >> 1) != (to_planes >> 1)) & (planes < PLANES)
    plane_rest = jnp.where(far, plane_load, 0)
    is_inner = ((planes & 1) + (planes >> 1)) == 1
    merged_load = total(plane_rest, 0)
    rest_load = jnp.where(is_inner, 0, plane_rest)
    near_load = jnp.where(((planes ^ to_planes) == 1), plane_load, 0)
    most_merged = jnp.max(merged_load.astype(jnp.float32))
    most_rest = jnp.max(rest_load.astype(jnp.float32))
    most_near = jnp.max(near_load.astype(jnp.float32))
    tier = jnp.int32(0)
    for merge, rest, near in tiers:
        over = (most_merged > merge) | (most_rest > rest) | (most_near > near)
        tier = tier + jnp.where(over, 1, 0)
    tier_ref[0] = tier

    line = lax.broadcasted_iota(jnp.int32, (1, LANES), 1)
    own_offset = total(jnp.where(owner == me, offset, 0), 0)
    own_live = total(jnp.where(owner == me, live, 0), 0)
    within = ((line - own_offset) & (devices - 1)) + (line >> bits) * devices
    table_ref[0:1, :] = jnp.minimum(within, capacity - 1)

    ids = jnp.where(line < capacity, jnp.concatenate([ids_ref[...]] * (LANES // capacity), 1), 0)
    slot_ids = jnp.zeros((1, LANES), jnp.int32)
    for turn in range(bucket):
        slot_ids = jnp.where((line >> bits) == turn, turned(ids, own_offset, turn), slot_ids)
    extra_ref[0:1, :] = jnp.where(within < own_live, slot_ids, -1)

    for number, k in enumerate(CLASSES[:3]):
        to_plane = (plane // 2 + k // 2) % 2 * 2 + (plane % 2 + k % 2) % 2
        target = row * cols_n + to_plane * width + lane
        listed = jnp.zeros(shape, jnp.int32)
        used = jnp.zeros((devices, 1), jnp.int32)
        sent_first = jnp.where(owner_plane == plane, column(firsts, target), 0)
        sent_first = jnp.max(sent_first.astype(jnp.float32), axis=0, keepdims=True)
        sent_first = sent_first.astype(jnp.int32)
        unit = jnp.where(line < direct_units, line, sent_first + line - direct_units)
        for turn in range(bucket):
            size = column(by_turn[turn], target)
            size = jnp.where(owner_plane == plane, size, 0)
            at = unit - column(starts[turn], target)
            base = (turn * in_plane + owner_place) * parts
            listed = listed + jnp.where((at >= 0) & (at < size), base + at, 0)
            used = used + size
        listed = total(listed, 0)
        listed = jnp.where(
            line < direct_units, jnp.minimum(listed, in_plane * parts - 1), listed
        )
        table_ref[1 + number : 2 + number, :] = listed
        if number < 2:
            own_rest = total(used, 0) - sent_first
            merged = jnp.where(line < own_rest, line, spare_units + line - own_rest)
            merged = jnp.minimum(jnp.maximum(merged, 0), 2 * spare_units - 1)
            table_ref[4 + number : 5 + number, :] = merged

    inner_plane = 2 - plane // 2
    own_sizes = [column(by_turn[turn], me) for turn in range(bucket)]
    own_firsts = column(firsts, me)
    from_inner = owner_plane == inner_plane
    inner_first = jnp.where(from_inner, own_firsts, 0).astype(jnp.float32)
    inner_first = jnp.max(inner_first, axis=0, keepdims=True).astype(jnp.int32)
    inner_rest = total(jnp.where(from_inner, sum(own_sizes), 0), 0) - inner_first
    first_base = places * parts
    merged_base = first_base + 3 * direct_units
    near_base = merged_base + spare_units
    zero_base = near_base + spare_units
    from_own, from_near = owner_plane == plane, (owner_plane ^ 1) == plane
    same_side = (owner_plane & 1) == plane % 2
    low = jnp.where(from_near, 2 * direct_units, jnp.where(same_side, 0, direct_units))
    low = first_base + low
    high = jnp.where(from_near, near_base, merged_base + jnp.where(from_inner, 0, inner_rest))
    high = high - own_firsts
    finals = [jnp.zeros(shape, jnp.int32) for _ in range(graphs_out * parts // LANES)]
    arrival = jnp.zeros(shape, jnp.int32)
    part = lanes & (parts - 1)
    graph = lanes >> (parts.bit_length() - 1)
    for turn in range(bucket):
        within = ((me - offset) & (devices - 1)) + turn * devices
        place = jnp.where(within < live, (offset + within) >> bits, -1)
        at = column(starts[turn], me) + part
        address = jnp.where(at < own_firsts, low + at, high + at)
        held = (turn * in_plane + owner_place) * parts + part
        address = jnp.where(from_own, held, address)
        address = jnp.where(part < own_sizes[turn], address - zero_base, 0)
        for half in range(len(finals)):
            mine = graph + half * (LANES // parts) == place
            finals[half] = finals[half] + jnp.where(mine, address, 0)
        arrival = arrival + jnp.where(lanes == place, owner * bucket + turn, 0)
    for half, values in enumerate(finals):
        address = jnp.clip(total(values, 0) + zero_base, 0, zero_base)
        table_ref[6 + half : 7 + half, :] = address
    extra_ref[1:2, :] = total(arrival, 0)


def layer_kernel(
    sizes,
    bucket,
    picked_ref,
    counts_ref,
    arrival_ref,
    weight_ref,
    features_ref,
    edges_ref,
    ids_ref,
    w_first_ref,
    b_first_ref,
    w_second_ref,
    b_second_ref,
    w_third_ref,
    b_third_ref,
    out_ref,
    readout_ref,
    sent,
    arrived,
    pooled,
    terms,
    terms_in,
    send_sem,
    recv_sem,
    terms_send_sem,
    terms_recv_sem,
):
    devices = sizes[0] * sizes[1]
    read_rows = readout_ref.shape[0]
    block, hidden = features_ref.shape[1:]
    me = lax.axis_index("row") * sizes[1] + lax.axis_index("col")
    barrier = greet(sizes)

    def graph_copy(step, target, slot):
        where, _, _ = partners(step, sizes)
        return pltpu.make_async_remote_copy(
            src_ref=sent.at[target],
            dst_ref=arrived.at[slot],
            send_sem=send_sem.at[step],
            recv_sem=recv_sem.at[step],
            device_id=where,
            device_id_type=MESH,
        )

    def terms_copy(step, target, slot):
        where, _, _ = partners(step, sizes)
        return pltpu.make_async_remote_copy(
            src_ref=terms.at[target],
            dst_ref=terms_in.at[slot],
            send_sem=terms_send_sem.at[step],
            recv_sem=terms_recv_sem.at[step],
            device_id=where,
            device_id_type=MESH,
        )

    node_rows = lax.broadcasted_iota(jnp.int32, (block, edges_ref.shape[2]), 0)
    node_index = lax.broadcasted_iota(jnp.int32, (block, hidden), 0)

    def compute(target, store):
        blends = []
        for j in range(bucket):
            graph = picked_ref[j * devices + target]
            features = features_ref[graph]
            edges = edges_ref[graph]
            sources = (node_rows == edges[0:1, :]).astype(jnp.float32).astype(jnp.bfloat16)
            targets = (node_rows == edges[1:2, :]).astype(jnp.float32).astype(jnp.bfloat16)
            adjacency = lax.dot_general(
                targets,
                sources,
                (((1,), (1,)), ((), ())),
                preferred_element_type=jnp.float32,
            ).astype(jnp.bfloat16)
            neighbour = jnp.dot(adjacency, features, preferred_element_type=jnp.float32)
            blends.append(
                (weight_ref[0] * features.astype(jnp.float32) + neighbour).astype(jnp.bfloat16)
            )
        blended = jnp.concatenate(blends, axis=0) if bucket > 1 else blends[0]
        hidden_one = jnp.maximum(
            jnp.dot(blended, w_first_ref[...], preferred_element_type=jnp.float32)
            + b_first_ref[...],
            0.0,
        ).astype(jnp.bfloat16)
        hidden_two = jnp.maximum(
            jnp.dot(hidden_one, w_second_ref[...], preferred_element_type=jnp.float32)
            + b_second_ref[...],
            0.0,
        ).astype(jnp.bfloat16)
        result = (
            jnp.dot(hidden_two, w_third_ref[...], preferred_element_type=jnp.float32)
            + b_third_ref[...]
        )
        for j in range(bucket):
            count = counts_ref[picked_ref[j * devices + target]]
            rows = jnp.where(node_index < count, result[j * block : (j + 1) * block], 0.0)
            rows = rows.astype(jnp.bfloat16)
            store(j, rows)
            total = jnp.sum(rows.astype(jnp.float32), axis=0, keepdims=True)
            pooled[j * devices + target] = total / jnp.full((1, hidden), count).astype(jnp.float32)

    pl.semaphore_wait(barrier, devices - 1)

    def compute_and_send(step, carry):
        _, target, _ = partners(step, sizes)

        def store(j, rows):
            sent[target, j] = rows

        compute(target, store)

        @pl.when(step > 0)
        def _():
            graph_copy(step, target, me).start()

        return carry

    lax.fori_loop(0, devices, compute_and_send, 0)
    for j in range(bucket):
        arrived[me, j] = sent[me, j]

    slots = devices * bucket
    keys = lax.broadcasted_iota(jnp.int32, (devices * read_rows, slots), 0)
    members = (keys == ids_ref[0:1, :slots]).astype(jnp.float32)
    all_terms = jnp.dot(
        members,
        pooled[...].reshape(slots, hidden),
        precision=lax.Precision.HIGHEST,
        preferred_element_type=jnp.float32,
    )
    terms[...] = all_terms.reshape(devices, read_rows, hidden)

    def send_terms(step, carry):
        _, target, _ = partners(step, sizes)
        terms_copy(step, target, me).start()
        return carry

    lax.fori_loop(1, devices, send_terms, 0)
    terms_in[me] = terms[me]

    def finish(step, carry):
        _, target, source = partners(step, sizes)
        graph_copy(step, target, me).wait_send()
        graph_copy(step, target, source).wait_recv()
        terms_copy(step, target, me).wait_send()
        terms_copy(step, target, source).wait_recv()
        return carry

    lax.fori_loop(1, devices, finish, 0)
    readout_ref[...] = jnp.sum(terms_in[...], axis=0)

    def place(slot, carry):
        which = arrival_ref[slot]
        out_ref[slot] = arrived[which // bucket, which % bucket]
        return carry

    lax.fori_loop(0, out_ref.shape[0], place, 0)


def relay_kernel(
    sizes,
    bucket,
    direct_units,
    spare_units,
    caps,
    table_ref,
    counts_ref,
    weight_ref,
    features_hbm_ref,
    edges_ref,
    ids_ref,
    w_first_ref,
    b_first_ref,
    w_second_ref,
    b_second_ref,
    w_third_ref,
    b_third_ref,
    out_ref,
    readout_ref,
    sent,
    early_a,
    early_b,
    early_c,
    arrived_a,
    arrived_b,
    arrived_c,
    mixed_a,
    mixed_b,
    firsts,
    merged,
    near,
    unpacked,
    pooled,
    terms,
    terms_in,
    plane_terms,
    final_terms,
    send_sem,
    recv_sem,
    first_send_sem,
    first_recv_sem,
    rest_send_sem,
    rest_recv_sem,
    merged_send_sem,
    merged_recv_sem,
    near_send_sem,
    near_recv_sem,
    terms_send_sem,
    terms_recv_sem,
    final_send_sem,
    final_recv_sem,
    out_sem,
    features_ref,
    load_sem,
):
    merge_units, rest_units, near_units = caps
    rows_n, cols_n = sizes
    devices = rows_n * cols_n
    width = cols_n // PLANES
    in_plane = rows_n * width
    read_rows = readout_ref.shape[0]
    block, hidden = features_ref.shape[1:]
    parts = block // UNIT
    slots = devices * bucket
    places = in_plane * bucket
    list_at, merge_at, final_at = LANES, 4 * LANES, 6 * LANES
    first_base = places * parts
    merged_base = first_base + 3 * direct_units
    near_base = merged_base + spare_units
    zero_base = near_base + spare_units
    early = (early_a, early_b, early_c)
    arrived = (arrived_a, arrived_b, arrived_c) if bucket > 1 else early
    mixed = (mixed_a, mixed_b)
    row, col = lax.axis_index("row"), lax.axis_index("col")
    plane, lane = col // width, col % width
    own_place = row * width + lane
    inner = plane % 2 + plane // 2 == 1

    def other_plane(k):
        return (plane // 2 + k // 2) % 2 * 2 + (plane % 2 + k % 2) % 2

    def neighbour_at(step):
        to_row, to_lane = (row + step // width) % rows_n, (lane + step % width) % width
        from_row = (row + rows_n - step // width) % rows_n
        from_lane = (lane + width - step % width) % width
        return (to_row, plane * width + to_lane), to_row, to_lane, from_row * width + from_lane

    barrier = pltpu.get_barrier_semaphore()

    def signal(step, carry):
        where, _, _, _ = neighbour_at(step)
        pl.semaphore_signal(barrier, inc=1, device_id=where, device_id_type=MESH)
        return carry

    lax.fori_loop(1, in_plane, signal, 0)
    for k in range(1, PLANES):
        where = (row, other_plane(k) * width + lane)
        pl.semaphore_signal(barrier, inc=1, device_id=where, device_id_type=MESH)
    quarter = features_ref.shape[0] // 4
    loads = [
        pltpu.make_async_copy(
            features_hbm_ref.at[pl.ds(n * quarter, quarter)],
            features_ref.at[pl.ds(n * quarter, quarter)],
            load_sem.at[n],
        )
        for n in range(4)
    ]
    for load in loads:
        load.start()
    unpacked[zero_base] = jnp.zeros((UNIT, hidden), jnp.bfloat16)

    stages = [(0, 0), (1, 0)]
    for late in ((0, 1), (2,), (3,)):
        for turn in range(bucket):
            stages += [(number, turn) for number in late if (number, turn) not in stages]

    def landing(stage, place):
        number, turn = stages[stage]
        if number < 3 and turn == 0:
            return early[number].at[pl.ds(place * parts, parts)]
        into = arrived[number] if number < 3 else unpacked
        return into.at[pl.ds((turn * in_plane + place) * parts, parts)]

    def graph_copy(stage, step, place):
        where, _, _, _ = neighbour_at(step)
        return pltpu.make_async_remote_copy(
            src_ref=sent.at[stage * in_plane + step],
            dst_ref=landing(stage, place),
            send_sem=send_sem.at[stage * in_plane + step],
            recv_sem=recv_sem.at[stage * in_plane + step],
            device_id=where,
            device_id_type=MESH,
        )

    def column_copy(source, target, send, recv, k):
        return pltpu.make_async_remote_copy(
            src_ref=source,
            dst_ref=target,
            send_sem=send,
            recv_sem=recv,
            device_id=(row, other_plane(k) * width + lane),
            device_id_type=MESH,
        )

    def first_copy(number):
        return column_copy(
            firsts.at[number],
            unpacked.at[pl.ds(first_base + number * direct_units, direct_units)],
            first_send_sem.at[number],
            first_recv_sem.at[number],
            CLASSES[number],
        )

    def rest_copy(number):
        return column_copy(
            mixed[number].at[pl.ds(0, rest_units)],
            mixed[1 - number].at[pl.ds(spare_units, rest_units)],
            rest_send_sem.at[number],
            rest_recv_sem.at[1 - number],
            1,
        )

    def merged_copy(number):
        return column_copy(
            merged.at[number],
            unpacked.at[pl.ds(merged_base, merge_units)],
            merged_send_sem.at[number],
            merged_recv_sem.at[0],
            CLASSES[number],
        )

    def near_copy():
        return column_copy(
            near,
            unpacked.at[pl.ds(near_base, near_units)],
            near_send_sem.at[0],
            near_recv_sem.at[0],
            1,
        )

    def terms_copy(step, target, slot):
        where, _, _, _ = neighbour_at(step)
        return pltpu.make_async_remote_copy(
            src_ref=terms.at[target],
            dst_ref=terms_in.at[slot],
            send_sem=terms_send_sem.at[step],
            recv_sem=terms_recv_sem.at[step],
            device_id=where,
            device_id_type=MESH,
        )

    def final_copy(k, to_plane, from_plane):
        return column_copy(
            plane_terms.at[to_plane],
            final_terms.at[from_plane],
            final_send_sem.at[k],
            final_recv_sem.at[k],
            k,
        )

    node_rows = lax.broadcasted_iota(jnp.int32, (block, edges_ref.shape[2]), 0)
    node_index = lax.broadcasted_iota(jnp.int32, (block, hidden), 0)

    def compute(picks, store):
        blends = []
        for pick in picks:
            graph = table_ref[pick]
            features = features_ref[graph]
            edges = edges_ref[graph]
            sources = (node_rows == edges[0:1, :]).astype(jnp.float32).astype(jnp.bfloat16)
            ends = (node_rows == edges[1:2, :]).astype(jnp.float32).astype(jnp.bfloat16)
            adjacency = lax.dot_general(
                ends,
                sources,
                (((1,), (1,)), ((), ())),
                preferred_element_type=jnp.float32,
            ).astype(jnp.bfloat16)
            neighbour = jnp.dot(adjacency, features, preferred_element_type=jnp.float32)
            blends.append(
                (weight_ref[0] * features.astype(jnp.float32) + neighbour).astype(jnp.bfloat16)
            )
        blended = jnp.concatenate(blends, axis=0)
        hidden_one = jnp.maximum(
            jnp.dot(blended, w_first_ref[...], preferred_element_type=jnp.float32)
            + b_first_ref[...],
            0.0,
        ).astype(jnp.bfloat16)
        hidden_two = jnp.maximum(
            jnp.dot(hidden_one, w_second_ref[...], preferred_element_type=jnp.float32)
            + b_second_ref[...],
            0.0,
        ).astype(jnp.bfloat16)
        result = (
            jnp.dot(hidden_two, w_third_ref[...], preferred_element_type=jnp.float32)
            + b_third_ref[...]
        )
        for n, pick in enumerate(picks):
            count = counts_ref[table_ref[pick]]
            rows = jnp.where(node_index < count, result[n * block : (n + 1) * block], 0.0)
            rows = rows.astype(jnp.bfloat16)
            store(n, rows.reshape(parts, UNIT, hidden))
            total = jnp.sum(rows.astype(jnp.float32), axis=0, keepdims=True)
            pooled[pick] = total / jnp.full((1, hidden), count).astype(jnp.float32)

    group = 4
    turns = in_plane // group
    early_stages = min(4, len(stages))

    def start_stage(stage):
        def start(step, carry):
            graph_copy(stage, step, own_place).start()
            return carry

        lax.fori_loop(1, in_plane, start, 0)

    def finish_stage(stage):
        def finish(step, carry):
            _, _, _, source = neighbour_at(step)
            graph_copy(stage, step, own_place).wait_send()
            graph_copy(stage, step, source).wait_recv()
            return carry

        lax.fori_loop(1, in_plane, finish, 0)
        own = landing(stage, own_place)
        for n in range(parts):
            own[n] = sent[stage * in_plane, n]

    def finish_stages(number, turn_range):
        for turn in turn_range:
            finish_stage(stages.index((number, turn)))

    def gather_units(source, table_base, count, store):
        def gather(step, carry):
            for n in range(4):
                unit = step * 4 + n
                store(unit, source[table_ref[table_base + unit]])
            return carry

        lax.fori_loop(0, count // 4, gather, 0)

    def send_first(number):
        finish_stages(number, range(1))

        def store_first(unit, value):
            firsts[number, unit] = value

        gather_units(early[number], list_at + number * LANES, direct_units, store_first)
        first_copy(number).start()

        def keep(step, carry):
            for n in range(4):
                arrived[number][step * 4 + n] = early[number][step * 4 + n]
            return carry

        if bucket > 1:
            lax.fori_loop(0, in_plane * parts // 4, keep, 0)

    def send_rest(number):
        finish_stages(number, range(1, bucket))

        def store_rest(unit, value):
            mixed[number][unit] = value

        base = list_at + number * LANES + direct_units
        gather_units(arrived[number], base, max(merge_units, rest_units), store_rest)

        @pl.when(jnp.logical_not(inner))
        def _():
            rest_copy(number).start()

    def send_merged():
        @pl.when(inner)
        def _():
            for number in (1, 0):
                rest_copy(1 - number).wait_recv()

                def store(unit, value, number=number):
                    merged[number, unit] = value

                gather_units(mixed[number], merge_at + number * LANES, merge_units, store)
                merged_copy(number).start()

    def send_near():
        finish_stages(2, range(1, bucket))

        def store(unit, value):
            near[unit] = value

        base = list_at + 2 * LANES + direct_units
        gather_units(arrived[2], base, near_units, store)
        near_copy().start()

    def chosen(stage, values):
        result = values[0]
        for n, value in enumerate(values[1:]):
            result = jnp.where(stage > n, value, result)
        return result

    def compute_class(turn, carry):
        @pl.when(turn == first_turn)
        def _():
            send_first(0)

        stage = turn // turns
        half = chosen(stage, [CLASSES[number] // 2 for number, _ in stages])
        parity = chosen(stage, [CLASSES[number] % 2 for number, _ in stages])
        offset = chosen(stage, [turn_of * devices for _, turn_of in stages])
        to_plane = (plane // 2 + half) % 2 * 2 + (plane % 2 + parity) % 2
        steps = [turn % turns * group + n for n in range(group)]
        picks = []
        for step in steps:
            _, to_row, to_lane, _ = neighbour_at(step)
            picks.append(offset + to_row * cols_n + to_plane * width + to_lane)

        def store(n, rows):
            sent[stage * in_plane + steps[n]] = rows

        compute(picks, store)
        for early_stage in range(early_stages):

            @pl.when(stage == early_stage)
            def _():
                for n in range(1, group):
                    graph_copy(early_stage, steps[n], own_place).start()

            @pl.when(jnp.logical_and(stage == early_stage, steps[0] > 0))
            def _():
                graph_copy(early_stage, steps[0], own_place).start()

        return carry

    pl.semaphore_wait(barrier, in_plane - 1 + PLANES - 1)
    for load in loads:
        load.wait()
    first_turn = min(5, len(stages) - 1) * turns
    lax.fori_loop(0, len(stages) * turns, compute_class, 0)

    keys = lax.broadcasted_iota(jnp.int32, (devices * read_rows, slots), 0)
    members = (keys == ids_ref[0:1, :slots]).astype(jnp.float32)
    all_terms = jnp.dot(
        members,
        pooled[...].reshape(slots, hidden),
        precision=lax.Precision.HIGHEST,
        preferred_element_type=jnp.float32,
    )
    for place in range(in_plane):
        for to_plane in range(PLANES):
            device = place // width * cols_n + to_plane * width + place % width
            terms[place, to_plane] = all_terms[device * read_rows : (device + 1) * read_rows]

    def send_terms(step, carry):
        _, to_row, to_lane, _ = neighbour_at(step)
        terms_copy(step, to_row * width + to_lane, own_place).start()
        return carry

    lax.fori_loop(1, in_plane, send_terms, 0)
    terms_in[own_place] = terms[own_place]

    for stage in range(early_stages, len(stages)):
        start_stage(stage)
    send_first(1)
    send_rest(0)
    send_rest(1)
    send_merged()
    send_first(2)
    send_near()
    finish_stages(3, range(bucket))

    def finish_terms(step, carry):
        _, to_row, to_lane, source = neighbour_at(step)
        terms_copy(step, to_row * width + to_lane, own_place).wait_send()
        terms_copy(step, to_row * width + to_lane, source).wait_recv()
        return carry

    lax.fori_loop(1, in_plane, finish_terms, 0)
    plane_terms[...] = jnp.sum(terms_in[...], axis=0)
    final_terms[plane] = plane_terms[plane]
    for k in range(1, PLANES):
        final_copy(k, other_plane(k), plane).start()

    for number in range(3):
        first_copy(number).wait_send()
        first_copy(number).wait_recv()
    near_copy().wait_send()
    near_copy().wait_recv()

    @pl.when(inner)
    def _():
        for number in range(2):
            merged_copy(number).wait_send()

    @pl.when(jnp.logical_not(inner))
    def _():
        for number in range(2):
            rest_copy(number).wait_send()

    merged_copy(0).wait_recv()

    def out_copy(slot):
        return pltpu.make_async_copy(
            sent.at[slot],
            out_ref.at[slot],
            out_sem.at[slot],
        )

    def place_graph(slot, carry):
        for part in range(parts):
            value = unpacked[table_ref[final_at + slot * parts + part]]
            sent[slot, part] = value
        out_copy(slot).start()
        return carry

    lax.fori_loop(0, out_ref.shape[0], place_graph, 0)
    for k in range(1, PLANES):
        final_copy(k, other_plane(k), plane).wait_send()
        final_copy(k, other_plane(k), other_plane(k)).wait_recv()
    readout_ref[...] = jnp.sum(final_terms[...], axis=0)

    def finish_out(slot, carry):
        out_copy(slot).wait()
        return carry

    lax.fori_loop(0, out_ref.shape[0], finish_out, 0)


def body(
    sizes,
    node_features,
    node_counts,
    edge_list,
    readout_ids,
    live_graphs,
    self_weight,
    w_first,
    b_first,
    w_second,
    b_second,
    w_third,
    b_third,
):
    rows_n, cols_n = sizes
    devices = rows_n * cols_n
    width = cols_n // PLANES
    in_plane = rows_n * width
    capacity, block, hidden = node_features.shape
    parts = block // UNIT
    graphs_out = capacity // 2
    read_rows = 8
    bucket = (capacity + devices - 1) // devices
    slots_n = devices * bucket
    mean_units = graphs_out * parts // PLANES
    direct_units = mean_units // 2
    spare_units = mean_units
    span = direct_units + spare_units
    tiers = [tuple(mean_units * part // 64 for part in tier) for tier in TIERS]
    places = in_plane * bucket
    zero_base = places * parts + 3 * direct_units + 2 * spare_units
    every = gather_counts(node_counts, live_graphs, sizes)
    table, extra, tier = pl.pallas_call(
        functools.partial(
            plan_kernel,
            sizes,
            capacity,
            bucket,
            parts,
            graphs_out,
            (direct_units, spare_units),
            tiers,
        ),
        out_shape=(
            jax.ShapeDtypeStruct((6 + graphs_out * parts // LANES, LANES), jnp.int32),
            jax.ShapeDtypeStruct((8, LANES), jnp.int32),
            jax.ShapeDtypeStruct((1,), jnp.int32),
        ),
        in_specs=[VMEM, VMEM],
        out_specs=(VMEM, VMEM, SMEM),
        name="plan",
    )(every, readout_ids.reshape(1, -1))
    table = table.reshape(-1)

    out_shape = (
        jax.ShapeDtypeStruct((graphs_out, block, hidden), jnp.bfloat16),
        jax.ShapeDtypeStruct((read_rows, hidden), jnp.float32),
    )
    pooled_scratch = pltpu.VMEM((slots_n, 1, hidden), jnp.float32)

    def semaphores(count):
        return [pltpu.SemaphoreType.DMA((count,)), pltpu.SemaphoreType.DMA((count,))]

    def relayed(tier, caps, *operands):
        table, extra, node_counts, self_weight, node_features, edge_list = operands[:6]
        merge_units, rest_units, near_units = caps

        def graphs(*count):
            return pltpu.VMEM((*count, UNIT, hidden), jnp.bfloat16)

        whole_terms = pltpu.VMEM((in_plane, PLANES, read_rows, hidden), jnp.float32)
        some_terms = pltpu.VMEM((PLANES, read_rows, hidden), jnp.float32)
        node_out, readout = pl.pallas_call(
            functools.partial(relay_kernel, sizes, bucket, direct_units, spare_units, caps),
            out_shape=(
                jax.ShapeDtypeStruct((graphs_out, parts, UNIT, hidden), jnp.bfloat16),
                out_shape[1],
            ),
            in_specs=[SMEM] * 3 + [HBM] + [VMEM] * 8,
            out_specs=(HBM, VMEM),
            scratch_shapes=[graphs(slots_n, parts)]
            + [graphs(in_plane * parts)] * 3
            + [graphs(places * parts if bucket > 1 else 1)] * 3
            + [graphs(2 * spare_units)] * 2
            + [
                graphs(3, direct_units),
                graphs(2, merge_units),
                graphs(near_units),
                graphs(zero_base + 1),
            ]
            + [pooled_scratch, whole_terms, whole_terms, some_terms, some_terms]
            + semaphores(slots_n)
            + semaphores(3)
            + semaphores(2)
            + semaphores(2)
            + semaphores(1)
            + semaphores(in_plane)
            + semaphores(PLANES)
            + [
                pltpu.SemaphoreType.DMA((graphs_out,)),
                pltpu.VMEM((capacity, block, hidden), jnp.bfloat16),
                pltpu.SemaphoreType.DMA((4,)),
            ],
            compiler_params=pltpu.CompilerParams(
                collective_id=2 + tier, has_side_effects=True, vmem_limit_bytes=61 * 1024 * 1024
            ),
            name="gin_relay",
        )(table, node_counts, self_weight, node_features, edge_list, extra, *operands[6:])
        return node_out.reshape(graphs_out, block, hidden), readout

    def direct(*operands):
        table, extra, node_counts, self_weight, node_features, edge_list = operands[:6]
        all_terms = pltpu.VMEM((devices, read_rows, hidden), jnp.float32)
        graphs = pltpu.VMEM((devices, bucket, block, hidden), jnp.bfloat16)
        return pl.pallas_call(
            functools.partial(layer_kernel, sizes, bucket),
            out_shape=out_shape,
            in_specs=[SMEM] * 4 + [VMEM] * 9,
            out_specs=(VMEM, VMEM),
            scratch_shapes=[graphs, graphs]
            + [pooled_scratch, all_terms, all_terms]
            + semaphores(devices)
            + semaphores(devices),
            compiler_params=pltpu.CompilerParams(
                collective_id=1, has_side_effects=True, vmem_limit_bytes=60 * 1024 * 1024
            ),
            name="gin_direct",
        )(
            table,
            node_counts,
            extra[1],
            self_weight,
            node_features,
            edge_list,
            extra,
            *operands[6:],
        )

    branches = [functools.partial(relayed, number, cap) for number, cap in enumerate(tiers)]
    return lax.switch(
        tier[0],
        branches + [direct],
        table,
        extra,
        node_counts,
        self_weight,
        node_features,
        edge_list,
        w_first,
        b_first.reshape(1, -1),
        w_second,
        b_second.reshape(1, -1),
        w_third,
        b_third.reshape(1, -1),
    )


def solution(mesh):
    sizes = (mesh.shape["row"], mesh.shape["col"])
    both = ("row", "col")
    in_specs = (
        P(both, None, None),
        P(both),
        P(both, None, None),
        P(both),
        P(both),
        P(),
        P(),
        P(),
        P(),
        P(),
        P(),
        P(),
    )
    out_specs = (P(both, None, None), P(both, None))
    return jax.shard_map(
        functools.partial(body, sizes),
        mesh=mesh,
        in_specs=in_specs,
        out_specs=out_specs,
        check_vma=False,
    )
```

```python
import functools

import jax
import jax.numpy as jnp
from jax import lax
from jax.experimental import pallas as pl
from jax.experimental.pallas import tpu as pltpu
from jax.sharding import PartitionSpec as P

MESH = pl.DeviceIdType.MESH
VMEM = pl.BlockSpec(memory_space=pltpu.VMEM)
SMEM = pl.BlockSpec(memory_space=pltpu.SMEM)
HBM = pl.BlockSpec(memory_space=pltpu.HBM)
PLANES = 4
UNIT = 16
LANES = 128
CLASSES = (2, 3, 1, 0)
TIERS = ((36, 36, 40), (40, 36, 40), (44, 36, 40), (52, 40, 44), (60, 48, 56))


def partners(step, sizes):
    rows, cols = sizes
    row, col = lax.axis_index("row"), lax.axis_index("col")
    by_row, by_col = step // cols, (step % cols) * 3 % cols
    to_row, to_col = (row + by_row) % rows, (col + by_col) % cols
    from_row, from_col = (row + rows - by_row) % rows, (col + cols - by_col) % cols
    return (to_row, to_col), to_row * cols + to_col, from_row * cols + from_col


def greet(sizes):
    barrier = pltpu.get_barrier_semaphore()
    devices = sizes[0] * sizes[1]

    def signal(step, carry):
        where, _, _ = partners(step, sizes)
        pl.semaphore_signal(barrier, inc=1, device_id=where, device_id_type=MESH)
        return carry

    lax.fori_loop(1, devices, signal, 0)
    return barrier


def gather_kernel(sizes, counts_ref, live_ref, all_ref, own, send_sem, recv_sem):
    devices = sizes[0] * sizes[1]
    capacity = counts_ref.shape[1]
    me = lax.axis_index("row") * sizes[1] + lax.axis_index("col")
    barrier = greet(sizes)
    own[:, :capacity] = counts_ref[...]
    own[:, capacity:] = jnp.full((1, own.shape[1] - capacity), live_ref[0])
    all_ref[me] = own[...]
    pl.semaphore_wait(barrier, devices - 1)

    def copy(step, slot):
        where, _, _ = partners(step, sizes)
        return pltpu.make_async_remote_copy(
            src_ref=own,
            dst_ref=all_ref.at[slot],
            send_sem=send_sem.at[step],
            recv_sem=recv_sem.at[step],
            device_id=where,
            device_id_type=MESH,
        )

    def send(step, carry):
        copy(step, me).start()
        return carry

    def finish(step, carry):
        _, _, source = partners(step, sizes)
        copy(step, me).wait_send()
        copy(step, source).wait_recv()
        return carry

    lax.fori_loop(1, devices, send, 0)
    lax.fori_loop(1, devices, finish, 0)


def gather_counts(node_counts, live_graphs, sizes):
    devices = sizes[0] * sizes[1]
    return pl.pallas_call(
        functools.partial(gather_kernel, sizes),
        out_shape=jax.ShapeDtypeStruct((devices, 1, LANES), jnp.int32),
        in_specs=[VMEM, SMEM],
        out_specs=VMEM,
        scratch_shapes=[
            pltpu.VMEM((1, LANES), jnp.int32),
            pltpu.SemaphoreType.DMA((devices,)),
            pltpu.SemaphoreType.DMA((devices,)),
        ],
        compiler_params=pltpu.CompilerParams(collective_id=0, has_side_effects=True),
        name="gather_counts",
    )(node_counts.reshape(1, -1), live_graphs)


def plan_kernel(
    sizes, capacity, bucket, parts, graphs_out, units, tiers, every_ref, ids_ref,
    table_ref, extra_ref, tier_ref,
):
    direct_units, spare_units = units
    rows_n, cols_n = sizes
    devices = rows_n * cols_n
    bits = devices.bit_length() - 1
    width = cols_n // PLANES
    in_plane = rows_n * width
    places = in_plane * bucket
    row, col = lax.axis_index("row"), lax.axis_index("col")
    plane, lane = col // width, col % width
    me = row * cols_n + col
    shape = (devices, LANES)
    lanes = lax.broadcasted_iota(jnp.int32, shape, 1)
    owner = lax.broadcasted_iota(jnp.int32, (devices, 1), 0)
    owner_col = owner & (cols_n - 1)
    owner_plane = owner_col >> (width.bit_length() - 1)
    owner_place = (owner >> (cols_n.bit_length() - 1)) * width + (owner & (width - 1))

    def total(values, axis):
        return jnp.sum(values.astype(jnp.float32), axis=axis, keepdims=True).astype(jnp.int32)

    def column(values, index):
        return total(jnp.where(lanes == index, values, 0), 1)

    def product(left, right):
        left, right = left.astype(jnp.float32), right.astype(jnp.float32)
        exact = jnp.dot(
            left.astype(jnp.bfloat16),
            right.astype(jnp.bfloat16),
            preferred_element_type=jnp.float32,
        )
        return exact.astype(jnp.int32)

    every = every_ref[:, 0, :]
    live = column(every, capacity)
    first = lax.broadcasted_iota(jnp.int32, (devices, devices), 0)
    second = lax.broadcasted_iota(jnp.int32, (devices, devices), 1)
    offset = column(product((second < first).astype(jnp.int32), every), capacity)
    sizes_all = jnp.where(lanes < live, (every + (UNIT - 1)) >> (UNIT.bit_length() - 1), 0)

    def turned(values, by, turn):
        values = jnp.where((lanes[: values.shape[0]] >> bits) == turn, values, 0)
        shift = devices
        while shift < LANES:
            values = values + pltpu.roll(values, shift, 1)
            shift *= 2
        for bit in range(bits):
            rolled = pltpu.roll(values, 1 << bit, 1)
            values = jnp.where(((by >> bit) & 1) == 1, rolled, values)
        return values

    by_turn = [turned(sizes_all, offset, turn) for turn in range(bucket)]
    size_sum = sum(by_turn)
    early = by_turn[0]
    same_plane = ((first & (cols_n - 1)) >> (width.bit_length() - 1)) == (
        (second & (cols_n - 1)) >> (width.bit_length() - 1)
    )
    starts, begun = [], jnp.zeros(shape, jnp.int32)
    for turn in range(bucket):
        earlier = (same_plane & (second < first)).astype(jnp.int32)
        starts.append(begun + product(earlier, by_turn[turn]))
        begun = begun + product(same_plane.astype(jnp.int32), by_turn[turn])
        if turn == 0:
            firsts = jnp.minimum(begun, direct_units)

    plane_row = lax.broadcasted_iota(jnp.int32, (8, devices), 0)
    plane_of = lax.broadcasted_iota(jnp.int32, (8, devices), 1)
    plane_of = (plane_of & (cols_n - 1)) >> (width.bit_length() - 1)
    of_plane = (plane_row == plane_of).astype(jnp.int32)
    plane_load = product(of_plane, size_sum)
    plane_load = plane_load - jnp.minimum(product(of_plane, early), direct_units)
    planes = lax.broadcasted_iota(jnp.int32, (8, LANES), 0)
    to_planes = lax.broadcasted_iota(jnp.int32, (8, LANES), 1) & (cols_n - 1)
    to_planes = to_planes >> (width.bit_length() - 1)
    far = ((planes >> 1) != (to_planes >> 1)) & (planes < PLANES)
    plane_rest = jnp.where(far, plane_load, 0)
    is_inner = ((planes & 1) + (planes >> 1)) == 1
    merged_load = total(plane_rest, 0)
    rest_load = jnp.where(is_inner, 0, plane_rest)
    near_load = jnp.where(((planes ^ to_planes) == 1), plane_load, 0)
    most_merged = jnp.max(merged_load.astype(jnp.float32))
    most_rest = jnp.max(rest_load.astype(jnp.float32))
    most_near = jnp.max(near_load.astype(jnp.float32))
    tier = jnp.int32(0)
    for merge, rest, near in tiers:
        over = (most_merged > merge) | (most_rest > rest) | (most_near > near)
        tier = tier + jnp.where(over, 1, 0)
    tier_ref[0] = tier

    line = lax.broadcasted_iota(jnp.int32, (1, LANES), 1)
    own_offset = total(jnp.where(owner == me, offset, 0), 0)
    own_live = total(jnp.where(owner == me, live, 0), 0)
    within = ((line - own_offset) & (devices - 1)) + (line >> bits) * devices
    table_ref[0:1, :] = jnp.minimum(within, capacity - 1)

    ids = jnp.where(line < capacity, jnp.concatenate([ids_ref[...]] * (LANES // capacity), 1), 0)
    slot_ids = jnp.zeros((1, LANES), jnp.int32)
    for turn in range(bucket):
        slot_ids = jnp.where((line >> bits) == turn, turned(ids, own_offset, turn), slot_ids)
    extra_ref[0:1, :] = jnp.where(within < own_live, slot_ids, -1)

    for number, k in enumerate(CLASSES[:3]):
        to_plane = (plane // 2 + k // 2) % 2 * 2 + (plane % 2 + k % 2) % 2
        target = row * cols_n + to_plane * width + lane
        listed = jnp.zeros(shape, jnp.int32)
        used = jnp.zeros((devices, 1), jnp.int32)
        sent_first = jnp.where(owner_plane == plane, column(firsts, target), 0)
        sent_first = jnp.max(sent_first.astype(jnp.float32), axis=0, keepdims=True)
        sent_first = sent_first.astype(jnp.int32)
        unit = jnp.where(line < direct_units, line, sent_first + line - direct_units)
        for turn in range(bucket):
            size = column(by_turn[turn], target)
            size = jnp.where(owner_plane == plane, size, 0)
            at = unit - column(starts[turn], target)
            base = (turn * in_plane + owner_place) * parts
            listed = listed + jnp.where((at >= 0) & (at < size), base + at, 0)
            used = used + size
        listed = total(listed, 0)
        listed = jnp.where(
            line < direct_units, jnp.minimum(listed, in_plane * parts - 1), listed
        )
        table_ref[1 + number : 2 + number, :] = listed
        if number < 2:
            own_rest = total(used, 0) - sent_first
            merged = jnp.where(line < own_rest, line, spare_units + line - own_rest)
            merged = jnp.minimum(jnp.maximum(merged, 0), 2 * spare_units - 1)
            table_ref[4 + number : 5 + number, :] = merged

    inner_plane = 2 - plane // 2
    own_sizes = [column(by_turn[turn], me) for turn in range(bucket)]
    own_firsts = column(firsts, me)
    from_inner = owner_plane == inner_plane
    inner_first = jnp.where(from_inner, own_firsts, 0).astype(jnp.float32)
    inner_first = jnp.max(inner_first, axis=0, keepdims=True).astype(jnp.int32)
    inner_rest = total(jnp.where(from_inner, sum(own_sizes), 0), 0) - inner_first
    first_base = places * parts
    merged_base = first_base + 3 * direct_units
    near_base = merged_base + spare_units
    zero_base = near_base + spare_units
    from_own, from_near = owner_plane == plane, (owner_plane ^ 1) == plane
    same_side = (owner_plane & 1) == plane % 2
    low = jnp.where(from_near, 2 * direct_units, jnp.where(same_side, 0, direct_units))
    low = first_base + low
    high = jnp.where(from_near, near_base, merged_base + jnp.where(from_inner, 0, inner_rest))
    high = high - own_firsts
    finals = [jnp.zeros(shape, jnp.int32) for _ in range(graphs_out * parts // LANES)]
    arrival = jnp.zeros(shape, jnp.int32)
    part = lanes & (parts - 1)
    graph = lanes >> (parts.bit_length() - 1)
    for turn in range(bucket):
        within = ((me - offset) & (devices - 1)) + turn * devices
        place = jnp.where(within < live, (offset + within) >> bits, -1)
        at = column(starts[turn], me) + part
        address = jnp.where(at < own_firsts, low + at, high + at)
        held = (turn * in_plane + owner_place) * parts + part
        address = jnp.where(from_own, held, address)
        address = jnp.where(part < own_sizes[turn], address - zero_base, 0)
        for half in range(len(finals)):
            mine = graph + half * (LANES // parts) == place
            finals[half] = finals[half] + jnp.where(mine, address, 0)
        arrival = arrival + jnp.where(lanes == place, owner * bucket + turn, 0)
    for half, values in enumerate(finals):
        address = jnp.clip(total(values, 0) + zero_base, 0, zero_base)
        table_ref[6 + half : 7 + half, :] = address
    extra_ref[1:2, :] = total(arrival, 0)


def layer_kernel(
    sizes,
    bucket,
    picked_ref,
    counts_ref,
    arrival_ref,
    weight_ref,
    features_ref,
    edges_ref,
    ids_ref,
    w_first_ref,
    b_first_ref,
    w_second_ref,
    b_second_ref,
    w_third_ref,
    b_third_ref,
    out_ref,
    readout_ref,
    sent,
    arrived,
    pooled,
    terms,
    terms_in,
    send_sem,
    recv_sem,
    terms_send_sem,
    terms_recv_sem,
):
    devices = sizes[0] * sizes[1]
    read_rows = readout_ref.shape[0]
    block, hidden = features_ref.shape[1:]
    me = lax.axis_index("row") * sizes[1] + lax.axis_index("col")
    barrier = greet(sizes)

    def graph_copy(step, target, slot):
        where, _, _ = partners(step, sizes)
        return pltpu.make_async_remote_copy(
            src_ref=sent.at[target],
            dst_ref=arrived.at[slot],
            send_sem=send_sem.at[step],
            recv_sem=recv_sem.at[step],
            device_id=where,
            device_id_type=MESH,
        )

    def terms_copy(step, target, slot):
        where, _, _ = partners(step, sizes)
        return pltpu.make_async_remote_copy(
            src_ref=terms.at[target],
            dst_ref=terms_in.at[slot],
            send_sem=terms_send_sem.at[step],
            recv_sem=terms_recv_sem.at[step],
            device_id=where,
            device_id_type=MESH,
        )

    node_rows = lax.broadcasted_iota(jnp.int32, (block, edges_ref.shape[2]), 0)
    node_index = lax.broadcasted_iota(jnp.int32, (block, hidden), 0)

    def compute(target, store):
        blends = []
        for j in range(bucket):
            graph = picked_ref[j * devices + target]
            features = features_ref[graph]
            edges = edges_ref[graph]
            sources = (node_rows == edges[0:1, :]).astype(jnp.float32).astype(jnp.bfloat16)
            targets = (node_rows == edges[1:2, :]).astype(jnp.float32).astype(jnp.bfloat16)
            adjacency = lax.dot_general(
                targets,
                sources,
                (((1,), (1,)), ((), ())),
                preferred_element_type=jnp.float32,
            ).astype(jnp.bfloat16)
            neighbour = jnp.dot(adjacency, features, preferred_element_type=jnp.float32)
            blends.append(
                (weight_ref[0] * features.astype(jnp.float32) + neighbour).astype(jnp.bfloat16)
            )
        blended = jnp.concatenate(blends, axis=0) if bucket > 1 else blends[0]
        hidden_one = jnp.maximum(
            jnp.dot(blended, w_first_ref[...], preferred_element_type=jnp.float32)
            + b_first_ref[...],
            0.0,
        ).astype(jnp.bfloat16)
        hidden_two = jnp.maximum(
            jnp.dot(hidden_one, w_second_ref[...], preferred_element_type=jnp.float32)
            + b_second_ref[...],
            0.0,
        ).astype(jnp.bfloat16)
        result = (
            jnp.dot(hidden_two, w_third_ref[...], preferred_element_type=jnp.float32)
            + b_third_ref[...]
        )
        for j in range(bucket):
            count = counts_ref[picked_ref[j * devices + target]]
            rows = jnp.where(node_index < count, result[j * block : (j + 1) * block], 0.0)
            rows = rows.astype(jnp.bfloat16)
            store(j, rows)
            total = jnp.sum(rows.astype(jnp.float32), axis=0, keepdims=True)
            pooled[j * devices + target] = total / jnp.full((1, hidden), count).astype(jnp.float32)

    pl.semaphore_wait(barrier, devices - 1)

    def compute_and_send(step, carry):
        _, target, _ = partners(step, sizes)

        def store(j, rows):
            sent[target, j] = rows

        compute(target, store)

        @pl.when(step > 0)
        def _():
            graph_copy(step, target, me).start()

        return carry

    lax.fori_loop(0, devices, compute_and_send, 0)
    for j in range(bucket):
        arrived[me, j] = sent[me, j]

    slots = devices * bucket
    keys = lax.broadcasted_iota(jnp.int32, (devices * read_rows, slots), 0)
    members = (keys == ids_ref[0:1, :slots]).astype(jnp.float32)
    all_terms = jnp.dot(
        members,
        pooled[...].reshape(slots, hidden),
        precision=lax.Precision.HIGHEST,
        preferred_element_type=jnp.float32,
    )
    terms[...] = all_terms.reshape(devices, read_rows, hidden)

    def send_terms(step, carry):
        _, target, _ = partners(step, sizes)
        terms_copy(step, target, me).start()
        return carry

    lax.fori_loop(1, devices, send_terms, 0)
    terms_in[me] = terms[me]

    def finish(step, carry):
        _, target, source = partners(step, sizes)
        graph_copy(step, target, me).wait_send()
        graph_copy(step, target, source).wait_recv()
        terms_copy(step, target, me).wait_send()
        terms_copy(step, target, source).wait_recv()
        return carry

    lax.fori_loop(1, devices, finish, 0)
    readout_ref[...] = jnp.sum(terms_in[...], axis=0)

    def place(slot, carry):
        which = arrival_ref[slot]
        out_ref[slot] = arrived[which // bucket, which % bucket]
        return carry

    lax.fori_loop(0, out_ref.shape[0], place, 0)


def relay_kernel(
    sizes,
    bucket,
    direct_units,
    spare_units,
    caps,
    table_ref,
    counts_ref,
    weight_ref,
    features_hbm_ref,
    edges_ref,
    ids_ref,
    w_first_ref,
    b_first_ref,
    w_second_ref,
    b_second_ref,
    w_third_ref,
    b_third_ref,
    out_ref,
    readout_ref,
    sent,
    early_a,
    early_b,
    early_c,
    arrived_a,
    arrived_b,
    arrived_c,
    mixed_a,
    mixed_b,
    firsts,
    merged,
    near,
    unpacked,
    pooled,
    whole_terms,
    terms,
    terms_in,
    plane_terms,
    final_terms,
    send_sem,
    recv_sem,
    first_send_sem,
    first_recv_sem,
    rest_send_sem,
    rest_recv_sem,
    merged_send_sem,
    merged_recv_sem,
    near_send_sem,
    near_recv_sem,
    terms_send_sem,
    terms_recv_sem,
    final_send_sem,
    final_recv_sem,
    out_sem,
    features_ref,
    load_sem,
):
    merge_units, rest_units, near_units = caps
    rows_n, cols_n = sizes
    devices = rows_n * cols_n
    width = cols_n // PLANES
    in_plane = rows_n * width
    read_rows = readout_ref.shape[0]
    block, hidden = features_ref.shape[1:]
    parts = block // UNIT
    slots = devices * bucket
    places = in_plane * bucket
    list_at, merge_at, final_at = LANES, 4 * LANES, 6 * LANES
    first_base = places * parts
    merged_base = first_base + 3 * direct_units
    near_base = merged_base + spare_units
    zero_base = near_base + spare_units
    early = (early_a, early_b, early_c)
    arrived = (arrived_a, arrived_b, arrived_c) if bucket > 1 else early
    mixed = (mixed_a, mixed_b)
    row, col = lax.axis_index("row"), lax.axis_index("col")
    plane, lane = col // width, col % width
    own_place = row * width + lane
    inner = plane % 2 + plane // 2 == 1

    def other_plane(k):
        return (plane // 2 + k // 2) % 2 * 2 + (plane % 2 + k % 2) % 2

    def neighbour_at(step):
        to_row, to_lane = (row + step // width) % rows_n, (lane + step % width) % width
        from_row = (row + rows_n - step // width) % rows_n
        from_lane = (lane + width - step % width) % width
        return (to_row, plane * width + to_lane), to_row, to_lane, from_row * width + from_lane

    barrier = pltpu.get_barrier_semaphore()

    def signal(step, carry):
        where, _, _, _ = neighbour_at(step)
        pl.semaphore_signal(barrier, inc=1, device_id=where, device_id_type=MESH)
        return carry

    lax.fori_loop(1, in_plane, signal, 0)
    for k in range(1, PLANES):
        where = (row, other_plane(k) * width + lane)
        pl.semaphore_signal(barrier, inc=1, device_id=where, device_id_type=MESH)
    quarter = features_ref.shape[0] // 4
    loads = [
        pltpu.make_async_copy(
            features_hbm_ref.at[pl.ds(n * quarter, quarter)],
            features_ref.at[pl.ds(n * quarter, quarter)],
            load_sem.at[n],
        )
        for n in range(4)
    ]
    for load in loads:
        load.start()
    unpacked[zero_base] = jnp.zeros((UNIT, hidden), jnp.bfloat16)

    stages = [(0, 0), (1, 0)]
    for late in ((0, 1), (2,), (3,)):
        for turn in range(bucket):
            stages += [(number, turn) for number in late if (number, turn) not in stages]

    def landing(stage, place):
        number, turn = stages[stage]
        if number < 3 and turn == 0:
            return early[number].at[pl.ds(place * parts, parts)]
        into = arrived[number] if number < 3 else unpacked
        return into.at[pl.ds((turn * in_plane + place) * parts, parts)]

    def graph_copy(stage, step, place):
        where, _, _, _ = neighbour_at(step)
        return pltpu.make_async_remote_copy(
            src_ref=sent.at[stage * in_plane + step],
            dst_ref=landing(stage, place),
            send_sem=send_sem.at[stage * in_plane + step],
            recv_sem=recv_sem.at[stage * in_plane + step],
            device_id=where,
            device_id_type=MESH,
        )

    def column_copy(source, target, send, recv, k):
        return pltpu.make_async_remote_copy(
            src_ref=source,
            dst_ref=target,
            send_sem=send,
            recv_sem=recv,
            device_id=(row, other_plane(k) * width + lane),
            device_id_type=MESH,
        )

    def first_copy(number):
        return column_copy(
            firsts.at[number],
            unpacked.at[pl.ds(first_base + number * direct_units, direct_units)],
            first_send_sem.at[number],
            first_recv_sem.at[number],
            CLASSES[number],
        )

    def rest_copy(number):
        return column_copy(
            mixed[number].at[pl.ds(0, rest_units)],
            mixed[1 - number].at[pl.ds(spare_units, rest_units)],
            rest_send_sem.at[number],
            rest_recv_sem.at[1 - number],
            1,
        )

    def merged_copy(number):
        return column_copy(
            merged.at[number],
            unpacked.at[pl.ds(merged_base, merge_units)],
            merged_send_sem.at[number],
            merged_recv_sem.at[0],
            CLASSES[number],
        )

    def near_copy():
        return column_copy(
            near,
            unpacked.at[pl.ds(near_base, near_units)],
            near_send_sem.at[0],
            near_recv_sem.at[0],
            1,
        )

    def terms_copy(step, target, slot):
        where, _, _, _ = neighbour_at(step)
        return pltpu.make_async_remote_copy(
            src_ref=terms.at[target],
            dst_ref=terms_in.at[slot],
            send_sem=terms_send_sem.at[step],
            recv_sem=terms_recv_sem.at[step],
            device_id=where,
            device_id_type=MESH,
        )

    def final_copy(k, to_plane, from_plane):
        return column_copy(
            plane_terms.at[to_plane],
            final_terms.at[from_plane],
            final_send_sem.at[k],
            final_recv_sem.at[k],
            k,
        )

    node_rows = lax.broadcasted_iota(jnp.int32, (block, edges_ref.shape[2]), 0)
    node_index = lax.broadcasted_iota(jnp.int32, (block, hidden), 0)

    def compute(picks, store):
        blends = []
        for pick in picks:
            graph = table_ref[pick]
            features = features_ref[graph]
            edges = edges_ref[graph]
            sources = (node_rows == edges[0:1, :]).astype(jnp.float32).astype(jnp.bfloat16)
            ends = (node_rows == edges[1:2, :]).astype(jnp.float32).astype(jnp.bfloat16)
            adjacency = lax.dot_general(
                ends,
                sources,
                (((1,), (1,)), ((), ())),
                preferred_element_type=jnp.float32,
            ).astype(jnp.bfloat16)
            neighbour = jnp.dot(adjacency, features, preferred_element_type=jnp.float32)
            blends.append(
                (weight_ref[0] * features.astype(jnp.float32) + neighbour).astype(jnp.bfloat16)
            )
        blended = jnp.concatenate(blends, axis=0)
        hidden_one = jnp.maximum(
            jnp.dot(blended, w_first_ref[...], preferred_element_type=jnp.float32)
            + b_first_ref[...],
            0.0,
        ).astype(jnp.bfloat16)
        hidden_two = jnp.maximum(
            jnp.dot(hidden_one, w_second_ref[...], preferred_element_type=jnp.float32)
            + b_second_ref[...],
            0.0,
        ).astype(jnp.bfloat16)
        result = (
            jnp.dot(hidden_two, w_third_ref[...], preferred_element_type=jnp.float32)
            + b_third_ref[...]
        )
        for n, pick in enumerate(picks):
            count = counts_ref[table_ref[pick]]
            rows = jnp.where(node_index < count, result[n * block : (n + 1) * block], 0.0)
            rows = rows.astype(jnp.bfloat16)
            store(n, rows.reshape(parts, UNIT, hidden))
            total = jnp.sum(rows.astype(jnp.float32), axis=0, keepdims=True)
            pooled[pick] = total / jnp.full((1, hidden), count).astype(jnp.float32)

    group = 4
    turns = in_plane // group
    early_stages = min(4, len(stages))

    def start_stage(stage):
        def start(step, carry):
            graph_copy(stage, step, own_place).start()
            return carry

        lax.fori_loop(1, in_plane, start, 0)

    def finish_stage(stage):
        def finish(step, carry):
            _, _, _, source = neighbour_at(step)
            graph_copy(stage, step, own_place).wait_send()
            graph_copy(stage, step, source).wait_recv()
            return carry

        lax.fori_loop(1, in_plane, finish, 0)
        own = landing(stage, own_place)
        for n in range(parts):
            own[n] = sent[stage * in_plane, n]

    def finish_stages(number, turn_range):
        for turn in turn_range:
            finish_stage(stages.index((number, turn)))

    def gather_units(source, table_base, count, store):
        def gather(step, carry):
            for n in range(4):
                unit = step * 4 + n
                store(unit, source[table_ref[table_base + unit]])
            return carry

        lax.fori_loop(0, count // 4, gather, 0)

    def send_first(number):
        finish_stages(number, range(1))

        def store_first(unit, value):
            firsts[number, unit] = value

        gather_units(early[number], list_at + number * LANES, direct_units, store_first)
        first_copy(number).start()

        def keep(step, carry):
            for n in range(4):
                arrived[number][step * 4 + n] = early[number][step * 4 + n]
            return carry

        if bucket > 1:
            lax.fori_loop(0, in_plane * parts // 4, keep, 0)

    def send_rest(number):
        finish_stages(number, range(1, bucket))

        def store_rest(unit, value):
            mixed[number][unit] = value

        base = list_at + number * LANES + direct_units
        gather_units(arrived[number], base, max(merge_units, rest_units), store_rest)

        @pl.when(jnp.logical_not(inner))
        def _():
            rest_copy(number).start()

    def send_merged():
        @pl.when(inner)
        def _():
            for number in (1, 0):
                rest_copy(1 - number).wait_recv()

                def store(unit, value, number=number):
                    merged[number, unit] = value

                gather_units(mixed[number], merge_at + number * LANES, merge_units, store)
                merged_copy(number).start()

    def send_near():
        finish_stages(2, range(1, bucket))

        def store(unit, value):
            near[unit] = value

        base = list_at + 2 * LANES + direct_units
        gather_units(arrived[2], base, near_units, store)
        near_copy().start()

    def chosen(stage, values):
        result = values[0]
        for n, value in enumerate(values[1:]):
            result = jnp.where(stage > n, value, result)
        return result

    def compute_class(turn, carry):
        @pl.when(turn == first_turn)
        def _():
            send_first(0)

        @pl.when(turn == second_turn)
        def _():
            send_first(1)

        stage = turn // turns
        half = chosen(stage, [CLASSES[number] // 2 for number, _ in stages])
        parity = chosen(stage, [CLASSES[number] % 2 for number, _ in stages])
        offset = chosen(stage, [turn_of * devices for _, turn_of in stages])
        to_plane = (plane // 2 + half) % 2 * 2 + (plane % 2 + parity) % 2
        steps = [turn % turns * group + n for n in range(group)]
        picks = []
        for step in steps:
            _, to_row, to_lane, _ = neighbour_at(step)
            picks.append(offset + to_row * cols_n + to_plane * width + to_lane)

        def store(n, rows):
            sent[stage * in_plane + steps[n]] = rows

        compute(picks, store)
        for early_stage in range(early_stages):

            @pl.when(stage == early_stage)
            def _():
                for n in range(1, group):
                    graph_copy(early_stage, steps[n], own_place).start()

            @pl.when(jnp.logical_and(stage == early_stage, steps[0] > 0))
            def _():
                graph_copy(early_stage, steps[0], own_place).start()

        return carry

    pl.semaphore_wait(barrier, in_plane - 1 + PLANES - 1)
    for load in loads:
        load.wait()
    first_turn = min(3, len(stages) - 2) * turns
    second_turn = min(6, len(stages) - 1) * turns
    lax.fori_loop(0, len(stages) * turns, compute_class, 0)

    keys = lax.broadcasted_iota(jnp.int32, (devices * read_rows, slots), 0)
    members = (keys == ids_ref[0:1, :slots]).astype(jnp.float32)
    all_terms = jnp.dot(
        members,
        pooled[...].reshape(slots, hidden),
        precision=lax.Precision.HIGHEST,
        preferred_element_type=jnp.float32,
    )
    for place in range(in_plane):
        for to_plane in range(PLANES):
            device = place // width * cols_n + to_plane * width + place % width
            part = all_terms[device * read_rows : (device + 1) * read_rows]
            whole_terms[place, pl.ds(to_plane * read_rows, read_rows)] = part
    terms[...] = whole_terms[...].astype(jnp.bfloat16)

    def send_terms(step, carry):
        _, to_row, to_lane, _ = neighbour_at(step)
        terms_copy(step, to_row * width + to_lane, own_place).start()
        return carry

    lax.fori_loop(1, in_plane, send_terms, 0)
    terms_in[own_place] = jnp.zeros_like(terms[own_place])

    for stage in range(early_stages, len(stages)):
        start_stage(stage)
    send_rest(0)
    send_rest(1)
    send_merged()
    send_first(2)
    send_near()
    def finish_terms(step, carry):
        _, to_row, to_lane, source = neighbour_at(step)
        terms_copy(step, to_row * width + to_lane, own_place).wait_send()
        terms_copy(step, to_row * width + to_lane, source).wait_recv()
        return carry

    lax.fori_loop(1, in_plane, finish_terms, 0)
    summed = jnp.sum(terms_in[...].astype(jnp.float32), axis=0) + whole_terms[own_place]
    for to_plane in range(PLANES):
        plane_terms[to_plane] = summed[to_plane * read_rows : (to_plane + 1) * read_rows]
    final_terms[plane] = plane_terms[plane]
    for k in range(1, PLANES):
        final_copy(k, other_plane(k), plane).start()

    finish_stages(3, range(bucket))

    for number in range(3):
        first_copy(number).wait_send()
        first_copy(number).wait_recv()
    near_copy().wait_send()
    near_copy().wait_recv()

    @pl.when(inner)
    def _():
        for number in range(2):
            merged_copy(number).wait_send()

    @pl.when(jnp.logical_not(inner))
    def _():
        for number in range(2):
            rest_copy(number).wait_send()

    merged_copy(0).wait_recv()

    def out_copy(slot):
        return pltpu.make_async_copy(
            sent.at[slot],
            out_ref.at[slot],
            out_sem.at[slot],
        )

    def place_graph(slot, carry):
        for part in range(parts):
            value = unpacked[table_ref[final_at + slot * parts + part]]
            sent[slot, part] = value
        out_copy(slot).start()
        return carry

    lax.fori_loop(0, out_ref.shape[0], place_graph, 0)
    for k in range(1, PLANES):
        final_copy(k, other_plane(k), plane).wait_send()
        final_copy(k, other_plane(k), other_plane(k)).wait_recv()
    readout_ref[...] = jnp.sum(final_terms[...], axis=0)

    def finish_out(slot, carry):
        out_copy(slot).wait()
        return carry

    lax.fori_loop(0, out_ref.shape[0], finish_out, 0)


def finish_kernel(from_ref, to_ref, held, sem, out_sem):
    size = from_ref.shape[0] // 8
    parts = [pl.ds(n * size, size) for n in range(8)]
    loads = [
        pltpu.make_async_copy(from_ref.at[part], held.at[part], sem.at[n])
        for n, part in enumerate(parts)
    ]
    stores = [
        pltpu.make_async_copy(held.at[part], to_ref.at[part], out_sem.at[n])
        for n, part in enumerate(parts)
    ]
    for load in loads:
        load.start()
    for load, store in zip(loads, stores):
        load.wait()
        store.start()
    for store in stores:
        store.wait()


def body(
    sizes,
    node_features,
    node_counts,
    edge_list,
    readout_ids,
    live_graphs,
    self_weight,
    w_first,
    b_first,
    w_second,
    b_second,
    w_third,
    b_third,
):
    rows_n, cols_n = sizes
    devices = rows_n * cols_n
    width = cols_n // PLANES
    in_plane = rows_n * width
    capacity, block, hidden = node_features.shape
    parts = block // UNIT
    graphs_out = capacity // 2
    read_rows = 8
    bucket = (capacity + devices - 1) // devices
    slots_n = devices * bucket
    mean_units = graphs_out * parts // PLANES
    direct_units = mean_units // 2
    spare_units = mean_units
    span = direct_units + spare_units
    tiers = [tuple(mean_units * part // 64 for part in tier) for tier in TIERS]
    places = in_plane * bucket
    zero_base = places * parts + 3 * direct_units + 2 * spare_units
    every = gather_counts(node_counts, live_graphs, sizes)
    table, extra, tier = pl.pallas_call(
        functools.partial(
            plan_kernel,
            sizes,
            capacity,
            bucket,
            parts,
            graphs_out,
            (direct_units, spare_units),
            tiers,
        ),
        out_shape=(
            jax.ShapeDtypeStruct((6 + graphs_out * parts // LANES, LANES), jnp.int32),
            jax.ShapeDtypeStruct((8, LANES), jnp.int32),
            jax.ShapeDtypeStruct((1,), jnp.int32),
        ),
        in_specs=[VMEM, VMEM],
        out_specs=(VMEM, VMEM, SMEM),
        name="plan",
    )(every, readout_ids.reshape(1, -1))
    table = table.reshape(-1)

    out_shape = (
        jax.ShapeDtypeStruct((graphs_out, block, hidden), jnp.bfloat16),
        jax.ShapeDtypeStruct((read_rows, hidden), jnp.float32),
    )
    pooled_scratch = pltpu.VMEM((slots_n, 1, hidden), jnp.float32)

    def semaphores(count):
        return [pltpu.SemaphoreType.DMA((count,)), pltpu.SemaphoreType.DMA((count,))]

    def relayed(tier, caps, *operands):
        table, extra, node_counts, self_weight, node_features, edge_list = operands[:6]
        merge_units, rest_units, near_units = caps

        def graphs(*count):
            return pltpu.VMEM((*count, UNIT, hidden), jnp.bfloat16)

        whole_terms = pltpu.VMEM((in_plane, PLANES * read_rows, hidden), jnp.float32)
        half_terms = pltpu.VMEM((in_plane, PLANES * read_rows, hidden), jnp.bfloat16)
        some_terms = pltpu.VMEM((PLANES, read_rows, hidden), jnp.float32)
        node_out, readout = pl.pallas_call(
            functools.partial(relay_kernel, sizes, bucket, direct_units, spare_units, caps),
            out_shape=(
                jax.ShapeDtypeStruct((graphs_out, parts, UNIT, hidden), jnp.bfloat16),
                out_shape[1],
            ),
            in_specs=[SMEM] * 3 + [HBM] + [VMEM] * 8,
            out_specs=(HBM, VMEM),
            scratch_shapes=[graphs(slots_n, parts)]
            + [graphs(in_plane * parts)] * 3
            + [graphs(places * parts if bucket > 1 else 1)] * 3
            + [graphs(2 * spare_units)] * 2
            + [
                graphs(3, direct_units),
                graphs(2, merge_units),
                graphs(near_units),
                graphs(zero_base + 1),
            ]
            + [pooled_scratch, whole_terms, half_terms, half_terms, some_terms, some_terms]
            + semaphores(slots_n)
            + semaphores(3)
            + semaphores(2)
            + semaphores(2)
            + semaphores(1)
            + semaphores(in_plane)
            + semaphores(PLANES)
            + [
                pltpu.SemaphoreType.DMA((graphs_out,)),
                pltpu.VMEM((capacity, block, hidden), jnp.bfloat16),
                pltpu.SemaphoreType.DMA((4,)),
            ],
            compiler_params=pltpu.CompilerParams(
                collective_id=2 + tier, has_side_effects=True, vmem_limit_bytes=61 * 1024 * 1024
            ),
            name="gin_relay",
        )(table, node_counts, self_weight, node_features, edge_list, extra, *operands[6:])
        return node_out.reshape(graphs_out, block, hidden), readout

    def direct(*operands):
        table, extra, node_counts, self_weight, node_features, edge_list = operands[:6]
        all_terms = pltpu.VMEM((devices, read_rows, hidden), jnp.float32)
        graphs = pltpu.VMEM((devices, bucket, block, hidden), jnp.bfloat16)
        return pl.pallas_call(
            functools.partial(layer_kernel, sizes, bucket),
            out_shape=out_shape,
            in_specs=[SMEM] * 4 + [VMEM] * 9,
            out_specs=(VMEM, VMEM),
            scratch_shapes=[graphs, graphs]
            + [pooled_scratch, all_terms, all_terms]
            + semaphores(devices)
            + semaphores(devices),
            compiler_params=pltpu.CompilerParams(
                collective_id=1, has_side_effects=True, vmem_limit_bytes=60 * 1024 * 1024
            ),
            name="gin_direct",
        )(
            table,
            node_counts,
            extra[1],
            self_weight,
            node_features,
            edge_list,
            extra,
            *operands[6:],
        )

    branches = [functools.partial(relayed, number, cap) for number, cap in enumerate(tiers)]
    node_out, readout = lax.switch(
        tier[0],
        branches + [direct],
        table,
        extra,
        node_counts,
        self_weight,
        node_features,
        edge_list,
        w_first,
        b_first.reshape(1, -1),
        w_second,
        b_second.reshape(1, -1),
        w_third,
        b_third.reshape(1, -1),
    )
    node_out = pl.pallas_call(
        finish_kernel,
        out_shape=jax.ShapeDtypeStruct(node_out.shape, node_out.dtype),
        in_specs=[HBM],
        out_specs=HBM,
        scratch_shapes=[
            pltpu.VMEM(node_out.shape, node_out.dtype),
            pltpu.SemaphoreType.DMA((8,)),
            pltpu.SemaphoreType.DMA((8,)),
        ],
        name="finish",
    )(node_out)
    return node_out, readout


def solution(mesh):
    sizes = (mesh.shape["row"], mesh.shape["col"])
    both = ("row", "col")
    in_specs = (
        P(both, None, None),
        P(both),
        P(both, None, None),
        P(both),
        P(both),
        P(),
        P(),
        P(),
        P(),
        P(),
        P(),
        P(),
    )
    out_specs = (P(both, None, None), P(both, None))
    return jax.shard_map(
        functools.partial(body, sizes),
        mesh=mesh,
        in_specs=in_specs,
        out_specs=out_specs,
        check_vma=False,
    )
```

```python
import functools

import jax
import jax.numpy as jnp
from jax import lax
from jax.experimental import pallas as pl
from jax.experimental.pallas import tpu as pltpu
from jax.sharding import PartitionSpec as P

MESH = pl.DeviceIdType.MESH
VMEM = pl.BlockSpec(memory_space=pltpu.VMEM)
SMEM = pl.BlockSpec(memory_space=pltpu.SMEM)
HBM = pl.BlockSpec(memory_space=pltpu.HBM)
PLANES = 4
UNIT = 16
LANES = 128
CLASSES = (2, 3, 1, 0)
TIERS = ((36, 36, 40), (40, 36, 40), (44, 36, 40), (52, 40, 44), (60, 48, 56), (68, 48, 56))


def partners(step, sizes):
    rows, cols = sizes
    row, col = lax.axis_index("row"), lax.axis_index("col")
    by_row, by_col = step // cols, (step % cols) * 3 % cols
    to_row, to_col = (row + by_row) % rows, (col + by_col) % cols
    from_row, from_col = (row + rows - by_row) % rows, (col + cols - by_col) % cols
    return (to_row, to_col), to_row * cols + to_col, from_row * cols + from_col


def greet(sizes):
    barrier = pltpu.get_barrier_semaphore()
    devices = sizes[0] * sizes[1]

    def signal(step, carry):
        where, _, _ = partners(step, sizes)
        pl.semaphore_signal(barrier, inc=1, device_id=where, device_id_type=MESH)
        return carry

    lax.fori_loop(1, devices, signal, 0)
    return barrier


def gather_kernel(sizes, counts_ref, live_ref, all_ref, own, send_sem, recv_sem):
    devices = sizes[0] * sizes[1]
    capacity = counts_ref.shape[1]
    me = lax.axis_index("row") * sizes[1] + lax.axis_index("col")
    barrier = greet(sizes)
    own[:, :capacity] = counts_ref[...]
    own[:, capacity:] = jnp.full((1, own.shape[1] - capacity), live_ref[0])
    all_ref[me] = own[...]
    pl.semaphore_wait(barrier, devices - 1)

    def copy(step, slot):
        where, _, _ = partners(step, sizes)
        return pltpu.make_async_remote_copy(
            src_ref=own,
            dst_ref=all_ref.at[slot],
            send_sem=send_sem.at[step],
            recv_sem=recv_sem.at[step],
            device_id=where,
            device_id_type=MESH,
        )

    def send(step, carry):
        copy(step, me).start()
        return carry

    def finish(step, carry):
        _, _, source = partners(step, sizes)
        copy(step, me).wait_send()
        copy(step, source).wait_recv()
        return carry

    lax.fori_loop(1, devices, send, 0)
    lax.fori_loop(1, devices, finish, 0)


def gather_counts(node_counts, live_graphs, sizes):
    devices = sizes[0] * sizes[1]
    return pl.pallas_call(
        functools.partial(gather_kernel, sizes),
        out_shape=jax.ShapeDtypeStruct((devices, 1, LANES), jnp.int32),
        in_specs=[VMEM, SMEM],
        out_specs=VMEM,
        scratch_shapes=[
            pltpu.VMEM((1, LANES), jnp.int32),
            pltpu.SemaphoreType.DMA((devices,)),
            pltpu.SemaphoreType.DMA((devices,)),
        ],
        compiler_params=pltpu.CompilerParams(collective_id=0, has_side_effects=True),
        name="gather_counts",
    )(node_counts.reshape(1, -1), live_graphs)


def plan_kernel(
    sizes, capacity, bucket, parts, graphs_out, units, tiers, every_ref, ids_ref,
    table_ref, extra_ref, tier_ref,
):
    direct_units, spare_units = units
    rows_n, cols_n = sizes
    devices = rows_n * cols_n
    bits = devices.bit_length() - 1
    width = cols_n // PLANES
    in_plane = rows_n * width
    places = in_plane * bucket
    row, col = lax.axis_index("row"), lax.axis_index("col")
    plane, lane = col // width, col % width
    me = row * cols_n + col
    shape = (devices, LANES)
    lanes = lax.broadcasted_iota(jnp.int32, shape, 1)
    owner = lax.broadcasted_iota(jnp.int32, (devices, 1), 0)
    owner_col = owner & (cols_n - 1)
    owner_plane = owner_col >> (width.bit_length() - 1)
    owner_place = (owner >> (cols_n.bit_length() - 1)) * width + (owner & (width - 1))

    def total(values, axis):
        return jnp.sum(values.astype(jnp.float32), axis=axis, keepdims=True).astype(jnp.int32)

    def column(values, index):
        return total(jnp.where(lanes == index, values, 0), 1)

    def product(left, right):
        left, right = left.astype(jnp.float32), right.astype(jnp.float32)
        exact = jnp.dot(
            left.astype(jnp.bfloat16),
            right.astype(jnp.bfloat16),
            preferred_element_type=jnp.float32,
        )
        return exact.astype(jnp.int32)

    every = every_ref[:, 0, :]
    live = column(every, capacity)
    first = lax.broadcasted_iota(jnp.int32, (devices, devices), 0)
    second = lax.broadcasted_iota(jnp.int32, (devices, devices), 1)
    offset = column(product((second < first).astype(jnp.int32), every), capacity)
    sizes_all = jnp.where(lanes < live, (every + (UNIT - 1)) >> (UNIT.bit_length() - 1), 0)

    def turned(values, by, turn):
        values = jnp.where((lanes[: values.shape[0]] >> bits) == turn, values, 0)
        shift = devices
        while shift < LANES:
            values = values + pltpu.roll(values, shift, 1)
            shift *= 2
        for bit in range(bits):
            rolled = pltpu.roll(values, 1 << bit, 1)
            values = jnp.where(((by >> bit) & 1) == 1, rolled, values)
        return values

    by_turn = [turned(sizes_all, offset, turn) for turn in range(bucket)]
    size_sum = sum(by_turn)
    early = by_turn[0]
    same_plane = ((first & (cols_n - 1)) >> (width.bit_length() - 1)) == (
        (second & (cols_n - 1)) >> (width.bit_length() - 1)
    )
    starts, begun = [], jnp.zeros(shape, jnp.int32)
    for turn in range(bucket):
        earlier = (same_plane & (second < first)).astype(jnp.int32)
        starts.append(begun + product(earlier, by_turn[turn]))
        begun = begun + product(same_plane.astype(jnp.int32), by_turn[turn])
        if turn == 0:
            firsts = jnp.minimum(begun, direct_units)

    plane_row = lax.broadcasted_iota(jnp.int32, (8, devices), 0)
    plane_of = lax.broadcasted_iota(jnp.int32, (8, devices), 1)
    plane_of = (plane_of & (cols_n - 1)) >> (width.bit_length() - 1)
    of_plane = (plane_row == plane_of).astype(jnp.int32)
    plane_load = product(of_plane, size_sum)
    plane_load = plane_load - jnp.minimum(product(of_plane, early), direct_units)
    planes = lax.broadcasted_iota(jnp.int32, (8, LANES), 0)
    to_planes = lax.broadcasted_iota(jnp.int32, (8, LANES), 1) & (cols_n - 1)
    to_planes = to_planes >> (width.bit_length() - 1)
    far = ((planes >> 1) != (to_planes >> 1)) & (planes < PLANES)
    plane_rest = jnp.where(far, plane_load, 0)
    is_inner = ((planes & 1) + (planes >> 1)) == 1
    merged_load = total(plane_rest, 0)
    rest_load = jnp.where(is_inner, 0, plane_rest)
    near_load = jnp.where(((planes ^ to_planes) == 1), plane_load, 0)
    most_merged = jnp.max(merged_load.astype(jnp.float32))
    most_rest = jnp.max(rest_load.astype(jnp.float32))
    most_near = jnp.max(near_load.astype(jnp.float32))
    tier = jnp.int32(0)
    for merge, rest, near in tiers:
        over = (most_merged > merge) | (most_rest > rest) | (most_near > near)
        tier = tier + jnp.where(over, 1, 0)
    tier_ref[0] = tier

    line = lax.broadcasted_iota(jnp.int32, (1, LANES), 1)
    own_offset = total(jnp.where(owner == me, offset, 0), 0)
    own_live = total(jnp.where(owner == me, live, 0), 0)
    within = ((line - own_offset) & (devices - 1)) + (line >> bits) * devices
    table_ref[0:1, :] = jnp.minimum(within, capacity - 1)

    ids = jnp.where(line < capacity, jnp.concatenate([ids_ref[...]] * (LANES // capacity), 1), 0)
    slot_ids = jnp.zeros((1, LANES), jnp.int32)
    for turn in range(bucket):
        slot_ids = jnp.where((line >> bits) == turn, turned(ids, own_offset, turn), slot_ids)
    extra_ref[0:1, :] = jnp.where(within < own_live, slot_ids, -1)

    for number, k in enumerate(CLASSES[:3]):
        to_plane = (plane // 2 + k // 2) % 2 * 2 + (plane % 2 + k % 2) % 2
        target = row * cols_n + to_plane * width + lane
        listed = jnp.zeros(shape, jnp.int32)
        used = jnp.zeros((devices, 1), jnp.int32)
        sent_first = jnp.where(owner_plane == plane, column(firsts, target), 0)
        sent_first = jnp.max(sent_first.astype(jnp.float32), axis=0, keepdims=True)
        sent_first = sent_first.astype(jnp.int32)
        unit = jnp.where(line < direct_units, line, sent_first + line - direct_units)
        for turn in range(bucket):
            size = column(by_turn[turn], target)
            size = jnp.where(owner_plane == plane, size, 0)
            at = unit - column(starts[turn], target)
            base = (turn * in_plane + owner_place) * parts
            listed = listed + jnp.where((at >= 0) & (at < size), base + at, 0)
            used = used + size
        listed = total(listed, 0)
        listed = jnp.where(
            line < direct_units, jnp.minimum(listed, in_plane * parts - 1), listed
        )
        table_ref[1 + number : 2 + number, :] = listed
        if number < 2:
            own_rest = total(used, 0) - sent_first
            merged = jnp.where(line < own_rest, line, spare_units + line - own_rest)
            merged = jnp.minimum(jnp.maximum(merged, 0), 2 * spare_units - 1)
            table_ref[4 + number : 5 + number, :] = merged

    inner_plane = 2 - plane // 2
    own_sizes = [column(by_turn[turn], me) for turn in range(bucket)]
    own_firsts = column(firsts, me)
    from_inner = owner_plane == inner_plane
    inner_first = jnp.where(from_inner, own_firsts, 0).astype(jnp.float32)
    inner_first = jnp.max(inner_first, axis=0, keepdims=True).astype(jnp.int32)
    inner_rest = total(jnp.where(from_inner, sum(own_sizes), 0), 0) - inner_first
    first_base = places * parts
    merged_base = first_base + 3 * direct_units
    near_base = merged_base + spare_units
    zero_base = near_base + spare_units
    from_own, from_near = owner_plane == plane, (owner_plane ^ 1) == plane
    same_side = (owner_plane & 1) == plane % 2
    low = jnp.where(from_near, 2 * direct_units, jnp.where(same_side, 0, direct_units))
    low = first_base + low
    high = jnp.where(from_near, near_base, merged_base + jnp.where(from_inner, 0, inner_rest))
    high = high - own_firsts
    finals = [jnp.zeros(shape, jnp.int32) for _ in range(graphs_out * parts // LANES)]
    arrival = jnp.zeros(shape, jnp.int32)
    part = lanes & (parts - 1)
    graph = lanes >> (parts.bit_length() - 1)
    for turn in range(bucket):
        within = ((me - offset) & (devices - 1)) + turn * devices
        place = jnp.where(within < live, (offset + within) >> bits, -1)
        at = column(starts[turn], me) + part
        address = jnp.where(at < own_firsts, low + at, high + at)
        held = (turn * in_plane + owner_place) * parts + part
        address = jnp.where(from_own, held, address)
        address = jnp.where(part < own_sizes[turn], address - zero_base, 0)
        for half in range(len(finals)):
            mine = graph + half * (LANES // parts) == place
            finals[half] = finals[half] + jnp.where(mine, address, 0)
        arrival = arrival + jnp.where(lanes == place, owner * bucket + turn, 0)
    for half, values in enumerate(finals):
        address = jnp.clip(total(values, 0) + zero_base, 0, zero_base)
        table_ref[6 + half : 7 + half, :] = address
    extra_ref[1:2, :] = total(arrival, 0)


def layer_kernel(
    sizes,
    bucket,
    picked_ref,
    counts_ref,
    arrival_ref,
    weight_ref,
    features_ref,
    edges_ref,
    ids_ref,
    w_first_ref,
    b_first_ref,
    w_second_ref,
    b_second_ref,
    w_third_ref,
    b_third_ref,
    out_ref,
    readout_ref,
    sent,
    arrived,
    pooled,
    terms,
    terms_in,
    send_sem,
    recv_sem,
    terms_send_sem,
    terms_recv_sem,
):
    devices = sizes[0] * sizes[1]
    read_rows = readout_ref.shape[0]
    block, hidden = features_ref.shape[1:]
    me = lax.axis_index("row") * sizes[1] + lax.axis_index("col")
    barrier = greet(sizes)

    def graph_copy(step, target, slot):
        where, _, _ = partners(step, sizes)
        return pltpu.make_async_remote_copy(
            src_ref=sent.at[target],
            dst_ref=arrived.at[slot],
            send_sem=send_sem.at[step],
            recv_sem=recv_sem.at[step],
            device_id=where,
            device_id_type=MESH,
        )

    def terms_copy(step, target, slot):
        where, _, _ = partners(step, sizes)
        return pltpu.make_async_remote_copy(
            src_ref=terms.at[target],
            dst_ref=terms_in.at[slot],
            send_sem=terms_send_sem.at[step],
            recv_sem=terms_recv_sem.at[step],
            device_id=where,
            device_id_type=MESH,
        )

    node_rows = lax.broadcasted_iota(jnp.int32, (block, edges_ref.shape[2]), 0)
    node_index = lax.broadcasted_iota(jnp.int32, (block, hidden), 0)

    def compute(target, store):
        blends = []
        for j in range(bucket):
            graph = picked_ref[j * devices + target]
            features = features_ref[graph]
            edges = edges_ref[graph]
            sources = (node_rows == edges[0:1, :]).astype(jnp.float32).astype(jnp.bfloat16)
            targets = (node_rows == edges[1:2, :]).astype(jnp.float32).astype(jnp.bfloat16)
            adjacency = lax.dot_general(
                targets,
                sources,
                (((1,), (1,)), ((), ())),
                preferred_element_type=jnp.float32,
            ).astype(jnp.bfloat16)
            neighbour = jnp.dot(adjacency, features, preferred_element_type=jnp.float32)
            blends.append(
                (weight_ref[0] * features.astype(jnp.float32) + neighbour).astype(jnp.bfloat16)
            )
        blended = jnp.concatenate(blends, axis=0) if bucket > 1 else blends[0]
        hidden_one = jnp.maximum(
            jnp.dot(blended, w_first_ref[...], preferred_element_type=jnp.float32)
            + b_first_ref[...],
            0.0,
        ).astype(jnp.bfloat16)
        hidden_two = jnp.maximum(
            jnp.dot(hidden_one, w_second_ref[...], preferred_element_type=jnp.float32)
            + b_second_ref[...],
            0.0,
        ).astype(jnp.bfloat16)
        result = (
            jnp.dot(hidden_two, w_third_ref[...], preferred_element_type=jnp.float32)
            + b_third_ref[...]
        )
        for j in range(bucket):
            count = counts_ref[picked_ref[j * devices + target]]
            rows = jnp.where(node_index < count, result[j * block : (j + 1) * block], 0.0)
            rows = rows.astype(jnp.bfloat16)
            store(j, rows)
            total = jnp.sum(rows.astype(jnp.float32), axis=0, keepdims=True)
            pooled[j * devices + target] = total / jnp.full((1, hidden), count).astype(jnp.float32)

    pl.semaphore_wait(barrier, devices - 1)

    def compute_and_send(step, carry):
        _, target, _ = partners(step, sizes)

        def store(j, rows):
            sent[target, j] = rows

        compute(target, store)

        @pl.when(step > 0)
        def _():
            graph_copy(step, target, me).start()

        return carry

    lax.fori_loop(0, devices, compute_and_send, 0)
    for j in range(bucket):
        arrived[me, j] = sent[me, j]

    slots = devices * bucket
    keys = lax.broadcasted_iota(jnp.int32, (devices * read_rows, slots), 0)
    members = (keys == ids_ref[0:1, :slots]).astype(jnp.float32)
    all_terms = jnp.dot(
        members,
        pooled[...].reshape(slots, hidden),
        precision=lax.Precision.HIGHEST,
        preferred_element_type=jnp.float32,
    )
    terms[...] = all_terms.reshape(devices, read_rows, hidden)

    def send_terms(step, carry):
        _, target, _ = partners(step, sizes)
        terms_copy(step, target, me).start()
        return carry

    lax.fori_loop(1, devices, send_terms, 0)
    terms_in[me] = terms[me]

    def finish(step, carry):
        _, target, source = partners(step, sizes)
        graph_copy(step, target, me).wait_send()
        graph_copy(step, target, source).wait_recv()
        terms_copy(step, target, me).wait_send()
        terms_copy(step, target, source).wait_recv()
        return carry

    lax.fori_loop(1, devices, finish, 0)
    readout_ref[...] = jnp.sum(terms_in[...], axis=0)

    def place(slot, carry):
        which = arrival_ref[slot]
        out_ref[slot] = arrived[which // bucket, which % bucket]
        return carry

    lax.fori_loop(0, out_ref.shape[0], place, 0)


def relay_kernel(
    sizes,
    bucket,
    direct_units,
    spare_units,
    caps,
    table_ref,
    counts_ref,
    weight_ref,
    features_hbm_ref,
    edges_ref,
    ids_ref,
    w_first_ref,
    b_first_ref,
    w_second_ref,
    b_second_ref,
    w_third_ref,
    b_third_ref,
    out_ref,
    readout_ref,
    sent,
    early_a,
    early_b,
    early_c,
    arrived_a,
    arrived_b,
    arrived_c,
    mixed_a,
    mixed_b,
    firsts,
    merged,
    near,
    unpacked,
    pooled,
    whole_terms,
    terms,
    terms_in,
    plane_terms,
    final_terms,
    send_sem,
    recv_sem,
    first_send_sem,
    first_recv_sem,
    rest_send_sem,
    rest_recv_sem,
    merged_send_sem,
    merged_recv_sem,
    near_send_sem,
    near_recv_sem,
    terms_send_sem,
    terms_recv_sem,
    final_send_sem,
    final_recv_sem,
    out_sem,
    features_ref,
    load_sem,
):
    merge_units, rest_units, near_units = caps
    rows_n, cols_n = sizes
    devices = rows_n * cols_n
    width = cols_n // PLANES
    in_plane = rows_n * width
    read_rows = readout_ref.shape[0]
    block, hidden = features_ref.shape[1:]
    parts = block // UNIT
    slots = devices * bucket
    places = in_plane * bucket
    list_at, merge_at, final_at = LANES, 4 * LANES, 6 * LANES
    first_base = places * parts
    merged_base = first_base + 3 * direct_units
    near_base = merged_base + spare_units
    zero_base = near_base + spare_units
    early = (early_a, early_b, early_c)
    arrived = (arrived_a, arrived_b, arrived_c) if bucket > 1 else early
    mixed = (mixed_a, mixed_b)
    row, col = lax.axis_index("row"), lax.axis_index("col")
    plane, lane = col // width, col % width
    own_place = row * width + lane
    inner = plane % 2 + plane // 2 == 1

    def other_plane(k):
        return (plane // 2 + k // 2) % 2 * 2 + (plane % 2 + k % 2) % 2

    def neighbour_at(step):
        to_row, to_lane = (row + step // width) % rows_n, (lane + step % width) % width
        from_row = (row + rows_n - step // width) % rows_n
        from_lane = (lane + width - step % width) % width
        return (to_row, plane * width + to_lane), to_row, to_lane, from_row * width + from_lane

    barrier = pltpu.get_barrier_semaphore()

    def signal(step, carry):
        where, _, _, _ = neighbour_at(step)
        pl.semaphore_signal(barrier, inc=1, device_id=where, device_id_type=MESH)
        return carry

    lax.fori_loop(1, in_plane, signal, 0)
    for k in range(1, PLANES):
        where = (row, other_plane(k) * width + lane)
        pl.semaphore_signal(barrier, inc=1, device_id=where, device_id_type=MESH)
    quarter = features_ref.shape[0] // 4
    loads = [
        pltpu.make_async_copy(
            features_hbm_ref.at[pl.ds(n * quarter, quarter)],
            features_ref.at[pl.ds(n * quarter, quarter)],
            load_sem.at[n],
        )
        for n in range(4)
    ]
    for load in loads:
        load.start()
    unpacked[zero_base] = jnp.zeros((UNIT, hidden), jnp.bfloat16)

    stages = [(0, 0), (1, 0)]
    for late in ((0, 1), (2,), (3,)):
        for turn in range(bucket):
            stages += [(number, turn) for number in late if (number, turn) not in stages]

    def landing(stage, place):
        number, turn = stages[stage]
        if number < 3 and turn == 0:
            return early[number].at[pl.ds(place * parts, parts)]
        into = arrived[number] if number < 3 else unpacked
        return into.at[pl.ds((turn * in_plane + place) * parts, parts)]

    def graph_copy(stage, step, place):
        where, _, _, _ = neighbour_at(step)
        return pltpu.make_async_remote_copy(
            src_ref=sent.at[stage * in_plane + step],
            dst_ref=landing(stage, place),
            send_sem=send_sem.at[stage * in_plane + step],
            recv_sem=recv_sem.at[stage * in_plane + step],
            device_id=where,
            device_id_type=MESH,
        )

    def column_copy(source, target, send, recv, k):
        return pltpu.make_async_remote_copy(
            src_ref=source,
            dst_ref=target,
            send_sem=send,
            recv_sem=recv,
            device_id=(row, other_plane(k) * width + lane),
            device_id_type=MESH,
        )

    def first_copy(number):
        return column_copy(
            firsts.at[number],
            unpacked.at[pl.ds(first_base + number * direct_units, direct_units)],
            first_send_sem.at[number],
            first_recv_sem.at[number],
            CLASSES[number],
        )

    def rest_copy(number):
        return column_copy(
            mixed[number].at[pl.ds(0, rest_units)],
            mixed[1 - number].at[pl.ds(spare_units, rest_units)],
            rest_send_sem.at[number],
            rest_recv_sem.at[1 - number],
            1,
        )

    def merged_copy(number):
        return column_copy(
            merged.at[number],
            unpacked.at[pl.ds(merged_base, merge_units)],
            merged_send_sem.at[number],
            merged_recv_sem.at[0],
            CLASSES[number],
        )

    def near_copy():
        return column_copy(
            near,
            unpacked.at[pl.ds(near_base, near_units)],
            near_send_sem.at[0],
            near_recv_sem.at[0],
            1,
        )

    def terms_copy(step, target, slot):
        where, _, _, _ = neighbour_at(step)
        return pltpu.make_async_remote_copy(
            src_ref=terms.at[target],
            dst_ref=terms_in.at[slot],
            send_sem=terms_send_sem.at[step],
            recv_sem=terms_recv_sem.at[step],
            device_id=where,
            device_id_type=MESH,
        )

    def final_copy(k, to_plane, from_plane):
        return column_copy(
            plane_terms.at[to_plane],
            final_terms.at[from_plane],
            final_send_sem.at[k],
            final_recv_sem.at[k],
            k,
        )

    node_rows = lax.broadcasted_iota(jnp.int32, (block, edges_ref.shape[2]), 0)
    node_index = lax.broadcasted_iota(jnp.int32, (block, hidden), 0)

    def compute(picks, store):
        blends = []
        for pick in picks:
            graph = table_ref[pick]
            features = features_ref[graph]
            edges = edges_ref[graph]
            sources = (node_rows == edges[0:1, :]).astype(jnp.float32).astype(jnp.bfloat16)
            ends = (node_rows == edges[1:2, :]).astype(jnp.float32).astype(jnp.bfloat16)
            adjacency = lax.dot_general(
                ends,
                sources,
                (((1,), (1,)), ((), ())),
                preferred_element_type=jnp.float32,
            ).astype(jnp.bfloat16)
            neighbour = jnp.dot(adjacency, features, preferred_element_type=jnp.float32)
            blends.append(
                (weight_ref[0] * features.astype(jnp.float32) + neighbour).astype(jnp.bfloat16)
            )
        blended = jnp.concatenate(blends, axis=0)
        hidden_one = jnp.maximum(
            jnp.dot(blended, w_first_ref[...], preferred_element_type=jnp.float32)
            + b_first_ref[...],
            0.0,
        ).astype(jnp.bfloat16)
        hidden_two = jnp.maximum(
            jnp.dot(hidden_one, w_second_ref[...], preferred_element_type=jnp.float32)
            + b_second_ref[...],
            0.0,
        ).astype(jnp.bfloat16)
        result = (
            jnp.dot(hidden_two, w_third_ref[...], preferred_element_type=jnp.float32)
            + b_third_ref[...]
        )
        for n, pick in enumerate(picks):
            count = counts_ref[table_ref[pick]]
            rows = jnp.where(node_index < count, result[n * block : (n + 1) * block], 0.0)
            rows = rows.astype(jnp.bfloat16)
            store(n, rows.reshape(parts, UNIT, hidden))
            total = jnp.sum(rows.astype(jnp.float32), axis=0, keepdims=True)
            pooled[pick] = total / jnp.full((1, hidden), count).astype(jnp.float32)

    group = 4
    turns = in_plane // group
    early_stages = min(4, len(stages))

    def start_stage(stage):
        def start(step, carry):
            graph_copy(stage, step, own_place).start()
            return carry

        lax.fori_loop(1, in_plane, start, 0)

    def finish_stage(stage):
        def finish(step, carry):
            _, _, _, source = neighbour_at(step)
            graph_copy(stage, step, own_place).wait_send()
            graph_copy(stage, step, source).wait_recv()
            return carry

        lax.fori_loop(1, in_plane, finish, 0)
        own = landing(stage, own_place)
        for n in range(parts):
            own[n] = sent[stage * in_plane, n]

    def finish_stages(number, turn_range):
        for turn in turn_range:
            finish_stage(stages.index((number, turn)))

    def gather_units(source, table_base, count, store):
        def gather(step, carry):
            for n in range(4):
                unit = step * 4 + n
                store(unit, source[table_ref[table_base + unit]])
            return carry

        lax.fori_loop(0, count // 4, gather, 0)

    def send_first(number):
        finish_stages(number, range(1))

        def store_first(unit, value):
            firsts[number, unit] = value

        gather_units(early[number], list_at + number * LANES, direct_units, store_first)
        first_copy(number).start()

        def keep(step, carry):
            for n in range(4):
                arrived[number][step * 4 + n] = early[number][step * 4 + n]
            return carry

        if bucket > 1:
            lax.fori_loop(0, in_plane * parts // 4, keep, 0)

    def send_rest(number):
        finish_stages(number, range(1, bucket))

        def store_rest(unit, value):
            mixed[number][unit] = value

        base = list_at + number * LANES + direct_units
        gather_units(arrived[number], base, max(merge_units, rest_units), store_rest)

        @pl.when(jnp.logical_not(inner))
        def _():
            rest_copy(number).start()

    def send_merged():
        @pl.when(inner)
        def _():
            for number in (1, 0):
                rest_copy(1 - number).wait_recv()

                def store(unit, value, number=number):
                    merged[number, unit] = value

                gather_units(mixed[number], merge_at + number * LANES, merge_units, store)
                merged_copy(number).start()

    def send_near():
        finish_stages(2, range(1, bucket))

        def store(unit, value):
            near[unit] = value

        base = list_at + 2 * LANES + direct_units
        gather_units(arrived[2], base, near_units, store)
        near_copy().start()

    def chosen(stage, values):
        result = values[0]
        for n, value in enumerate(values[1:]):
            result = jnp.where(stage > n, value, result)
        return result

    def compute_class(turn, carry):
        @pl.when(turn == first_turn)
        def _():
            send_first(0)

        @pl.when(turn == second_turn)
        def _():
            send_first(1)

        stage = turn // turns
        half = chosen(stage, [CLASSES[number] // 2 for number, _ in stages])
        parity = chosen(stage, [CLASSES[number] % 2 for number, _ in stages])
        offset = chosen(stage, [turn_of * devices for _, turn_of in stages])
        to_plane = (plane // 2 + half) % 2 * 2 + (plane % 2 + parity) % 2
        steps = [turn % turns * group + n for n in range(group)]
        picks = []
        for step in steps:
            _, to_row, to_lane, _ = neighbour_at(step)
            picks.append(offset + to_row * cols_n + to_plane * width + to_lane)

        def store(n, rows):
            sent[stage * in_plane + steps[n]] = rows

        compute(picks, store)
        for early_stage in range(early_stages):

            @pl.when(stage == early_stage)
            def _():
                for n in range(1, group):
                    graph_copy(early_stage, steps[n], own_place).start()

            @pl.when(jnp.logical_and(stage == early_stage, steps[0] > 0))
            def _():
                graph_copy(early_stage, steps[0], own_place).start()

        return carry

    pl.semaphore_wait(barrier, in_plane - 1 + PLANES - 1)
    for load in loads:
        load.wait()
    first_turn = min(3, len(stages) - 2) * turns
    second_turn = min(6, len(stages) - 1) * turns
    lax.fori_loop(0, len(stages) * turns, compute_class, 0)

    keys = lax.broadcasted_iota(jnp.int32, (devices * read_rows, slots), 0)
    members = (keys == ids_ref[0:1, :slots]).astype(jnp.float32)
    all_terms = jnp.dot(
        members,
        pooled[...].reshape(slots, hidden),
        precision=lax.Precision.HIGHEST,
        preferred_element_type=jnp.float32,
    )
    for place in range(in_plane):
        for to_plane in range(PLANES):
            device = place // width * cols_n + to_plane * width + place % width
            part = all_terms[device * read_rows : (device + 1) * read_rows]
            whole_terms[place, pl.ds(to_plane * read_rows, read_rows)] = part
    terms[...] = whole_terms[...].astype(jnp.bfloat16)

    def send_terms(step, carry):
        _, to_row, to_lane, _ = neighbour_at(step)
        terms_copy(step, to_row * width + to_lane, own_place).start()
        return carry

    lax.fori_loop(1, in_plane, send_terms, 0)
    terms_in[own_place] = jnp.zeros_like(terms[own_place])

    for stage in range(early_stages, len(stages)):
        start_stage(stage)
    send_rest(0)
    send_rest(1)
    send_merged()
    send_first(2)
    send_near()
    def finish_terms(step, carry):
        _, to_row, to_lane, source = neighbour_at(step)
        terms_copy(step, to_row * width + to_lane, own_place).wait_send()
        terms_copy(step, to_row * width + to_lane, source).wait_recv()
        return carry

    lax.fori_loop(1, in_plane, finish_terms, 0)
    summed = jnp.sum(terms_in[...].astype(jnp.float32), axis=0) + whole_terms[own_place]
    for to_plane in range(PLANES):
        plane_terms[to_plane] = summed[to_plane * read_rows : (to_plane + 1) * read_rows]
    final_terms[plane] = plane_terms[plane]
    for k in range(1, PLANES):
        final_copy(k, other_plane(k), plane).start()

    finish_stages(3, range(bucket))

    for number in range(3):
        first_copy(number).wait_send()
        first_copy(number).wait_recv()
    near_copy().wait_send()
    near_copy().wait_recv()

    @pl.when(inner)
    def _():
        for number in range(2):
            merged_copy(number).wait_send()

    @pl.when(jnp.logical_not(inner))
    def _():
        for number in range(2):
            rest_copy(number).wait_send()

    merged_copy(0).wait_recv()

    def out_copy(slot):
        return pltpu.make_async_copy(
            sent.at[slot],
            out_ref.at[slot],
            out_sem.at[slot],
        )

    def place_graph(slot, carry):
        for part in range(parts):
            value = unpacked[table_ref[final_at + slot * parts + part]]
            sent[slot, part] = value
        out_copy(slot).start()
        return carry

    lax.fori_loop(0, out_ref.shape[0], place_graph, 0)
    for k in range(1, PLANES):
        final_copy(k, other_plane(k), plane).wait_send()
        final_copy(k, other_plane(k), other_plane(k)).wait_recv()
    readout_ref[...] = jnp.sum(final_terms[...], axis=0)

    def finish_out(slot, carry):
        out_copy(slot).wait()
        return carry

    lax.fori_loop(0, out_ref.shape[0], finish_out, 0)


def finish_kernel(from_ref, to_ref, held, sem, out_sem):
    size = from_ref.shape[0] // 8
    parts = [pl.ds(n * size, size) for n in range(8)]
    loads = [
        pltpu.make_async_copy(from_ref.at[part], held.at[part], sem.at[n])
        for n, part in enumerate(parts)
    ]
    stores = [
        pltpu.make_async_copy(held.at[part], to_ref.at[part], out_sem.at[n])
        for n, part in enumerate(parts)
    ]
    for load in loads:
        load.start()
    for load, store in zip(loads, stores):
        load.wait()
        store.start()
    for store in stores:
        store.wait()


def body(
    sizes,
    node_features,
    node_counts,
    edge_list,
    readout_ids,
    live_graphs,
    self_weight,
    w_first,
    b_first,
    w_second,
    b_second,
    w_third,
    b_third,
):
    rows_n, cols_n = sizes
    devices = rows_n * cols_n
    width = cols_n // PLANES
    in_plane = rows_n * width
    capacity, block, hidden = node_features.shape
    parts = block // UNIT
    graphs_out = capacity // 2
    read_rows = 8
    bucket = (capacity + devices - 1) // devices
    slots_n = devices * bucket
    mean_units = graphs_out * parts // PLANES
    direct_units = mean_units // 2
    spare_units = mean_units * 9 // 8
    span = direct_units + spare_units
    tiers = [tuple(mean_units * part // 64 for part in tier) for tier in TIERS]
    places = in_plane * bucket
    zero_base = places * parts + 3 * direct_units + 2 * spare_units
    every = gather_counts(node_counts, live_graphs, sizes)
    table, extra, tier = pl.pallas_call(
        functools.partial(
            plan_kernel,
            sizes,
            capacity,
            bucket,
            parts,
            graphs_out,
            (direct_units, spare_units),
            tiers,
        ),
        out_shape=(
            jax.ShapeDtypeStruct((6 + graphs_out * parts // LANES, LANES), jnp.int32),
            jax.ShapeDtypeStruct((8, LANES), jnp.int32),
            jax.ShapeDtypeStruct((1,), jnp.int32),
        ),
        in_specs=[VMEM, VMEM],
        out_specs=(VMEM, VMEM, SMEM),
        name="plan",
    )(every, readout_ids.reshape(1, -1))
    table = table.reshape(-1)

    out_shape = (
        jax.ShapeDtypeStruct((graphs_out, block, hidden), jnp.bfloat16),
        jax.ShapeDtypeStruct((read_rows, hidden), jnp.float32),
    )
    pooled_scratch = pltpu.VMEM((slots_n, 1, hidden), jnp.float32)

    def semaphores(count):
        return [pltpu.SemaphoreType.DMA((count,)), pltpu.SemaphoreType.DMA((count,))]

    def relayed(tier, caps, *operands):
        table, extra, node_counts, self_weight, node_features, edge_list = operands[:6]
        merge_units, rest_units, near_units = caps

        def graphs(*count):
            return pltpu.VMEM((*count, UNIT, hidden), jnp.bfloat16)

        whole_terms = pltpu.VMEM((in_plane, PLANES * read_rows, hidden), jnp.float32)
        half_terms = pltpu.VMEM((in_plane, PLANES * read_rows, hidden), jnp.bfloat16)
        some_terms = pltpu.VMEM((PLANES, read_rows, hidden), jnp.float32)
        node_out, readout = pl.pallas_call(
            functools.partial(relay_kernel, sizes, bucket, direct_units, spare_units, caps),
            out_shape=(
                jax.ShapeDtypeStruct((graphs_out, parts, UNIT, hidden), jnp.bfloat16),
                out_shape[1],
            ),
            in_specs=[SMEM] * 3 + [HBM] + [VMEM] * 8,
            out_specs=(HBM, VMEM),
            scratch_shapes=[graphs(slots_n, parts)]
            + [graphs(in_plane * parts)] * 3
            + [graphs(places * parts if bucket > 1 else 1)] * 3
            + [graphs(2 * spare_units)] * 2
            + [
                graphs(3, direct_units),
                graphs(2, merge_units),
                graphs(near_units),
                graphs(zero_base + 1),
            ]
            + [pooled_scratch, whole_terms, half_terms, half_terms, some_terms, some_terms]
            + semaphores(slots_n)
            + semaphores(3)
            + semaphores(2)
            + semaphores(2)
            + semaphores(1)
            + semaphores(in_plane)
            + semaphores(PLANES)
            + [
                pltpu.SemaphoreType.DMA((graphs_out,)),
                pltpu.VMEM((capacity, block, hidden), jnp.bfloat16),
                pltpu.SemaphoreType.DMA((4,)),
            ],
            compiler_params=pltpu.CompilerParams(
                collective_id=2 + tier, has_side_effects=True, vmem_limit_bytes=61 * 1024 * 1024
            ),
            name="gin_relay",
        )(table, node_counts, self_weight, node_features, edge_list, extra, *operands[6:])
        return node_out.reshape(graphs_out, block, hidden), readout

    def direct(*operands):
        table, extra, node_counts, self_weight, node_features, edge_list = operands[:6]
        all_terms = pltpu.VMEM((devices, read_rows, hidden), jnp.float32)
        graphs = pltpu.VMEM((devices, bucket, block, hidden), jnp.bfloat16)
        return pl.pallas_call(
            functools.partial(layer_kernel, sizes, bucket),
            out_shape=out_shape,
            in_specs=[SMEM] * 4 + [VMEM] * 9,
            out_specs=(VMEM, VMEM),
            scratch_shapes=[graphs, graphs]
            + [pooled_scratch, all_terms, all_terms]
            + semaphores(devices)
            + semaphores(devices),
            compiler_params=pltpu.CompilerParams(
                collective_id=1, has_side_effects=True, vmem_limit_bytes=60 * 1024 * 1024
            ),
            name="gin_direct",
        )(
            table,
            node_counts,
            extra[1],
            self_weight,
            node_features,
            edge_list,
            extra,
            *operands[6:],
        )

    branches = [functools.partial(relayed, number, cap) for number, cap in enumerate(tiers)]
    node_out, readout = lax.switch(
        tier[0],
        branches + [direct],
        table,
        extra,
        node_counts,
        self_weight,
        node_features,
        edge_list,
        w_first,
        b_first.reshape(1, -1),
        w_second,
        b_second.reshape(1, -1),
        w_third,
        b_third.reshape(1, -1),
    )
    node_out = pl.pallas_call(
        finish_kernel,
        out_shape=jax.ShapeDtypeStruct(node_out.shape, node_out.dtype),
        in_specs=[HBM],
        out_specs=HBM,
        scratch_shapes=[
            pltpu.VMEM(node_out.shape, node_out.dtype),
            pltpu.SemaphoreType.DMA((8,)),
            pltpu.SemaphoreType.DMA((8,)),
        ],
        name="finish",
    )(node_out)
    return node_out, readout


def solution(mesh):
    sizes = (mesh.shape["row"], mesh.shape["col"])
    both = ("row", "col")
    in_specs = (
        P(both, None, None),
        P(both),
        P(both, None, None),
        P(both),
        P(both),
        P(),
        P(),
        P(),
        P(),
        P(),
        P(),
        P(),
    )
    out_specs = (P(both, None, None), P(both, None))
    return jax.shard_map(
        functools.partial(body, sizes),
        mesh=mesh,
        in_specs=in_specs,
        out_specs=out_specs,
        check_vma=False,
    )
```

```python
import functools

import jax
import jax.numpy as jnp
from jax import lax
from jax.experimental import pallas as pl
from jax.experimental.pallas import tpu as pltpu
from jax.sharding import PartitionSpec as P

MESH = pl.DeviceIdType.MESH
VMEM = pl.BlockSpec(memory_space=pltpu.VMEM)
SMEM = pl.BlockSpec(memory_space=pltpu.SMEM)
HBM = pl.BlockSpec(memory_space=pltpu.HBM)
PLANES = 4
UNIT = 16
LANES = 128
CLASSES = (2, 3, 1, 0)
TIERS = ((36, 36, 40), (40, 36, 40), (44, 36, 40), (48, 36, 40), (52, 40, 44), (60, 48, 56), (68, 48, 56))


def partners(step, sizes):
    rows, cols = sizes
    row, col = lax.axis_index("row"), lax.axis_index("col")
    by_row, by_col = step // cols, (step % cols) * 3 % cols
    to_row, to_col = (row + by_row) % rows, (col + by_col) % cols
    from_row, from_col = (row + rows - by_row) % rows, (col + cols - by_col) % cols
    return (to_row, to_col), to_row * cols + to_col, from_row * cols + from_col


def greet(sizes):
    barrier = pltpu.get_barrier_semaphore()
    devices = sizes[0] * sizes[1]

    def signal(step, carry):
        where, _, _ = partners(step, sizes)
        pl.semaphore_signal(barrier, inc=1, device_id=where, device_id_type=MESH)
        return carry

    lax.fori_loop(1, devices, signal, 0)
    return barrier


def gather_kernel(sizes, counts_ref, live_ref, all_ref, own, send_sem, recv_sem):
    devices = sizes[0] * sizes[1]
    capacity = counts_ref.shape[1]
    me = lax.axis_index("row") * sizes[1] + lax.axis_index("col")
    barrier = greet(sizes)
    own[:, :capacity] = counts_ref[...]
    own[:, capacity:] = jnp.full((1, own.shape[1] - capacity), live_ref[0])
    all_ref[me] = own[...]
    pl.semaphore_wait(barrier, devices - 1)

    def copy(step, slot):
        where, _, _ = partners(step, sizes)
        return pltpu.make_async_remote_copy(
            src_ref=own,
            dst_ref=all_ref.at[slot],
            send_sem=send_sem.at[step],
            recv_sem=recv_sem.at[step],
            device_id=where,
            device_id_type=MESH,
        )

    def send(step, carry):
        copy(step, me).start()
        return carry

    def finish(step, carry):
        _, _, source = partners(step, sizes)
        copy(step, me).wait_send()
        copy(step, source).wait_recv()
        return carry

    lax.fori_loop(1, devices, send, 0)
    lax.fori_loop(1, devices, finish, 0)


def gather_counts(node_counts, live_graphs, sizes):
    devices = sizes[0] * sizes[1]
    return pl.pallas_call(
        functools.partial(gather_kernel, sizes),
        out_shape=jax.ShapeDtypeStruct((devices, 1, LANES), jnp.int32),
        in_specs=[VMEM, SMEM],
        out_specs=VMEM,
        scratch_shapes=[
            pltpu.VMEM((1, LANES), jnp.int32),
            pltpu.SemaphoreType.DMA((devices,)),
            pltpu.SemaphoreType.DMA((devices,)),
        ],
        compiler_params=pltpu.CompilerParams(collective_id=0, has_side_effects=True),
        name="gather_counts",
    )(node_counts.reshape(1, -1), live_graphs)


def plan_kernel(
    sizes, capacity, bucket, parts, graphs_out, units, tiers, every_ref, ids_ref,
    table_ref, extra_ref, tier_ref,
):
    direct_units, spare_units = units
    rows_n, cols_n = sizes
    devices = rows_n * cols_n
    bits = devices.bit_length() - 1
    width = cols_n // PLANES
    in_plane = rows_n * width
    places = in_plane * bucket
    row, col = lax.axis_index("row"), lax.axis_index("col")
    plane, lane = col // width, col % width
    me = row * cols_n + col
    shape = (devices, LANES)
    lanes = lax.broadcasted_iota(jnp.int32, shape, 1)
    owner = lax.broadcasted_iota(jnp.int32, (devices, 1), 0)
    owner_col = owner & (cols_n - 1)
    owner_plane = owner_col >> (width.bit_length() - 1)
    owner_place = (owner >> (cols_n.bit_length() - 1)) * width + (owner & (width - 1))

    def total(values, axis):
        return jnp.sum(values.astype(jnp.float32), axis=axis, keepdims=True).astype(jnp.int32)

    def column(values, index):
        return total(jnp.where(lanes == index, values, 0), 1)

    def product(left, right):
        left, right = left.astype(jnp.float32), right.astype(jnp.float32)
        exact = jnp.dot(
            left.astype(jnp.bfloat16),
            right.astype(jnp.bfloat16),
            preferred_element_type=jnp.float32,
        )
        return exact.astype(jnp.int32)

    every = every_ref[:, 0, :]
    live = column(every, capacity)
    first = lax.broadcasted_iota(jnp.int32, (devices, devices), 0)
    second = lax.broadcasted_iota(jnp.int32, (devices, devices), 1)
    offset = column(product((second < first).astype(jnp.int32), every), capacity)
    sizes_all = jnp.where(lanes < live, (every + (UNIT - 1)) >> (UNIT.bit_length() - 1), 0)

    def turned(values, by, turn):
        values = jnp.where((lanes[: values.shape[0]] >> bits) == turn, values, 0)
        shift = devices
        while shift < LANES:
            values = values + pltpu.roll(values, shift, 1)
            shift *= 2
        for bit in range(bits):
            rolled = pltpu.roll(values, 1 << bit, 1)
            values = jnp.where(((by >> bit) & 1) == 1, rolled, values)
        return values

    by_turn = [turned(sizes_all, offset, turn) for turn in range(bucket)]
    size_sum = sum(by_turn)
    early = by_turn[0]
    same_plane = ((first & (cols_n - 1)) >> (width.bit_length() - 1)) == (
        (second & (cols_n - 1)) >> (width.bit_length() - 1)
    )
    starts, begun = [], jnp.zeros(shape, jnp.int32)
    for turn in range(bucket):
        earlier = (same_plane & (second < first)).astype(jnp.int32)
        starts.append(begun + product(earlier, by_turn[turn]))
        begun = begun + product(same_plane.astype(jnp.int32), by_turn[turn])
        if turn == 0:
            firsts = jnp.minimum(begun, direct_units)

    plane_row = lax.broadcasted_iota(jnp.int32, (8, devices), 0)
    plane_of = lax.broadcasted_iota(jnp.int32, (8, devices), 1)
    plane_of = (plane_of & (cols_n - 1)) >> (width.bit_length() - 1)
    of_plane = (plane_row == plane_of).astype(jnp.int32)
    plane_load = product(of_plane, size_sum)
    plane_load = plane_load - jnp.minimum(product(of_plane, early), direct_units)
    planes = lax.broadcasted_iota(jnp.int32, (8, LANES), 0)
    to_planes = lax.broadcasted_iota(jnp.int32, (8, LANES), 1) & (cols_n - 1)
    to_planes = to_planes >> (width.bit_length() - 1)
    far = ((planes >> 1) != (to_planes >> 1)) & (planes < PLANES)
    plane_rest = jnp.where(far, plane_load, 0)
    is_inner = ((planes & 1) + (planes >> 1)) == 1
    merged_load = total(plane_rest, 0)
    rest_load = jnp.where(is_inner, 0, plane_rest)
    near_load = jnp.where(((planes ^ to_planes) == 1), plane_load, 0)
    most_merged = jnp.max(merged_load.astype(jnp.float32))
    most_rest = jnp.max(rest_load.astype(jnp.float32))
    most_near = jnp.max(near_load.astype(jnp.float32))
    tier = jnp.int32(0)
    for merge, rest, near in tiers:
        over = (most_merged > merge) | (most_rest > rest) | (most_near > near)
        tier = tier + jnp.where(over, 1, 0)
    tier_ref[0] = tier

    line = lax.broadcasted_iota(jnp.int32, (1, LANES), 1)
    own_offset = total(jnp.where(owner == me, offset, 0), 0)
    own_live = total(jnp.where(owner == me, live, 0), 0)
    within = ((line - own_offset) & (devices - 1)) + (line >> bits) * devices
    table_ref[0:1, :] = jnp.minimum(within, capacity - 1)

    ids = jnp.where(line < capacity, jnp.concatenate([ids_ref[...]] * (LANES // capacity), 1), 0)
    slot_ids = jnp.zeros((1, LANES), jnp.int32)
    for turn in range(bucket):
        slot_ids = jnp.where((line >> bits) == turn, turned(ids, own_offset, turn), slot_ids)
    extra_ref[0:1, :] = jnp.where(within < own_live, slot_ids, -1)

    for number, k in enumerate(CLASSES[:3]):
        to_plane = (plane // 2 + k // 2) % 2 * 2 + (plane % 2 + k % 2) % 2
        target = row * cols_n + to_plane * width + lane
        listed = jnp.zeros(shape, jnp.int32)
        used = jnp.zeros((devices, 1), jnp.int32)
        sent_first = jnp.where(owner_plane == plane, column(firsts, target), 0)
        sent_first = jnp.max(sent_first.astype(jnp.float32), axis=0, keepdims=True)
        sent_first = sent_first.astype(jnp.int32)
        unit = jnp.where(line < direct_units, line, sent_first + line - direct_units)
        for turn in range(bucket):
            size = column(by_turn[turn], target)
            size = jnp.where(owner_plane == plane, size, 0)
            at = unit - column(starts[turn], target)
            base = (turn * in_plane + owner_place) * parts
            listed = listed + jnp.where((at >= 0) & (at < size), base + at, 0)
            used = used + size
        listed = total(listed, 0)
        listed = jnp.where(
            line < direct_units, jnp.minimum(listed, in_plane * parts - 1), listed
        )
        table_ref[1 + number : 2 + number, :] = listed
        if number < 2:
            own_rest = total(used, 0) - sent_first
            merged = jnp.where(line < own_rest, line, spare_units + line - own_rest)
            merged = jnp.minimum(jnp.maximum(merged, 0), 2 * spare_units - 1)
            table_ref[4 + number : 5 + number, :] = merged

    inner_plane = 2 - plane // 2
    own_sizes = [column(by_turn[turn], me) for turn in range(bucket)]
    own_firsts = column(firsts, me)
    from_inner = owner_plane == inner_plane
    inner_first = jnp.where(from_inner, own_firsts, 0).astype(jnp.float32)
    inner_first = jnp.max(inner_first, axis=0, keepdims=True).astype(jnp.int32)
    inner_rest = total(jnp.where(from_inner, sum(own_sizes), 0), 0) - inner_first
    first_base = places * parts
    merged_base = first_base + 3 * direct_units
    near_base = merged_base + spare_units
    zero_base = near_base + spare_units
    from_own, from_near = owner_plane == plane, (owner_plane ^ 1) == plane
    same_side = (owner_plane & 1) == plane % 2
    low = jnp.where(from_near, 2 * direct_units, jnp.where(same_side, 0, direct_units))
    low = first_base + low
    high = jnp.where(from_near, near_base, merged_base + jnp.where(from_inner, 0, inner_rest))
    high = high - own_firsts
    finals = [jnp.zeros(shape, jnp.int32) for _ in range(graphs_out * parts // LANES)]
    arrival = jnp.zeros(shape, jnp.int32)
    part = lanes & (parts - 1)
    graph = lanes >> (parts.bit_length() - 1)
    for turn in range(bucket):
        within = ((me - offset) & (devices - 1)) + turn * devices
        place = jnp.where(within < live, (offset + within) >> bits, -1)
        at = column(starts[turn], me) + part
        address = jnp.where(at < own_firsts, low + at, high + at)
        held = (turn * in_plane + owner_place) * parts + part
        address = jnp.where(from_own, held, address)
        address = jnp.where(part < own_sizes[turn], address - zero_base, 0)
        for half in range(len(finals)):
            mine = graph + half * (LANES // parts) == place
            finals[half] = finals[half] + jnp.where(mine, address, 0)
        arrival = arrival + jnp.where(lanes == place, owner * bucket + turn, 0)
    for half, values in enumerate(finals):
        address = jnp.clip(total(values, 0) + zero_base, 0, zero_base)
        table_ref[6 + half : 7 + half, :] = address
    extra_ref[1:2, :] = total(arrival, 0)


def layer_kernel(
    sizes,
    bucket,
    picked_ref,
    counts_ref,
    arrival_ref,
    weight_ref,
    features_ref,
    edges_ref,
    ids_ref,
    w_first_ref,
    b_first_ref,
    w_second_ref,
    b_second_ref,
    w_third_ref,
    b_third_ref,
    out_ref,
    readout_ref,
    sent,
    arrived,
    pooled,
    terms,
    terms_in,
    send_sem,
    recv_sem,
    terms_send_sem,
    terms_recv_sem,
):
    devices = sizes[0] * sizes[1]
    read_rows = readout_ref.shape[0]
    block, hidden = features_ref.shape[1:]
    me = lax.axis_index("row") * sizes[1] + lax.axis_index("col")
    barrier = greet(sizes)

    def graph_copy(step, target, slot):
        where, _, _ = partners(step, sizes)
        return pltpu.make_async_remote_copy(
            src_ref=sent.at[target],
            dst_ref=arrived.at[slot],
            send_sem=send_sem.at[step],
            recv_sem=recv_sem.at[step],
            device_id=where,
            device_id_type=MESH,
        )

    def terms_copy(step, target, slot):
        where, _, _ = partners(step, sizes)
        return pltpu.make_async_remote_copy(
            src_ref=terms.at[target],
            dst_ref=terms_in.at[slot],
            send_sem=terms_send_sem.at[step],
            recv_sem=terms_recv_sem.at[step],
            device_id=where,
            device_id_type=MESH,
        )

    node_rows = lax.broadcasted_iota(jnp.int32, (block, edges_ref.shape[2]), 0)
    node_index = lax.broadcasted_iota(jnp.int32, (block, hidden), 0)

    def compute(target, store):
        blends = []
        for j in range(bucket):
            graph = picked_ref[j * devices + target]
            features = features_ref[graph]
            edges = edges_ref[graph]
            sources = (node_rows == edges[0:1, :]).astype(jnp.float32).astype(jnp.bfloat16)
            targets = (node_rows == edges[1:2, :]).astype(jnp.float32).astype(jnp.bfloat16)
            adjacency = lax.dot_general(
                targets,
                sources,
                (((1,), (1,)), ((), ())),
                preferred_element_type=jnp.float32,
            ).astype(jnp.bfloat16)
            neighbour = jnp.dot(adjacency, features, preferred_element_type=jnp.float32)
            blends.append(
                (weight_ref[0] * features.astype(jnp.float32) + neighbour).astype(jnp.bfloat16)
            )
        blended = jnp.concatenate(blends, axis=0) if bucket > 1 else blends[0]
        hidden_one = jnp.maximum(
            jnp.dot(blended, w_first_ref[...], preferred_element_type=jnp.float32)
            + b_first_ref[...],
            0.0,
        ).astype(jnp.bfloat16)
        hidden_two = jnp.maximum(
            jnp.dot(hidden_one, w_second_ref[...], preferred_element_type=jnp.float32)
            + b_second_ref[...],
            0.0,
        ).astype(jnp.bfloat16)
        result = (
            jnp.dot(hidden_two, w_third_ref[...], preferred_element_type=jnp.float32)
            + b_third_ref[...]
        )
        for j in range(bucket):
            count = counts_ref[picked_ref[j * devices + target]]
            rows = jnp.where(node_index < count, result[j * block : (j + 1) * block], 0.0)
            rows = rows.astype(jnp.bfloat16)
            store(j, rows)
            total = jnp.sum(rows.astype(jnp.float32), axis=0, keepdims=True)
            pooled[j * devices + target] = total / jnp.full((1, hidden), count).astype(jnp.float32)

    pl.semaphore_wait(barrier, devices - 1)

    def compute_and_send(step, carry):
        _, target, _ = partners(step, sizes)

        def store(j, rows):
            sent[target, j] = rows

        compute(target, store)

        @pl.when(step > 0)
        def _():
            graph_copy(step, target, me).start()

        return carry

    lax.fori_loop(0, devices, compute_and_send, 0)
    for j in range(bucket):
        arrived[me, j] = sent[me, j]

    slots = devices * bucket
    keys = lax.broadcasted_iota(jnp.int32, (devices * read_rows, slots), 0)
    members = (keys == ids_ref[0:1, :slots]).astype(jnp.float32)
    all_terms = jnp.dot(
        members,
        pooled[...].reshape(slots, hidden),
        precision=lax.Precision.HIGHEST,
        preferred_element_type=jnp.float32,
    )
    terms[...] = all_terms.reshape(devices, read_rows, hidden)

    def send_terms(step, carry):
        _, target, _ = partners(step, sizes)
        terms_copy(step, target, me).start()
        return carry

    lax.fori_loop(1, devices, send_terms, 0)
    terms_in[me] = terms[me]

    def finish(step, carry):
        _, target, source = partners(step, sizes)
        graph_copy(step, target, me).wait_send()
        graph_copy(step, target, source).wait_recv()
        terms_copy(step, target, me).wait_send()
        terms_copy(step, target, source).wait_recv()
        return carry

    lax.fori_loop(1, devices, finish, 0)
    readout_ref[...] = jnp.sum(terms_in[...], axis=0)

    def place(slot, carry):
        which = arrival_ref[slot]
        out_ref[slot] = arrived[which // bucket, which % bucket]
        return carry

    lax.fori_loop(0, out_ref.shape[0], place, 0)


def relay_kernel(
    sizes,
    bucket,
    direct_units,
    spare_units,
    caps,
    table_ref,
    counts_ref,
    weight_ref,
    features_hbm_ref,
    edges_ref,
    ids_ref,
    w_first_ref,
    b_first_ref,
    w_second_ref,
    b_second_ref,
    w_third_ref,
    b_third_ref,
    out_ref,
    readout_ref,
    sent,
    early_a,
    early_b,
    early_c,
    arrived_a,
    arrived_b,
    arrived_c,
    mixed_a,
    mixed_b,
    firsts,
    merged,
    near,
    unpacked,
    pooled,
    whole_terms,
    terms,
    terms_in,
    plane_terms,
    final_terms,
    send_sem,
    recv_sem,
    first_send_sem,
    first_recv_sem,
    rest_send_sem,
    rest_recv_sem,
    merged_send_sem,
    merged_recv_sem,
    near_send_sem,
    near_recv_sem,
    terms_send_sem,
    terms_recv_sem,
    final_send_sem,
    final_recv_sem,
    out_sem,
    features_ref,
    load_sem,
):
    merge_units, rest_units, near_units = caps
    rows_n, cols_n = sizes
    devices = rows_n * cols_n
    width = cols_n // PLANES
    in_plane = rows_n * width
    read_rows = readout_ref.shape[0]
    block, hidden = features_ref.shape[1:]
    parts = block // UNIT
    slots = devices * bucket
    places = in_plane * bucket
    list_at, merge_at, final_at = LANES, 4 * LANES, 6 * LANES
    first_base = places * parts
    merged_base = first_base + 3 * direct_units
    near_base = merged_base + spare_units
    zero_base = near_base + spare_units
    early = (early_a, early_b, early_c)
    arrived = (arrived_a, arrived_b, arrived_c) if bucket > 1 else early
    mixed = (mixed_a, mixed_b)
    row, col = lax.axis_index("row"), lax.axis_index("col")
    plane, lane = col // width, col % width
    own_place = row * width + lane
    inner = plane % 2 + plane // 2 == 1

    def other_plane(k):
        return (plane // 2 + k // 2) % 2 * 2 + (plane % 2 + k % 2) % 2

    def neighbour_at(step):
        to_row, to_lane = (row + step // width) % rows_n, (lane + step % width) % width
        from_row = (row + rows_n - step // width) % rows_n
        from_lane = (lane + width - step % width) % width
        return (to_row, plane * width + to_lane), to_row, to_lane, from_row * width + from_lane

    barrier = pltpu.get_barrier_semaphore()

    def signal(step, carry):
        where, _, _, _ = neighbour_at(step)
        pl.semaphore_signal(barrier, inc=1, device_id=where, device_id_type=MESH)
        return carry

    lax.fori_loop(1, in_plane, signal, 0)
    for k in range(1, PLANES):
        where = (row, other_plane(k) * width + lane)
        pl.semaphore_signal(barrier, inc=1, device_id=where, device_id_type=MESH)
    quarter = features_ref.shape[0] // 4
    loads = [
        pltpu.make_async_copy(
            features_hbm_ref.at[pl.ds(n * quarter, quarter)],
            features_ref.at[pl.ds(n * quarter, quarter)],
            load_sem.at[n],
        )
        for n in range(4)
    ]
    for load in loads:
        load.start()
    unpacked[zero_base] = jnp.zeros((UNIT, hidden), jnp.bfloat16)

    stages = [(0, 0), (1, 0)]
    for late in ((0, 1), (2,), (3,)):
        for turn in range(bucket):
            stages += [(number, turn) for number in late if (number, turn) not in stages]

    def landing(stage, place):
        number, turn = stages[stage]
        if number < 3 and turn == 0:
            return early[number].at[pl.ds(place * parts, parts)]
        into = arrived[number] if number < 3 else unpacked
        return into.at[pl.ds((turn * in_plane + place) * parts, parts)]

    def graph_copy(stage, step, place):
        where, _, _, _ = neighbour_at(step)
        return pltpu.make_async_remote_copy(
            src_ref=sent.at[stage * in_plane + step],
            dst_ref=landing(stage, place),
            send_sem=send_sem.at[stage * in_plane + step],
            recv_sem=recv_sem.at[stage * in_plane + step],
            device_id=where,
            device_id_type=MESH,
        )

    def column_copy(source, target, send, recv, k):
        return pltpu.make_async_remote_copy(
            src_ref=source,
            dst_ref=target,
            send_sem=send,
            recv_sem=recv,
            device_id=(row, other_plane(k) * width + lane),
            device_id_type=MESH,
        )

    def first_copy(number):
        return column_copy(
            firsts.at[number],
            unpacked.at[pl.ds(first_base + number * direct_units, direct_units)],
            first_send_sem.at[number],
            first_recv_sem.at[number],
            CLASSES[number],
        )

    def rest_copy(number):
        return column_copy(
            mixed[number].at[pl.ds(0, rest_units)],
            mixed[1 - number].at[pl.ds(spare_units, rest_units)],
            rest_send_sem.at[number],
            rest_recv_sem.at[1 - number],
            1,
        )

    def merged_copy(number):
        return column_copy(
            merged.at[number],
            unpacked.at[pl.ds(merged_base, merge_units)],
            merged_send_sem.at[number],
            merged_recv_sem.at[0],
            CLASSES[number],
        )

    def near_copy():
        return column_copy(
            near,
            unpacked.at[pl.ds(near_base, near_units)],
            near_send_sem.at[0],
            near_recv_sem.at[0],
            1,
        )

    def terms_copy(step, target, slot):
        where, _, _, _ = neighbour_at(step)
        return pltpu.make_async_remote_copy(
            src_ref=terms.at[target],
            dst_ref=terms_in.at[slot],
            send_sem=terms_send_sem.at[step],
            recv_sem=terms_recv_sem.at[step],
            device_id=where,
            device_id_type=MESH,
        )

    def final_copy(k, to_plane, from_plane):
        return column_copy(
            plane_terms.at[to_plane],
            final_terms.at[from_plane],
            final_send_sem.at[k],
            final_recv_sem.at[k],
            k,
        )

    node_rows = lax.broadcasted_iota(jnp.int32, (block, edges_ref.shape[2]), 0)
    node_index = lax.broadcasted_iota(jnp.int32, (block, hidden), 0)

    def compute(picks, store):
        blends = []
        for pick in picks:
            graph = table_ref[pick]
            features = features_ref[graph]
            edges = edges_ref[graph]
            sources = (node_rows == edges[0:1, :]).astype(jnp.float32).astype(jnp.bfloat16)
            ends = (node_rows == edges[1:2, :]).astype(jnp.float32).astype(jnp.bfloat16)
            adjacency = lax.dot_general(
                ends,
                sources,
                (((1,), (1,)), ((), ())),
                preferred_element_type=jnp.float32,
            ).astype(jnp.bfloat16)
            neighbour = jnp.dot(adjacency, features, preferred_element_type=jnp.float32)
            blends.append(
                (weight_ref[0] * features.astype(jnp.float32) + neighbour).astype(jnp.bfloat16)
            )
        blended = jnp.concatenate(blends, axis=0)
        hidden_one = jnp.maximum(
            jnp.dot(blended, w_first_ref[...], preferred_element_type=jnp.float32)
            + b_first_ref[...],
            0.0,
        ).astype(jnp.bfloat16)
        hidden_two = jnp.maximum(
            jnp.dot(hidden_one, w_second_ref[...], preferred_element_type=jnp.float32)
            + b_second_ref[...],
            0.0,
        ).astype(jnp.bfloat16)
        result = (
            jnp.dot(hidden_two, w_third_ref[...], preferred_element_type=jnp.float32)
            + b_third_ref[...]
        )
        for n, pick in enumerate(picks):
            count = counts_ref[table_ref[pick]]
            rows = jnp.where(node_index < count, result[n * block : (n + 1) * block], 0.0)
            rows = rows.astype(jnp.bfloat16)
            store(n, rows.reshape(parts, UNIT, hidden))
            total = jnp.sum(rows.astype(jnp.float32), axis=0, keepdims=True)
            pooled[pick] = total / jnp.full((1, hidden), count).astype(jnp.float32)

    group = 4
    turns = in_plane // group
    early_stages = min(4, len(stages))

    def start_stage(stage):
        def start(step, carry):
            graph_copy(stage, step, own_place).start()
            return carry

        lax.fori_loop(1, in_plane, start, 0)

    def finish_stage(stage):
        def finish(step, carry):
            _, _, _, source = neighbour_at(step)
            graph_copy(stage, step, own_place).wait_send()
            graph_copy(stage, step, source).wait_recv()
            return carry

        lax.fori_loop(1, in_plane, finish, 0)
        own = landing(stage, own_place)
        for n in range(parts):
            own[n] = sent[stage * in_plane, n]

    def finish_stages(number, turn_range):
        for turn in turn_range:
            finish_stage(stages.index((number, turn)))

    def gather_units(source, table_base, count, store):
        def gather(step, carry):
            for n in range(4):
                unit = step * 4 + n
                store(unit, source[table_ref[table_base + unit]])
            return carry

        lax.fori_loop(0, count // 4, gather, 0)

    def send_first(number):
        finish_stages(number, range(1))

        def store_first(unit, value):
            firsts[number, unit] = value

        gather_units(early[number], list_at + number * LANES, direct_units, store_first)
        first_copy(number).start()

        def keep(step, carry):
            for n in range(4):
                arrived[number][step * 4 + n] = early[number][step * 4 + n]
            return carry

        if bucket > 1:
            lax.fori_loop(0, in_plane * parts // 4, keep, 0)

    def send_rest(number):
        finish_stages(number, range(1, bucket))

        def store_rest(unit, value):
            mixed[number][unit] = value

        base = list_at + number * LANES + direct_units
        gather_units(arrived[number], base, max(merge_units, rest_units), store_rest)

        @pl.when(jnp.logical_not(inner))
        def _():
            rest_copy(number).start()

    def send_merged():
        @pl.when(inner)
        def _():
            for number in (1, 0):
                rest_copy(1 - number).wait_recv()

                def store(unit, value, number=number):
                    merged[number, unit] = value

                gather_units(mixed[number], merge_at + number * LANES, merge_units, store)
                merged_copy(number).start()

    def send_near():
        finish_stages(2, range(1, bucket))

        def store(unit, value):
            near[unit] = value

        base = list_at + 2 * LANES + direct_units
        gather_units(arrived[2], base, near_units, store)
        near_copy().start()

    def chosen(stage, values):
        result = values[0]
        for n, value in enumerate(values[1:]):
            result = jnp.where(stage > n, value, result)
        return result

    def compute_class(turn, carry):
        @pl.when(turn == first_turn)
        def _():
            send_first(0)

        @pl.when(turn == second_turn)
        def _():
            send_first(1)

        stage = turn // turns
        half = chosen(stage, [CLASSES[number] // 2 for number, _ in stages])
        parity = chosen(stage, [CLASSES[number] % 2 for number, _ in stages])
        offset = chosen(stage, [turn_of * devices for _, turn_of in stages])
        to_plane = (plane // 2 + half) % 2 * 2 + (plane % 2 + parity) % 2
        steps = [turn % turns * group + n for n in range(group)]
        picks = []
        for step in steps:
            _, to_row, to_lane, _ = neighbour_at(step)
            picks.append(offset + to_row * cols_n + to_plane * width + to_lane)

        def store(n, rows):
            sent[stage * in_plane + steps[n]] = rows

        compute(picks, store)
        for early_stage in range(early_stages):

            @pl.when(stage == early_stage)
            def _():
                for n in range(1, group):
                    graph_copy(early_stage, steps[n], own_place).start()

            @pl.when(jnp.logical_and(stage == early_stage, steps[0] > 0))
            def _():
                graph_copy(early_stage, steps[0], own_place).start()

        return carry

    pl.semaphore_wait(barrier, in_plane - 1 + PLANES - 1)
    for load in loads:
        load.wait()
    first_turn = min(3, len(stages) - 2) * turns
    second_turn = min(6, len(stages) - 1) * turns
    lax.fori_loop(0, len(stages) * turns, compute_class, 0)

    keys = lax.broadcasted_iota(jnp.int32, (devices * read_rows, slots), 0)
    members = (keys == ids_ref[0:1, :slots]).astype(jnp.float32)
    all_terms = jnp.dot(
        members,
        pooled[...].reshape(slots, hidden),
        precision=lax.Precision.HIGHEST,
        preferred_element_type=jnp.float32,
    )
    for place in range(in_plane):
        for to_plane in range(PLANES):
            device = place // width * cols_n + to_plane * width + place % width
            part = all_terms[device * read_rows : (device + 1) * read_rows]
            whole_terms[place, pl.ds(to_plane * read_rows, read_rows)] = part
    terms[...] = whole_terms[...].astype(jnp.bfloat16)

    def send_terms(step, carry):
        _, to_row, to_lane, _ = neighbour_at(step)
        terms_copy(step, to_row * width + to_lane, own_place).start()
        return carry

    lax.fori_loop(1, in_plane, send_terms, 0)
    terms_in[own_place] = jnp.zeros_like(terms[own_place])

    for stage in range(early_stages, len(stages)):
        start_stage(stage)
    send_rest(0)
    send_rest(1)
    send_merged()
    send_first(2)
    send_near()
    def finish_terms(step, carry):
        _, to_row, to_lane, source = neighbour_at(step)
        terms_copy(step, to_row * width + to_lane, own_place).wait_send()
        terms_copy(step, to_row * width + to_lane, source).wait_recv()
        return carry

    lax.fori_loop(1, in_plane, finish_terms, 0)
    summed = jnp.sum(terms_in[...].astype(jnp.float32), axis=0) + whole_terms[own_place]
    for to_plane in range(PLANES):
        plane_terms[to_plane] = summed[to_plane * read_rows : (to_plane + 1) * read_rows]
    final_terms[plane] = plane_terms[plane]
    for k in range(1, PLANES):
        final_copy(k, other_plane(k), plane).start()

    finish_stages(3, range(bucket))

    for number in range(3):
        first_copy(number).wait_send()
        first_copy(number).wait_recv()
    near_copy().wait_send()
    near_copy().wait_recv()

    @pl.when(inner)
    def _():
        for number in range(2):
            merged_copy(number).wait_send()

    @pl.when(jnp.logical_not(inner))
    def _():
        for number in range(2):
            rest_copy(number).wait_send()

    merged_copy(0).wait_recv()

    def out_copy(slot):
        return pltpu.make_async_copy(
            sent.at[slot],
            out_ref.at[slot],
            out_sem.at[slot],
        )

    def place_graph(slot, carry):
        for part in range(parts):
            value = unpacked[table_ref[final_at + slot * parts + part]]
            sent[slot, part] = value
        out_copy(slot).start()
        return carry

    lax.fori_loop(0, out_ref.shape[0], place_graph, 0)
    for k in range(1, PLANES):
        final_copy(k, other_plane(k), plane).wait_send()
        final_copy(k, other_plane(k), other_plane(k)).wait_recv()
    readout_ref[...] = jnp.sum(final_terms[...], axis=0)

    def finish_out(slot, carry):
        out_copy(slot).wait()
        return carry

    lax.fori_loop(0, out_ref.shape[0], finish_out, 0)


def finish_kernel(from_ref, to_ref, held, sem, out_sem):
    size = from_ref.shape[0] // 8
    parts = [pl.ds(n * size, size) for n in range(8)]
    loads = [
        pltpu.make_async_copy(from_ref.at[part], held.at[part], sem.at[n])
        for n, part in enumerate(parts)
    ]
    stores = [
        pltpu.make_async_copy(held.at[part], to_ref.at[part], out_sem.at[n])
        for n, part in enumerate(parts)
    ]
    for load in loads:
        load.start()
    for load, store in zip(loads, stores):
        load.wait()
        store.start()
    for store in stores:
        store.wait()


def body(
    sizes,
    node_features,
    node_counts,
    edge_list,
    readout_ids,
    live_graphs,
    self_weight,
    w_first,
    b_first,
    w_second,
    b_second,
    w_third,
    b_third,
):
    rows_n, cols_n = sizes
    devices = rows_n * cols_n
    width = cols_n // PLANES
    in_plane = rows_n * width
    capacity, block, hidden = node_features.shape
    parts = block // UNIT
    graphs_out = capacity // 2
    read_rows = 8
    bucket = (capacity + devices - 1) // devices
    slots_n = devices * bucket
    mean_units = graphs_out * parts // PLANES
    direct_units = mean_units // 2
    spare_units = mean_units * 9 // 8
    span = direct_units + spare_units
    tiers = [tuple(mean_units * part // 64 for part in tier) for tier in TIERS]
    places = in_plane * bucket
    zero_base = places * parts + 3 * direct_units + 2 * spare_units
    every = gather_counts(node_counts, live_graphs, sizes)
    table, extra, tier = pl.pallas_call(
        functools.partial(
            plan_kernel,
            sizes,
            capacity,
            bucket,
            parts,
            graphs_out,
            (direct_units, spare_units),
            tiers,
        ),
        out_shape=(
            jax.ShapeDtypeStruct((6 + graphs_out * parts // LANES, LANES), jnp.int32),
            jax.ShapeDtypeStruct((8, LANES), jnp.int32),
            jax.ShapeDtypeStruct((1,), jnp.int32),
        ),
        in_specs=[VMEM, VMEM],
        out_specs=(VMEM, VMEM, SMEM),
        name="plan",
    )(every, readout_ids.reshape(1, -1))
    table = table.reshape(-1)

    out_shape = (
        jax.ShapeDtypeStruct((graphs_out, block, hidden), jnp.bfloat16),
        jax.ShapeDtypeStruct((read_rows, hidden), jnp.float32),
    )
    pooled_scratch = pltpu.VMEM((slots_n, 1, hidden), jnp.float32)

    def semaphores(count):
        return [pltpu.SemaphoreType.DMA((count,)), pltpu.SemaphoreType.DMA((count,))]

    def relayed(tier, caps, *operands):
        table, extra, node_counts, self_weight, node_features, edge_list = operands[:6]
        merge_units, rest_units, near_units = caps

        def graphs(*count):
            return pltpu.VMEM((*count, UNIT, hidden), jnp.bfloat16)

        whole_terms = pltpu.VMEM((in_plane, PLANES * read_rows, hidden), jnp.float32)
        half_terms = pltpu.VMEM((in_plane, PLANES * read_rows, hidden), jnp.bfloat16)
        some_terms = pltpu.VMEM((PLANES, read_rows, hidden), jnp.float32)
        node_out, readout = pl.pallas_call(
            functools.partial(relay_kernel, sizes, bucket, direct_units, spare_units, caps),
            out_shape=(
                jax.ShapeDtypeStruct((graphs_out, parts, UNIT, hidden), jnp.bfloat16),
                out_shape[1],
            ),
            in_specs=[SMEM] * 3 + [HBM] + [VMEM] * 8,
            out_specs=(HBM, VMEM),
            scratch_shapes=[graphs(slots_n, parts)]
            + [graphs(in_plane * parts)] * 3
            + [graphs(places * parts if bucket > 1 else 1)] * 3
            + [graphs(2 * spare_units)] * 2
            + [
                graphs(3, direct_units),
                graphs(2, merge_units),
                graphs(near_units),
                graphs(zero_base + 1),
            ]
            + [pooled_scratch, whole_terms, half_terms, half_terms, some_terms, some_terms]
            + semaphores(slots_n)
            + semaphores(3)
            + semaphores(2)
            + semaphores(2)
            + semaphores(1)
            + semaphores(in_plane)
            + semaphores(PLANES)
            + [
                pltpu.SemaphoreType.DMA((graphs_out,)),
                pltpu.VMEM((capacity, block, hidden), jnp.bfloat16),
                pltpu.SemaphoreType.DMA((4,)),
            ],
            compiler_params=pltpu.CompilerParams(
                collective_id=2 + tier, has_side_effects=True, vmem_limit_bytes=61 * 1024 * 1024
            ),
            name="gin_relay",
        )(table, node_counts, self_weight, node_features, edge_list, extra, *operands[6:])
        return node_out.reshape(graphs_out, block, hidden), readout

    def direct(*operands):
        table, extra, node_counts, self_weight, node_features, edge_list = operands[:6]
        all_terms = pltpu.VMEM((devices, read_rows, hidden), jnp.float32)
        graphs = pltpu.VMEM((devices, bucket, block, hidden), jnp.bfloat16)
        return pl.pallas_call(
            functools.partial(layer_kernel, sizes, bucket),
            out_shape=out_shape,
            in_specs=[SMEM] * 4 + [VMEM] * 9,
            out_specs=(VMEM, VMEM),
            scratch_shapes=[graphs, graphs]
            + [pooled_scratch, all_terms, all_terms]
            + semaphores(devices)
            + semaphores(devices),
            compiler_params=pltpu.CompilerParams(
                collective_id=1, has_side_effects=True, vmem_limit_bytes=60 * 1024 * 1024
            ),
            name="gin_direct",
        )(
            table,
            node_counts,
            extra[1],
            self_weight,
            node_features,
            edge_list,
            extra,
            *operands[6:],
        )

    branches = [functools.partial(relayed, number, cap) for number, cap in enumerate(tiers)]
    node_out, readout = lax.switch(
        tier[0],
        branches + [direct],
        table,
        extra,
        node_counts,
        self_weight,
        node_features,
        edge_list,
        w_first,
        b_first.reshape(1, -1),
        w_second,
        b_second.reshape(1, -1),
        w_third,
        b_third.reshape(1, -1),
    )
    node_out = pl.pallas_call(
        finish_kernel,
        out_shape=jax.ShapeDtypeStruct(node_out.shape, node_out.dtype),
        in_specs=[HBM],
        out_specs=HBM,
        scratch_shapes=[
            pltpu.VMEM(node_out.shape, node_out.dtype),
            pltpu.SemaphoreType.DMA((8,)),
            pltpu.SemaphoreType.DMA((8,)),
        ],
        name="finish",
    )(node_out)
    return node_out, readout


def solution(mesh):
    sizes = (mesh.shape["row"], mesh.shape["col"])
    both = ("row", "col")
    in_specs = (
        P(both, None, None),
        P(both),
        P(both, None, None),
        P(both),
        P(both),
        P(),
        P(),
        P(),
        P(),
        P(),
        P(),
        P(),
    )
    out_specs = (P(both, None, None), P(both, None))
    return jax.shard_map(
        functools.partial(body, sizes),
        mesh=mesh,
        in_specs=in_specs,
        out_specs=out_specs,
        check_vma=False,
    )
```
